32 devices in a mesh: gx: 4 (over y, x), gy: 2 (over core), gz: 4 (over z).
Axes of the slice: x: 2, y: 2, z: 4, core: 2. Of those that a mesh axis runs over, the one named last changes fastest.
Arguments:
- positions: float32 [3, 16, 8, 8, 128], P(None, 'gx', 'gy', 'gz'), may hold values from 0 to 128, as said below
- grain_radii: float32 [16, 8, 8, 128], P('gx', 'gy', 'gz'), may hold values from 0.4 to 0.6
- film_liquid: float32 [16, 8, 8, 128], P('gx', 'gy', 'gz'), may hold values from 0.5 to 2
- pair_live: int32 [4, 2, 4, 864], P('gx', 'gy', 'gz'), may hold values from 0 to 1, as said below
- partner: int32 [4, 2, 4, 864, 128], P('gx', 'gy', 'gz'), may hold values from 0 to 127, as said below
- rupture: int32 [4, 2, 4, 864, 128], P('gx', 'gy', 'gz'), may hold values from 0 to 1
- volume: float32 [4, 2, 4, 864, 128], P('gx', 'gy', 'gz'), may hold values from 0.005 to 0.05
Outputs:
- forces: float32 [3, 16, 8, 8, 128], P(None, 'gx', 'gy', 'gz')
- film_next: float32 [16, 8, 8, 128], P('gx', 'gy', 'gz')
- volume_next: float32 [4, 2, 4, 864, 128], P('gx', 'gy', 'gz')
The draws below stay inside these ranges and needn't reach their ends.
Inputs may be any that keep to these rules, and one draw needn't show every extreme that they name: `pair_live`: slot s of a device is 1 only if its tile pair lies inside the grid; every pair of distinct touching tiles is listed at most once over all devices, by one of its two tiles; the slot of a tile with itself (s % 27 = 13) is always 1. partner[s, m] is never m itself. `positions`: the grains of tile (p, q, r) lie in its box, 8 wide along the first dimension and 4 along the others, the boxes side by side from the root; no two grains are closer than 0.5.
All inputs are finite; a program needn't handle non-finite values.
Results may differ from the reference program's by a relative error of at most 0.0003.
Values sent between devices are 32-bit elements; how exact they have to be, the bound alone decides.
A program may use at most 64 MiB of HBM per device.

```python
import math
import jax
import jax.numpy as jnp
from jax import lax

GRAINS = 128
BX = 4
BY = 4
BZ = 2
SLOTS = 864
TX = 16
TY = 8
TZ = 8
N_GX = 4
N_GY = 2
N_GZ = 4


shell_offsets = [(along_x, along_y, along_z) for along_x in (-1, 0, 1) for along_y in (-1, 0, 1) for along_z in (-1, 0, 1)]


def site_tables(key):
    scores = jax.random.randint(jax.random.fold_in(key, 41), (TX, TY, TZ, GRAINS), 0, 1048576)
    distinct = scores * GRAINS + jnp.arange(GRAINS, dtype=jnp.int32)
    site_of = jnp.argsort(distinct, axis=-1).astype(jnp.int32)
    grain_at = jnp.argsort(site_of, axis=-1).astype(jnp.int32)
    return (site_of, grain_at)


def draw_positions(key, part):
    site_of = site_tables(key)[0]
    spread = GRAINS // 16
    jitter = jax.random.uniform(key, (3, TX, TY, TZ, GRAINS), jnp.float32, -0.25, 0.25)
    root_x = (jnp.arange(TX, dtype=jnp.int32) * spread).astype(jnp.float32)[:, None, None, None]
    root_y = (jnp.arange(TY, dtype=jnp.int32) * 4).astype(jnp.float32)[None, :, None, None]
    root_z = (jnp.arange(TZ, dtype=jnp.int32) * 4).astype(jnp.float32)[None, None, :, None]
    coord_x = root_x + (site_of // 16).astype(jnp.float32) + 0.5 + jitter[0]
    coord_y = root_y + (site_of // 4 % 4).astype(jnp.float32) + 0.5 + jitter[1]
    coord_z = root_z + (site_of % 4).astype(jnp.float32) + 0.5 + jitter[2]
    return jnp.stack([coord_x, coord_y, coord_z], axis=0)


def bridge_links(key):
    subkeys = jax.random.split(jax.random.fold_in(key, 29), 3)
    site_of, grain_at = site_tables(key)
    layers = GRAINS // 16
    slot_total = 27 * BX * BY * BZ
    shape = (N_GX, N_GY, N_GZ, slot_total, GRAINS)
    full = (N_GX, N_GY, N_GZ, slot_total)
    slot = jnp.arange(slot_total, dtype=jnp.int32)
    tile = slot // 27
    code = slot % 27
    step_x = code // 9 - 1
    step_y = code // 3 % 3 - 1
    step_z = code % 3 - 1
    anchor_x = jnp.broadcast_to((jnp.arange(N_GX, dtype=jnp.int32) * BX)[:, None, None, None] + (tile // (BY * BZ))[None, None, None, :], full)
    anchor_y = jnp.broadcast_to((jnp.arange(N_GY, dtype=jnp.int32) * BY)[None, :, None, None] + (tile // BZ % BY)[None, None, None, :], full)
    anchor_z = jnp.broadcast_to((jnp.arange(N_GZ, dtype=jnp.int32) * BZ)[None, None, :, None] + (tile % BZ)[None, None, None, :], full)
    other_x = jnp.clip(anchor_x + step_x, 0, TX - 1)
    other_y = jnp.clip(anchor_y + step_y, 0, TY - 1)
    other_z = jnp.clip(anchor_z + step_z, 0, TZ - 1)
    site = site_of[anchor_x, anchor_y, anchor_z]
    site_x = site // 16
    site_y = site // 4 % 4
    site_z = site % 4
    heading = jax.random.randint(subkeys[0], shape, 0, 6)
    along = heading // 2
    sign = 2 * (heading % 2) - 1
    target_x = site_x + sign * (along == 0).astype(jnp.int32) - step_x[:, None] * layers
    target_y = site_y + sign * (along == 1).astype(jnp.int32) - step_y[:, None] * 4
    target_z = site_z + sign * (along == 2).astype(jnp.int32) - step_z[:, None] * 4
    inside = (target_x >= 0) & (target_x < layers) & (target_y >= 0) & (target_y < 4) & (target_z >= 0) & (target_z < 4)
    target_site = jnp.where(inside, target_x * 16 + target_y * 4 + target_z, 0).astype(jnp.int32)
    neighbour = jnp.take_along_axis(grain_at[other_x, other_y, other_z], target_site, axis=-1)
    grain = jnp.arange(GRAINS, dtype=jnp.int32)
    stride = jax.random.randint(subkeys[1], shape, 1, GRAINS)
    fallback = (grain + stride) % GRAINS
    partner = jnp.where(inside, neighbour, fallback).astype(jnp.int32)
    chance = jax.random.randint(subkeys[2], shape, 0, 4)
    rupture = jnp.where(inside, (chance == 0).astype(jnp.int32), (chance < 2).astype(jnp.int32)).astype(jnp.int32)
    return (partner, rupture)


def draw_partner(key, part):
    return bridge_links(key)[0]


def draw_rupture(key, part):
    return bridge_links(key)[1]


def draw_pair_live(key, part):
    subkeys = jax.random.split(jax.random.fold_in(key, 11), 3)
    level = jax.random.randint(subkeys[0], (N_GX, N_GY, N_GZ), 1, 7)
    level = jnp.repeat(jnp.repeat(jnp.repeat(level, BX, axis=0), BY, axis=1), BZ, axis=2)
    chance = jax.random.randint(subkeys[1], (13, TX, TY, TZ), 0, 12)
    owner = jax.random.randint(subkeys[2], (13, TX, TY, TZ), 0, 2)
    padded_level = jnp.pad(level, 1)
    inside = jnp.pad(jnp.ones((TX, TY, TZ), jnp.int32), 1)
    table = [jnp.zeros((TX, TY, TZ), jnp.int32) for number in range(27)]
    table[13] = jnp.ones((TX, TY, TZ), jnp.int32)
    upper_half = [offset for offset in shell_offsets if offset > (0, 0, 0)]
    for number, offset in enumerate(upper_half):
        start = (1 + offset[0], 1 + offset[1], 1 + offset[2])
        limit = (1 + offset[0] + TX, 1 + offset[1] + TY, 1 + offset[2] + TZ)
        near_level = lax.slice(padded_level, start, limit)
        near_inside = lax.slice(inside, start, limit)
        listed = (chance[number] < level + near_level) & (near_inside == 1)
        here = (listed & (owner[number] == 0)).astype(jnp.int32)
        there = (listed & (owner[number] == 1)).astype(jnp.int32)
        back_start = (1 - offset[0], 1 - offset[1], 1 - offset[2])
        back_limit = (1 - offset[0] + TX, 1 - offset[1] + TY, 1 - offset[2] + TZ)
        moved = lax.slice(jnp.pad(there, 1), back_start, back_limit)
        table[shell_offsets.index(offset)] = here
        table[shell_offsets.index((-offset[0], -offset[1], -offset[2]))] = moved
    stacked = jnp.stack(table, axis=-1)
    shaped = stacked.reshape(N_GX, BX, N_GY, BY, N_GZ, BZ, 27).transpose(0, 2, 4, 1, 3, 5, 6)
    return shaped.reshape(N_GX, N_GY, N_GZ, 27 * BX * BY * BZ)


def block_scale(stream_key, extent, shards, smallest, largest):
    level = 1.0
    for position, blocks in shards:
        steps = jax.random.uniform(jax.random.fold_in(jax.random.fold_in(stream_key, 6), position), (blocks,), jnp.float32, smallest / len(shards), largest / len(shards))
        level = level * jnp.repeat(jnp.exp(steps), extent[position] // blocks).reshape((-1,) + (1,) * (len(extent) - 1 - position))
    return level


def setup_inputs(seed: int = 0) -> dict:
    key_of = jax.random.split(jax.random.key(seed), 8)
    return {
        "positions": draw_positions(jax.random.fold_in(key_of[7], 71), 0),
        "grain_radii": jnp.clip(0.4 + 0.20000002 * jax.random.uniform(key_of[1], (TX, TY, TZ, GRAINS), jnp.float32) ** block_scale(key_of[1], (TX, TY, TZ, GRAINS), ((0, 4), (1, 2), (2, 4)), -0.2, 0.2), 0.4, 0.6),
        "film_liquid": jnp.clip(0.5 + 1.5 * jax.random.uniform(key_of[2], (TX, TY, TZ, GRAINS), jnp.float32) ** block_scale(key_of[2], (TX, TY, TZ, GRAINS), ((0, 4), (1, 2), (2, 4)), -0.2, 0.2), 0.5, 2.0),
        "pair_live": draw_pair_live(jax.random.fold_in(key_of[7], 71), 0),
        "partner": draw_partner(jax.random.fold_in(key_of[7], 71), 0),
        "rupture": draw_rupture(jax.random.fold_in(key_of[7], 71), 0),
        "volume": jnp.clip(jnp.exp(math.log(0.05) - 2.3025851 * jax.random.uniform(key_of[6], (N_GX, N_GY, N_GZ, SLOTS, GRAINS), jnp.float32) ** block_scale(key_of[6], (N_GX, N_GY, N_GZ, SLOTS, GRAINS), ((0, 4), (1, 2), (2, 4)), -0.2, 0.2)), 0.005, 0.05),
    }


ABSORB = 0.02
shell_offsets = [(along_x, along_y, along_z) for along_x in (-1, 0, 1) for along_y in (-1, 0, 1) for along_z in (-1, 0, 1)]

def evaluate(pieces):
    anchor, others, centre, active, partner, rupture, volume = pieces
    grains = anchor.shape[-1]
    identity = jnp.eye(grains, dtype=jnp.float32)
    diagonal = identity[None] * centre[:, None, None]
    deltas = [anchor[:, component, :, None] - others[:, component, None, :] for component in range(3)]
    squares = deltas[0] * deltas[0] + deltas[1] * deltas[1] + deltas[2] * deltas[2] + diagonal
    distance = jnp.sqrt(squares)
    reach_sum = anchor[:, 3, :, None] + others[:, 3, None, :]
    reduced = anchor[:, 3, :, None] * others[:, 3, None, :] / reach_sum
    intersection = jnp.maximum(reach_sum - distance, 0.0) * (1.0 - diagonal)
    repulse = jnp.sqrt(reduced) * intersection * jnp.sqrt(intersection) / distance * active[:, None, None]
    products = [repulse * member for member in deltas]
    keep_other = (1.0 - centre)[:, None]
    contact_a = jnp.stack([lax.optimization_barrier(jnp.sum(member, axis=2)) for member in products], axis=1)
    contact_b = jnp.stack([-lax.optimization_barrier(jnp.sum(member, axis=1)) * keep_other for member in products], axis=1)
    choose = (partner[:, :, None] == jnp.arange(grains, dtype=jnp.int32)[None, None, :]).astype(jnp.float32)
    matched = jnp.einsum('ncj,nij->nci', others, choose, precision=lax.Precision.HIGHEST)
    gap_vec = anchor[:, :3] - matched[:, :3]
    spacing = jnp.sqrt(lax.optimization_barrier(jnp.sum(gap_vec * gap_vec, axis=1)))
    radius_sum = anchor[:, 3] + matched[:, 3]
    harmonic = 2.0 * anchor[:, 3] * matched[:, 3] / radius_sum
    scaled_gap = jnp.maximum(spacing - radius_sum, 0.0) * jnp.sqrt(harmonic / volume)
    broken = rupture.astype(jnp.float32)
    intact = active[:, None] * (1.0 - broken)
    tension = intact * harmonic / (1.0 + 1.05 * scaled_gap + 2.5 * scaled_gap * scaled_gap) / spacing
    bridge_force = tension[:, None, :] * gap_vec
    released = active[:, None] * broken * volume
    volume_next = intact * (volume + ABSORB * (anchor[:, 4] + matched[:, 4]))
    liquid_anchor = 0.5 * released - ABSORB * intact * anchor[:, 4]
    liquid_other = 0.5 * released - ABSORB * intact * matched[:, 4]
    reaction = jnp.einsum('nci,nij->ncj', jnp.concatenate([bridge_force, liquid_other[:, None]], axis=1), choose, precision=lax.Precision.HIGHEST)
    anchor_side = jnp.concatenate([contact_a - bridge_force, liquid_anchor[:, None]], axis=1)
    other_side = jnp.concatenate([contact_b, jnp.zeros_like(liquid_anchor)[:, None]], axis=1) + reaction
    return (anchor_side, other_side, volume_next)

def tile_order(values):
    extra = values.shape[4:]
    shaped = values.reshape((N_GX, N_GY, N_GZ, BX, BY, BZ, 27) + extra)
    permute = (0, 3, 1, 4, 2, 5, 6) + tuple(range(7, 7 + len(extra)))
    return shaped.transpose(permute).reshape((TX, TY, TZ, 27) + extra)

def reference(positions, grain_radii, film_liquid, pair_live, partner, rupture, volume):
    grain_state = jnp.concatenate([positions, grain_radii[None], film_liquid[None]], axis=0)
    padded = jnp.pad(grain_state, ((0, 0), (1, 1), (1, 1), (1, 1), (0, 0)))
    tile_count = TX * TY * TZ
    groups = tile_count // (BX * BY * BZ)
    active = tile_order(pair_live).astype(jnp.float32)
    partners = tile_order(partner)
    ruptures = tile_order(rupture)
    volumes = tile_order(volume)
    anchor = grain_state.reshape(5, tile_count, GRAINS).transpose(1, 0, 2)
    totals = jnp.zeros((4, TX + 2, TY + 2, TZ + 2, GRAINS), jnp.float32)
    updated = []
    for number, offset in enumerate(shell_offsets):
        start = (0, 1 + offset[0], 1 + offset[1], 1 + offset[2], 0)
        limit = (5, 1 + offset[0] + TX, 1 + offset[1] + TY, 1 + offset[2] + TZ, GRAINS)
        others = lax.slice(padded, start, limit).reshape(5, tile_count, GRAINS).transpose(1, 0, 2)
        centre = jnp.full((tile_count,), 1.0 if number == 13 else 0.0, jnp.float32)
        pieces = (anchor, others, centre, active[:, :, :, number].reshape(tile_count), partners[:, :, :, number].reshape(tile_count, GRAINS), ruptures[:, :, :, number].reshape(tile_count, GRAINS), volumes[:, :, :, number].reshape(tile_count, GRAINS))
        blocked = jax.tree.map(lambda member: member.reshape((groups, tile_count // groups) + member.shape[1:]), pieces)
        anchor_side, other_side, fresh = lax.map(evaluate, blocked)
        anchor_side = anchor_side.reshape(tile_count, 4, GRAINS).transpose(1, 0, 2).reshape(4, TX, TY, TZ, GRAINS)
        other_side = other_side.reshape(tile_count, 4, GRAINS).transpose(1, 0, 2).reshape(4, TX, TY, TZ, GRAINS)
        totals = totals.at[:, 1:TX + 1, 1:TY + 1, 1:TZ + 1].add(anchor_side)
        totals = totals.at[:, 1 + offset[0]:1 + offset[0] + TX, 1 + offset[1]:1 + offset[1] + TY, 1 + offset[2]:1 + offset[2] + TZ].add(other_side)
        updated.append(fresh.reshape(TX, TY, TZ, GRAINS))
    stacked = jnp.stack(updated, axis=3).reshape(N_GX, BX, N_GY, BY, N_GZ, BZ, 27, GRAINS)
    volume_next = stacked.transpose(0, 2, 4, 1, 3, 5, 6, 7).reshape(N_GX, N_GY, N_GZ, 27 * BX * BY * BZ, GRAINS)
    interior = totals[:, 1:TX + 1, 1:TY + 1, 1:TZ + 1]
    return (interior[:3], film_liquid + interior[3], volume_next)
```

```python
import functools

import jax
import jax.numpy as jnp
from jax import lax
from jax.experimental import pallas as pl
from jax.experimental.pallas import tpu as pltpu
from jax.sharding import PartitionSpec as P

ABSORB = 0.02
TINY = 1e-30
RADIUS_MAX = 0.6
SLACK = 4e-3
AWAY = -1e4
FLOOR = 1e-12


def neighbours():
    return [
        (ex, ey, ez)
        for ex in (-1, 0, 1)
        for ey in (-1, 0, 1)
        for ez in (-1, 0, 1)
        if (ex, ey, ez) != (0, 0, 0)
    ]


AXES = ("gx", "gy", "gz")


def present(offset):
    found = None
    for axis, shift in zip(AXES, offset):
        if shift == 0:
            continue
        place = lax.axis_index(axis) + shift
        here = (place >= 0) & (place < lax.axis_size(axis))
        found = here if found is None else found & here
    return found


def device_at(offset):
    return tuple(lax.axis_index(axis) + shift for axis, shift in zip(AXES, offset))


def opposite(offset):
    return tuple(-shift for shift in offset)


def greet(offsets):
    barrier = pltpu.get_barrier_semaphore()
    count = jnp.int32(0)
    for offset in offsets:
        here = present(offset)
        count = count + here.astype(jnp.int32)

        @pl.when(here)
        def _():
            pl.semaphore_signal(
                barrier, inc=1, device_id=device_at(offset), device_id_type=pl.DeviceIdType.MESH
            )

    pl.semaphore_wait(barrier, count)


def cut(offset, extents, low, whole, high):
    pick = []
    for shift, extent in zip(offset, extents):
        if shift < 0:
            pick.append(pl.ds(low(extent), 1))
        elif shift > 0:
            pick.append(pl.ds(high(extent), 1))
        else:
            pick.append(pl.ds(whole, extent))
    return tuple(pick)


def rim(offset, extents):
    return cut(offset, extents, lambda n: 0, 1, lambda n: n + 1)


def edge(offset, extents):
    return cut(offset, extents, lambda n: 0, 0, lambda n: n - 1)


def spread_kernel(extents, state_ref, border_ref, send_sem, recv_sem):
    offsets = neighbours()
    greet(offsets)
    copies = []
    for i, offset in enumerate(offsets):
        copy = pltpu.make_async_remote_copy(
            src_ref=state_ref.at[edge(offset, extents)],
            dst_ref=border_ref.at[rim(opposite(offset), extents)],
            send_sem=send_sem.at[i],
            recv_sem=recv_sem.at[i],
            device_id=device_at(offset),
            device_id_type=pl.DeviceIdType.MESH,
        )
        copies.append(copy)
        pl.when(present(offset))(copy.start)
    border_ref[rim((0, 0, 0), extents)] = state_ref[...]
    for offset in offsets:

        @pl.when(jnp.logical_not(present(offset)))
        def _():
            region = rim(offset, extents)
            shape = tuple(p.size for p in region) + border_ref.shape[3:]
            border_ref[region] = jnp.zeros(shape, jnp.float32)

    for offset, copy in zip(offsets, copies):
        pl.when(present(offset))(copy.wait_send)
        pl.when(present(opposite(offset)))(copy.wait_recv)


def return_kernel(extents, totals_ref, out_ref, *scratch):
    offsets = neighbours()
    inbox, (send_sem, recv_sem) = scratch[:-2], scratch[-2:]
    greet(offsets)
    copies = []
    for i, offset in enumerate(offsets):
        copy = pltpu.make_async_remote_copy(
            src_ref=totals_ref.at[rim(offset, extents)],
            dst_ref=inbox[i],
            send_sem=send_sem.at[i],
            recv_sem=recv_sem.at[i],
            device_id=device_at(offset),
            device_id_type=pl.DeviceIdType.MESH,
        )
        copies.append(copy)
        pl.when(present(offset))(copy.start)
    out_ref[...] = totals_ref[rim((0, 0, 0), extents)]
    for i, (offset, copy) in enumerate(zip(offsets, copies)):

        @pl.when(present(opposite(offset)))
        def _():
            copy.wait_recv()
            region = edge(opposite(offset), extents)
            out_ref[region] = out_ref[region] + inbox[i][...]

    for offset, copy in zip(offsets, copies):
        pl.when(present(offset))(copy.wait_send)


def spread(state, extents):
    sems = pltpu.SemaphoreType.DMA((26,))
    vmem = pl.BlockSpec(memory_space=pltpu.VMEM)
    shape = tuple(n + 2 for n in extents) + state.shape[3:]
    return pl.pallas_call(
        functools.partial(spread_kernel, extents),
        out_shape=jax.ShapeDtypeStruct(shape, jnp.float32),
        in_specs=[vmem],
        out_specs=vmem,
        scratch_shapes=[sems, sems],
        compiler_params=pltpu.CompilerParams(collective_id=0, has_side_effects=True),
        name="spread",
    )(state)


def collect(totals, extents):
    sems = pltpu.SemaphoreType.DMA((26,))
    vmem = pl.BlockSpec(memory_space=pltpu.VMEM)
    tail = totals.shape[3:]
    boxes = [
        pltpu.VMEM(tuple(1 if e else n for e, n in zip(offset, extents)) + tail, jnp.float32)
        for offset in neighbours()
    ]
    return pl.pallas_call(
        functools.partial(return_kernel, extents),
        out_shape=jax.ShapeDtypeStruct(tuple(extents) + tail, jnp.float32),
        in_specs=[vmem],
        out_specs=vmem,
        scratch_shapes=boxes + [sems, sems],
        compiler_params=pltpu.CompilerParams(collective_id=1, has_side_effects=True),
        name="collect",
    )(totals)


def split(values):
    high = values.astype(jnp.bfloat16)
    low = (values - high.astype(jnp.float32)).astype(jnp.bfloat16)
    return high, low


def kernel(
    dims,
    border_ref,
    live_ref,
    partner_ref,
    rupture_ref,
    volume_ref,
    totals_ref,
    fresh_ref,
    others,
    flags,
    triangle,
    held,
    mask,
    before,
    offset,
    place,
    lists,
    summed,
    owned,
    table,
    acc,
    near,
    far,
    counts,
):
    bx, by, bz, grains = dims
    wy, wz = by + 2, bz + 2
    plane = by * bz
    step = pl.program_id(0)
    cells = (bx + 2) * wy * wz
    f32 = jnp.float32

    def other_row(x, j, c):
        return pl.multiple_of(((x * 9 + j) * 5 + c) * plane, plane)

    def far_row(x, j, c):
        return pl.multiple_of(((x * 9 + j) * 4 + c) * plane, plane)

    @pl.when(step == 0)
    def _():
        near[...] = jnp.zeros_like(near)
        far[...] = jnp.zeros_like(far)
        rows = lax.broadcasted_iota(jnp.int32, (grains, 2 * grains), 0)
        cols = lax.broadcasted_iota(jnp.int32, (grains, 2 * grains), 1)
        triangle[...] = (rows <= cols).astype(f32).astype(jnp.bfloat16)
        flags[...] = jnp.zeros_like(flags)
        for t in range(bx * plane):
            flags[t : t + 1, 0:27] = live_ref[0:1, t * 27 : t * 27 + 27].astype(f32)

        def arrange(x, carry):
            for j in range(9):
                ey, ez = j // 3, j % 3
                for c in range(5):
                    for z in range(bz):
                        start = ((x * wy + ey) * wz + z + ez) * 8 + c
                        got = border_ref[pl.ds(start, by, stride=wz * 8), :]
                        others[pl.ds(((x * 9 + j) * 5 + c) * plane + z, by, stride=bz), :] = got
            return carry

        lax.fori_loop(0, bx + 2, arrange, 0)

    own = [others[pl.ds(other_row(step + 1, 4, c), plane), :] for c in range(5)]
    twice = 2.0 * own[3]
    highs = [jnp.max(own[c], axis=1, keepdims=True) for c in range(3)]
    lows = [jnp.min(own[c], axis=1, keepdims=True) for c in range(3)]
    widest = jnp.max(own[3], axis=1, keepdims=True) + SLACK
    active_of = flags[pl.ds(pl.multiple_of(step * plane, plane), plane), :]
    sums = [jnp.zeros((plane, grains), f32)] * 4
    for s in range(27):
        x, j = step + s // 9, s % 9
        near_by = [others[pl.ds(other_row(x, j, c), plane), :] for c in range(5)]
        lines = pl.ds(s, plane, stride=27)
        partner = partner_ref[lines, :]
        got = [jnp.take_along_axis(member, partner, axis=1) for member in near_by]
        active = jnp.broadcast_to(active_of[:, s : s + 1], (plane, grains))
        gap = [own[c] - got[c] for c in range(3)]
        square = gap[0] * gap[0] + gap[1] * gap[1] + gap[2] * gap[2]
        inverse = lax.rsqrt(square)
        radius_sum = own[3] + got[3]
        product = twice * got[3]
        vol = volume_ref[lines, :]
        root = product * lax.rsqrt(product * (radius_sum * vol))
        scaled = jnp.maximum(square * inverse - radius_sum, 0.0) * root
        broken = rupture_ref[lines, :].astype(f32)
        intact = active * (1.0 - broken)
        curve = 1.0 + scaled * (1.05 + 2.5 * scaled)
        tension = jnp.where(intact > 0.0, product * inverse / (radius_sum * curve), 0.0)
        force = [tension * member for member in gap]
        released = 0.5 * active * broken * vol
        soaked = ABSORB * intact
        from_own = soaked * own[4]
        from_got = soaked * got[4]
        fresh_ref[lines, :] = intact * vol + (from_own + from_got)
        for c, member in enumerate(force + [released - from_got]):
            high = member.astype(jnp.bfloat16).astype(f32)
            held[pl.ds(s * 8 + c, plane, stride=27 * 8), :] = high
            held[pl.ds(s * 8 + c + 4, plane, stride=27 * 8), :] = member - high
        for c in range(3):
            sums[c] = sums[c] - force[c]
        sums[3] = sums[3] + (released - from_own)
        if s == 13:
            mask[s * plane : (s + 1) * plane, :] = jnp.zeros((plane, grains), f32)
        else:
            away = [
                jnp.maximum(jnp.maximum(lows[c] - near_by[c], near_by[c] - highs[c]), 0.0)
                for c in range(3)
            ]
            reach = widest + near_by[3]
            inside = away[0] * away[0] + away[1] * away[1] + away[2] * away[2] < reach * reach
            mask[s * plane : (s + 1) * plane, :] = jnp.where(inside, active, 0.0)
    for c in range(4):
        owned[c] = sums[c]

    prefix = lax.dot_general(
        mask[...].astype(jnp.bfloat16),
        triangle[...],
        (((1,), (0,)), ((), ())),
        preferred_element_type=f32,
    )
    total = jnp.zeros((plane, grains), f32)
    for s in range(27):
        part = slice(s * plane, (s + 1) * plane)
        ahead = prefix[part, 0:grains]
        before[part, :] = ahead
        offset[part, :] = total
        spot = jnp.where(mask[part, :] > 0.0, total + ahead - 1.0, -1.0)
        place[part, :] = spot.astype(jnp.int32)
        total = total + prefix[part, grains : 2 * grains]
    offset[27 * plane : 28 * plane, :] = total
    for t in range(plane):
        counts[t] = total[t, 0].astype(jnp.int32)
    most = jnp.max(total).astype(jnp.int32)
    lane = lax.broadcasted_iota(jnp.int32, (plane, grains), 1)

    def build(group):
        wanted = (lane + group * grains).astype(f32)
        found = [jnp.full((plane, grains), AWAY, f32)] * 3 + [jnp.full((plane, grains), 0.5, f32)]
        for s in range(27):
            if s == 13:
                continue
            part = slice(s * plane, (s + 1) * plane)
            low = offset[part, :]
            high = offset[(s + 1) * plane : (s + 2) * plane, :]
            here = (wanted >= low) & (wanted < high)
            rank = wanted - low
            ahead = before[part, :]
            index = jnp.zeros((plane, grains), jnp.int32)
            bit = grains // 2
            while bit:
                probe = jnp.take_along_axis(ahead, index + (bit - 1), axis=1)
                index = jnp.where(probe <= rank, index + bit, index)
                bit //= 2
            x, j = step + s // 9, s % 9
            for c in range(4):
                member = others[pl.ds(other_row(x, j, c), plane), :]
                found[c] = jnp.where(here, jnp.take_along_axis(member, index, axis=1), found[c])
        for c in range(4):
            lists[c * plane : (c + 1) * plane, :] = found[c]
        lists[4 * plane : 5 * plane, :] = 1.0 / found[3]

    def distribute(group):
        rows = [summed[c * plane : (c + 1) * plane, :] for c in range(3)]
        for s in range(27):
            if s == 13:
                continue
            spot = place[s * plane : (s + 1) * plane, :] - group * grains
            here = (spot >= 0) & (spot < grains)
            index = jnp.clip(spot, 0, grains - 1)
            for c in range(3):
                moved = jnp.where(here, jnp.take_along_axis(rows[c], index, axis=1), 0.0)
                line = pl.ds(far_row(step + s // 9, s % 9, c), plane)
                far[line, :] = far[line, :] - moved

    def cell_of(local):
        return ((step + 1) * wy + local // bz + 1) * wz + local % bz + 1

    def prepare(local):
        block = border_ref[pl.ds(pl.multiple_of(cell_of(local) * 8, 8), 8), :].T
        for n, c in enumerate((0, 1, 2, 3, 5)):
            table[n] = jnp.broadcast_to(block[:, c : c + 1], (grains, grains))

    def pushes(mine, theirs, own_tile):
        deltas = [mine[c] - theirs[c] for c in range(3)]
        square = deltas[0] * deltas[0] + deltas[1] * deltas[1] + deltas[2] * deltas[2]
        if own_tile:
            square = jnp.maximum(square, FLOOR)
        inverse = lax.rsqrt(square)
        inter = jnp.maximum(mine[3] + theirs[3] - square * inverse, TINY)
        push = inter * inter * inverse * lax.rsqrt(inter * (mine[4] + theirs[4]))
        return [push * member for member in deltas]

    def contacts(local, own_tile):
        listed = [
            jnp.broadcast_to(lists[pl.ds(c * plane + local, 1), :], (8, grains)) for c in range(5)
        ]
        cell = cell_of(local)
        selves = [
            jnp.broadcast_to(border_ref[pl.ds(cell * 8 + c, 1), :], (8, grains))
            for c in (0, 1, 2, 3, 5)
        ]
        collected = [jnp.zeros((8, grains), f32)] * 3
        for m in range(grains // 8):
            part = slice(8 * m, 8 * m + 8)
            mine = [table[c, part] for c in range(5)]
            products = pushes(mine, listed, False)
            for c in range(3):
                collected[c] = collected[c] + products[c]
            if own_tile:
                inner = pushes(mine, selves, True)
                products = [a + b for a, b in zip(products, inner)]
            for c in range(3):
                acc[c, part] = products[c]
        for c in range(3):
            line = jnp.sum(collected[c], axis=0, keepdims=True)
            summed[pl.ds(c * plane + local, 1), :] = line
        ones = jnp.ones((8, grains), jnp.bfloat16)
        across = (((1,), (1,)), ((), ()))
        for c in range(3):
            high, low = split(acc[c])
            value = lax.dot_general(ones, high, across, preferred_element_type=f32)
            value = value + lax.dot_general(ones, low, across, preferred_element_type=f32)
            line = pl.ds(local, 1)
            owned[c, line, :] = owned[c, line, :] + value[0:1]

    lanes = lax.broadcasted_iota(jnp.int32, (grains, grains), 0).astype(f32).astype(jnp.bfloat16)
    one = jnp.ones((grains, grains), jnp.bfloat16)
    zero = jnp.zeros((grains, grains), jnp.bfloat16)

    def bridges(local):
        cell = cell_of(local)
        for s in range(27):
            line = local * 27 + s
            values = held[pl.ds(pl.multiple_of(line * 8, 8), 8), :].astype(jnp.bfloat16)
            aim = partner_ref[pl.ds(line, 1), :].astype(f32).astype(jnp.bfloat16)
            chosen = jnp.where(lanes == jnp.broadcast_to(aim, (grains, grains)), one, zero)
            moved = lax.dot_general(
                values, chosen, (((1,), (1,)), ((), ())), preferred_element_type=f32
            )
            target = cell + ((s // 9 - 1) * wy + s // 3 % 3 - 1) * wz + s % 3 - 1
            rows = pl.ds(pl.multiple_of(target * 8, 8), 8)
            near[rows, :] = near[rows, :] + moved

    build(0)

    def tile_step(local, carry):
        prepare(local)
        contacts(local, True)
        bridges(local)
        return carry

    lax.fori_loop(0, plane, tile_step, 0)
    distribute(0)

    def more(group, carry):
        build(group)
        summed[...] = jnp.zeros_like(summed)

        def again(local, inner):
            @pl.when(counts[local] > group * grains)
            def _():
                prepare(local)
                contacts(local, False)

            return inner

        lax.fori_loop(0, plane, again, 0)
        distribute(group)
        return carry

    lax.fori_loop(1, (most + grains - 1) // grains, more, 0)
    for c in range(4):
        line = pl.ds(far_row(step + 1, 4, c), plane)
        far[line, :] = far[line, :] + owned[c]

    @pl.when(step == pl.num_programs(0) - 1)
    def _():
        def fold(x, carry):
            for j in range(9):
                ey, ez = j // 3, j % 3
                for c in range(4 if j == 4 else 3):
                    for z in range(bz):
                        start = ((x * wy + ey) * wz + z + ez) * 8 + c
                        line = pl.ds(start, by, stride=wz * 8)
                        add = far[pl.ds(((x * 9 + j) * 4 + c) * plane + z, by, stride=bz), :]
                        near[line, :] = near[line, :] + add
            return carry

        lax.fori_loop(0, bx + 2, fold, 0)

        def finish(cell, carry):
            value = near[pl.ds(pl.multiple_of(cell * 8, 8), 8), :]
            totals_ref[cell] = value[0:4] + value[4:8]
            return carry

        lax.fori_loop(0, cells, finish, 0)


def shards(positions, grain_radii, film_liquid, pair_live, partner, rupture, volume):
    bx, by, bz, grains = grain_radii.shape
    tiles = bx * by * bz
    slots = 27 * tiles
    cells = (bx + 2) * (by + 2) * (bz + 2)
    extents = (bx, by, bz)
    zero = jnp.zeros_like(grain_radii)
    parts = [positions[c] for c in range(3)]
    parts += [grain_radii, film_liquid, 1.0 / grain_radii, zero, zero]
    state = jnp.stack(parts, axis=3)
    border = spread(state, extents).reshape(cells * 8, grains)
    plane = by * bz
    span = 27 * plane
    wide = pl.BlockSpec((span, grains), lambda i: (i, 0))
    f32 = jnp.float32
    totals, fresh = pl.pallas_call(
        functools.partial(kernel, (bx, by, bz, grains)),
        grid_spec=pltpu.PrefetchScalarGridSpec(
            num_scalar_prefetch=0,
            grid=(bx,),
            in_specs=[
                pl.BlockSpec(border.shape, lambda i: (0, 0)),
                pl.BlockSpec((1, slots), lambda i: (0, 0)),
                wide,
                wide,
                wide,
            ],
            out_specs=[pl.BlockSpec((cells, 4, grains), lambda i: (0, 0, 0)), wide],
            scratch_shapes=[
                pltpu.VMEM(((bx + 2) * 9 * 5 * plane, grains), f32),
                pltpu.VMEM((tiles, grains), f32),
                pltpu.VMEM((grains, 2 * grains), jnp.bfloat16),
                pltpu.VMEM((span * 8, grains), f32),
                pltpu.VMEM((span, grains), f32),
                pltpu.VMEM((span, grains), f32),
                pltpu.VMEM((span + plane, grains), f32),
                pltpu.VMEM((span, grains), jnp.int32),
                pltpu.VMEM((5 * plane, grains), f32),
                pltpu.VMEM((3 * plane, grains), f32),
                pltpu.VMEM((4, plane, grains), f32),
                pltpu.VMEM((5, grains, grains), f32),
                pltpu.VMEM((3, grains, grains), f32),
                pltpu.VMEM((cells * 8, grains), f32),
                pltpu.VMEM(((bx + 2) * 9 * 4 * plane, grains), f32),
                pltpu.SMEM((plane,), jnp.int32),
            ],
        ),
        out_shape=[
            jax.ShapeDtypeStruct((cells, 4, grains), f32),
            jax.ShapeDtypeStruct((slots, grains), f32),
        ],
        name="slots",
    )(
        border,
        pair_live.reshape(1, slots),
        partner.reshape(slots, grains),
        rupture.reshape(slots, grains),
        volume.reshape(slots, grains),
    )
    totals = totals.reshape(bx + 2, by + 2, bz + 2, 4, grains)
    folded = collect(totals, extents).transpose(3, 0, 1, 2, 4)
    return (folded[:3], film_liquid + folded[3], fresh.reshape(1, 1, 1, slots, grains))


def solution(mesh):
    return jax.shard_map(
        shards,
        mesh=mesh,
        in_specs=(
            P(None, "gx", "gy", "gz", None),
            P("gx", "gy", "gz", None),
            P("gx", "gy", "gz", None),
            P("gx", "gy", "gz", None),
            P("gx", "gy", "gz", None, None),
            P("gx", "gy", "gz", None, None),
            P("gx", "gy", "gz", None, None),
        ),
        out_specs=(
            P(None, "gx", "gy", "gz", None),
            P("gx", "gy", "gz", None),
            P("gx", "gy", "gz", None, None),
        ),
        check_vma=False,
    )
```

```python
import functools

import jax
import jax.numpy as jnp
from jax import lax
from jax.experimental import pallas as pl
from jax.experimental.pallas import tpu as pltpu
from jax.sharding import PartitionSpec as P

ABSORB = 0.02
TINY = 1e-30
RADIUS_MAX = 0.6
SLACK = 4e-3
AWAY = -1e4
FLOOR = 1e-12


def neighbours():
    return [
        (ex, ey, ez)
        for ex in (-1, 0, 1)
        for ey in (-1, 0, 1)
        for ez in (-1, 0, 1)
        if (ex, ey, ez) != (0, 0, 0)
    ]


AXES = ("gx", "gy", "gz")


def present(offset):
    found = None
    for axis, shift in zip(AXES, offset):
        if shift == 0:
            continue
        place = lax.axis_index(axis) + shift
        here = (place >= 0) & (place < lax.axis_size(axis))
        found = here if found is None else found & here
    return found


def device_at(offset):
    return tuple(lax.axis_index(axis) + shift for axis, shift in zip(AXES, offset))


def opposite(offset):
    return tuple(-shift for shift in offset)


def greet(offsets):
    barrier = pltpu.get_barrier_semaphore()
    count = jnp.int32(0)
    for offset in offsets:
        here = present(offset)
        count = count + here.astype(jnp.int32)

        @pl.when(here)
        def _():
            pl.semaphore_signal(
                barrier, inc=1, device_id=device_at(offset), device_id_type=pl.DeviceIdType.MESH
            )

    pl.semaphore_wait(barrier, count)


def cut(offset, extents, low, whole, high):
    pick = []
    for shift, extent in zip(offset, extents):
        if shift < 0:
            pick.append(pl.ds(low(extent), 1))
        elif shift > 0:
            pick.append(pl.ds(high(extent), 1))
        else:
            pick.append(pl.ds(whole, extent))
    return tuple(pick)


def rim(offset, extents):
    return cut(offset, extents, lambda n: 0, 1, lambda n: n + 1)


def edge(offset, extents):
    return cut(offset, extents, lambda n: 0, 0, lambda n: n - 1)


def spread_kernel(extents, state_ref, border_ref, send_sem, recv_sem):
    offsets = neighbours()
    greet(offsets)
    copies = []
    for i, offset in enumerate(offsets):
        copy = pltpu.make_async_remote_copy(
            src_ref=state_ref.at[edge(offset, extents)],
            dst_ref=border_ref.at[rim(opposite(offset), extents)],
            send_sem=send_sem.at[i],
            recv_sem=recv_sem.at[i],
            device_id=device_at(offset),
            device_id_type=pl.DeviceIdType.MESH,
        )
        copies.append(copy)
        pl.when(present(offset))(copy.start)
    border_ref[rim((0, 0, 0), extents)] = state_ref[...]
    for offset in offsets:

        @pl.when(jnp.logical_not(present(offset)))
        def _():
            region = rim(offset, extents)
            shape = tuple(p.size for p in region) + border_ref.shape[3:]
            border_ref[region] = jnp.zeros(shape, jnp.float32)

    for offset, copy in zip(offsets, copies):
        pl.when(present(offset))(copy.wait_send)
        pl.when(present(opposite(offset)))(copy.wait_recv)


def return_kernel(extents, totals_ref, out_ref, *scratch):
    offsets = neighbours()
    inbox, (send_sem, recv_sem) = scratch[:-2], scratch[-2:]
    greet(offsets)
    copies = []
    for i, offset in enumerate(offsets):
        copy = pltpu.make_async_remote_copy(
            src_ref=totals_ref.at[rim(offset, extents)],
            dst_ref=inbox[i],
            send_sem=send_sem.at[i],
            recv_sem=recv_sem.at[i],
            device_id=device_at(offset),
            device_id_type=pl.DeviceIdType.MESH,
        )
        copies.append(copy)
        pl.when(present(offset))(copy.start)
    out_ref[...] = totals_ref[rim((0, 0, 0), extents)]
    for i, (offset, copy) in enumerate(zip(offsets, copies)):

        @pl.when(present(opposite(offset)))
        def _():
            copy.wait_recv()
            region = edge(opposite(offset), extents)
            out_ref[region] = out_ref[region] + inbox[i][...]

    for offset, copy in zip(offsets, copies):
        pl.when(present(offset))(copy.wait_send)


def spread(state, extents):
    sems = pltpu.SemaphoreType.DMA((26,))
    vmem = pl.BlockSpec(memory_space=pltpu.VMEM)
    shape = tuple(n + 2 for n in extents) + state.shape[3:]
    return pl.pallas_call(
        functools.partial(spread_kernel, extents),
        out_shape=jax.ShapeDtypeStruct(shape, jnp.float32),
        in_specs=[vmem],
        out_specs=vmem,
        scratch_shapes=[sems, sems],
        compiler_params=pltpu.CompilerParams(collective_id=0, has_side_effects=True),
        name="spread",
    )(state)


def collect(totals, extents):
    sems = pltpu.SemaphoreType.DMA((26,))
    vmem = pl.BlockSpec(memory_space=pltpu.VMEM)
    tail = totals.shape[3:]
    boxes = [
        pltpu.VMEM(tuple(1 if e else n for e, n in zip(offset, extents)) + tail, jnp.float32)
        for offset in neighbours()
    ]
    return pl.pallas_call(
        functools.partial(return_kernel, extents),
        out_shape=jax.ShapeDtypeStruct(tuple(extents) + tail, jnp.float32),
        in_specs=[vmem],
        out_specs=vmem,
        scratch_shapes=boxes + [sems, sems],
        compiler_params=pltpu.CompilerParams(collective_id=1, has_side_effects=True),
        name="collect",
    )(totals)


def split(values):
    high = values.astype(jnp.bfloat16)
    low = (values - high.astype(jnp.float32)).astype(jnp.bfloat16)
    return high, low


def take(values, index):
    return jnp.take_along_axis(
        values, index, axis=1, mode="promise_in_bounds", wrap_negative_indices=False
    )


def kernel(
    dims,
    border_ref,
    live_ref,
    partner_ref,
    rupture_ref,
    volume_ref,
    totals_ref,
    fresh_ref,
    others,
    flags,
    triangle,
    held,
    mask,
    before,
    offset,
    place,
    lists,
    summed,
    owned,
    table,
    acc,
    near,
    far,
    counts,
):
    bx, by, bz, grains = dims
    wy, wz = by + 2, bz + 2
    plane = by * bz
    step = pl.program_id(0)
    cells = (bx + 2) * wy * wz
    f32 = jnp.float32

    def other_row(x, j, c):
        return pl.multiple_of(((x * 9 + j) * 5 + c) * plane, plane)

    def far_row(x, j, c):
        return pl.multiple_of(((x * 9 + j) * 4 + c) * plane, plane)

    @pl.when(step == 0)
    def _():
        near[...] = jnp.zeros_like(near)
        far[...] = jnp.zeros_like(far)
        rows = lax.broadcasted_iota(jnp.int32, (grains, 2 * grains), 0)
        cols = lax.broadcasted_iota(jnp.int32, (grains, 2 * grains), 1)
        triangle[...] = (rows <= cols).astype(f32).astype(jnp.bfloat16)
        flags[...] = jnp.zeros_like(flags)
        for t in range(bx * plane):
            flags[t : t + 1, 0:27] = live_ref[0:1, t * 27 : t * 27 + 27].astype(f32)

        def arrange(x, carry):
            for j in range(9):
                ey, ez = j // 3, j % 3
                for c in range(5):
                    for z in range(bz):
                        start = ((x * wy + ey) * wz + z + ez) * 8 + c
                        got = border_ref[pl.ds(start, by, stride=wz * 8), :]
                        others[pl.ds(((x * 9 + j) * 5 + c) * plane + z, by, stride=bz), :] = got
            return carry

        lax.fori_loop(0, bx + 2, arrange, 0)

    def plane_of(x):
        return pl.ds(pl.multiple_of(x * plane, plane), plane)

    def prescan(x):
        mine = [others[pl.ds(other_row(x + 1, 4, c), plane), :] for c in range(4)]
        highs = [jnp.max(mine[c], axis=1, keepdims=True) for c in range(3)]
        lows = [jnp.min(mine[c], axis=1, keepdims=True) for c in range(3)]
        widest = jnp.max(mine[3], axis=1, keepdims=True) + SLACK
        listed = flags[plane_of(x), :]

        def select(s):
            part = slice(s * plane, (s + 1) * plane)
            if s == 13:
                mask[part, :] = jnp.zeros((plane, grains), f32)
                return
            there = [others[pl.ds(other_row(x + s // 9, s % 9, c), plane), :] for c in range(4)]
            away = [
                jnp.maximum(jnp.maximum(lows[c] - there[c], there[c] - highs[c]), 0.0)
                for c in range(3)
            ]
            reach = widest + there[3]
            inside = away[0] * away[0] + away[1] * away[1] + away[2] * away[2] < reach * reach
            active = jnp.broadcast_to(listed[:, s : s + 1], (plane, grains))
            mask[part, :] = jnp.where(inside, active, 0.0)

        return select

    def scan(slot):
        prefix = lax.dot_general(
            mask[...].astype(jnp.bfloat16),
            triangle[...],
            (((1,), (0,)), ((), ())),
            preferred_element_type=f32,
        )
        total = jnp.zeros((plane, grains), f32)
        for s in range(27):
            part = slice(s * plane, (s + 1) * plane)
            ahead = prefix[part, 0:grains]
            before[slot, part, :] = ahead
            offset[slot, part, :] = total
            spot = jnp.where(mask[part, :] > 0.0, total + ahead - 1.0, -1.0)
            place[slot, part, :] = spot.astype(jnp.int32)
            total = total + prefix[part, grains : 2 * grains]
        offset[slot, 27 * plane : 28 * plane, :] = total
        for t in range(plane):
            counts[slot, t] = total[t, 0].astype(jnp.int32)
        counts[slot, plane] = jnp.max(total).astype(jnp.int32)

    now = step % 2
    lane = lax.broadcasted_iota(jnp.int32, (plane, grains), 1)
    outer = [s for s in range(27) if s != 13]

    def build(group, beside):
        wanted = (lane + group * grains).astype(f32)
        index = {s: jnp.zeros((plane, grains), jnp.int32) for s in outer}
        bit = grains // 2
        level = 0
        while bit:
            for s in outer:
                part = slice(s * plane, (s + 1) * plane)
                rank = wanted - offset[now, part, :]
                probe = take(before[now, part, :], index[s] + (bit - 1))
                index[s] = jnp.where(probe <= rank, index[s] + bit, index[s])
            for work in beside[level::7]:
                work()
            bit //= 2
            level += 1
        found = [jnp.full((plane, grains), AWAY, f32)] * 3 + [jnp.full((plane, grains), 0.5, f32)]
        for s in outer:
            low = offset[now, s * plane : (s + 1) * plane, :]
            high = offset[now, (s + 1) * plane : (s + 2) * plane, :]
            here = (wanted >= low) & (wanted < high)
            for c in range(4):
                member = others[pl.ds(other_row(step + s // 9, s % 9, c), plane), :]
                found[c] = jnp.where(here, take(member, index[s]), found[c])
        for c in range(4):
            lists[c * plane : (c + 1) * plane, :] = found[c]
        lists[4 * plane : 5 * plane, :] = 1.0 / found[3]

    @pl.when(step == 0)
    def _():
        select = prescan(0)
        for s in range(27):
            select(s)
        scan(0)

    own = [others[pl.ds(other_row(step + 1, 4, c), plane), :] for c in range(5)]
    twice = 2.0 * own[3]
    active_of = flags[plane_of(step), :]
    sums = [jnp.zeros((plane, grains), f32)] * 4
    select = prescan(jnp.minimum(step + 1, bx - 1))

    def bridge(s):
        near_by = [others[pl.ds(other_row(step + s // 9, s % 9, c), plane), :] for c in range(5)]
        lines = pl.ds(s, plane, stride=27)
        partner = partner_ref[lines, :]
        got = [take(member, partner) for member in near_by]
        active = jnp.broadcast_to(active_of[:, s : s + 1], (plane, grains))
        gap = [own[c] - got[c] for c in range(3)]
        square = gap[0] * gap[0] + gap[1] * gap[1] + gap[2] * gap[2]
        inverse = lax.rsqrt(square)
        radius_sum = own[3] + got[3]
        product = twice * got[3]
        vol = volume_ref[lines, :]
        root = product * lax.rsqrt(product * (radius_sum * vol))
        scaled = jnp.maximum(square * inverse - radius_sum, 0.0) * root
        broken = rupture_ref[lines, :].astype(f32)
        intact = active * (1.0 - broken)
        curve = 1.0 + scaled * (1.05 + 2.5 * scaled)
        tension = jnp.where(intact > 0.0, product * inverse / (radius_sum * curve), 0.0)
        force = [tension * member for member in gap]
        released = 0.5 * active * broken * vol
        soaked = ABSORB * intact
        from_own = soaked * own[4]
        from_got = soaked * got[4]
        fresh_ref[lines, :] = intact * vol + (from_own + from_got)
        for c, member in enumerate(force + [released - from_got]):
            high = member.astype(jnp.bfloat16).astype(f32)
            held[pl.ds(s * 8 + c, plane, stride=27 * 8), :] = high
            held[pl.ds(s * 8 + c + 4, plane, stride=27 * 8), :] = member - high
        for c in range(3):
            sums[c] = sums[c] - force[c]
        sums[3] = sums[3] + (released - from_own)
        select(s)

    build(0, [functools.partial(bridge, s) for s in range(27)])
    for c in range(4):
        owned[c] = sums[c]
    most = counts[now, plane]

    def distribute(group):
        rows = [summed[c * plane : (c + 1) * plane, :] for c in range(3)]
        for s in outer:
            spot = place[now, s * plane : (s + 1) * plane, :] - group * grains
            here = (spot >= 0) & (spot < grains)
            index = spot & (grains - 1)
            for c in range(3):
                moved = jnp.where(here, take(rows[c], index), 0.0)
                line = pl.ds(far_row(step + s // 9, s % 9, c), plane)
                far[line, :] = far[line, :] - moved

    def cell_at(tile):
        x, local = tile // plane, tile % plane
        return ((x + 1) * wy + local // bz + 1) * wz + local % bz + 1

    def columns_of(cell):
        return border_ref[pl.ds(pl.multiple_of(cell * 8, 8), 8), :].T

    def spread_columns(slot, columns, m):
        part = slice(8 * m, 8 * m + 8)
        for n, c in enumerate((0, 1, 2, 3, 5)):
            table[slot, n, part] = jnp.broadcast_to(columns[part, c : c + 1], (8, grains))

    def pushes(mine, theirs, own_tile):
        deltas = [mine[c] - theirs[c] for c in range(3)]
        square = deltas[0] * deltas[0] + deltas[1] * deltas[1] + deltas[2] * deltas[2]
        if own_tile:
            square = jnp.maximum(square, FLOOR)
        inverse = lax.rsqrt(square)
        inter = jnp.maximum(mine[3] + theirs[3] - square * inverse, TINY)
        push = inter * inter * inverse * lax.rsqrt(inter * (mine[4] + theirs[4]))
        return [push * member for member in deltas]

    def contacts(local, slot, own_tile, beside):
        listed = [
            jnp.broadcast_to(lists[pl.ds(c * plane + local, 1), :], (8, grains)) for c in range(5)
        ]
        cell = cell_at(step * plane + local)
        selves = [
            jnp.broadcast_to(border_ref[pl.ds(cell * 8 + c, 1), :], (8, grains))
            for c in (0, 1, 2, 3, 5)
        ]
        collected = [jnp.zeros((8, grains), f32)] * 3
        for m in range(grains // 8):
            part = slice(8 * m, 8 * m + 8)
            mine = [table[slot, c, part] for c in range(5)]
            products = pushes(mine, listed, False)
            for c in range(3):
                collected[c] = collected[c] + products[c]
            if own_tile:
                inner = pushes(mine, selves, True)
                products = [a + b for a, b in zip(products, inner)]
            for c in range(3):
                acc[c, part] = products[c]
            beside(m)
        for c in range(3):
            line = jnp.sum(collected[c], axis=0, keepdims=True)
            summed[pl.ds(c * plane + local, 1), :] = line
        ones = jnp.ones((8, 2 * grains), jnp.bfloat16)
        for c in range(3):
            both = jnp.concatenate(split(acc[c]), axis=1)
            value = lax.dot_general(ones, both, across, preferred_element_type=f32)
            line = pl.ds(local, 1)
            owned[c, line, :] = owned[c, line, :] + value[0:1]

    across = (((1,), (1,)), ((), ()))
    lanes = lax.broadcasted_iota(jnp.int32, (grains, grains), 0).astype(f32).astype(jnp.bfloat16)
    one = jnp.ones((grains, grains), jnp.bfloat16)
    zero = jnp.zeros((grains, grains), jnp.bfloat16)
    blank = jnp.zeros((8, grains), jnp.bfloat16)

    def bridges(local, pair):
        cell = cell_at(step * plane + local)
        slots = pair if len(pair) == 2 else (pair[0], pair[0])
        chosen, left = [], []
        for s in slots:
            line = local * 27 + s
            left.append(held[pl.ds(pl.multiple_of(line * 8, 8), 8), :])
            aim = partner_ref[pl.ds(line, 1), :].astype(f32).astype(jnp.bfloat16)
            chosen.append(jnp.where(lanes == jnp.broadcast_to(aim, (grains, grains)), one, zero))
        none = jnp.zeros((8, grains), f32)
        first = jnp.concatenate([left[0], none], axis=0).astype(jnp.bfloat16)
        second = jnp.concatenate([none, left[1]], axis=0).astype(jnp.bfloat16)
        moved = lax.dot_general(
            jnp.concatenate([first, second], axis=1),
            jnp.concatenate(chosen, axis=1),
            across,
            preferred_element_type=f32,
        )
        for n, s in enumerate(pair):
            target = cell + ((s // 9 - 1) * wy + s // 3 % 3 - 1) * wz + s % 3 - 1
            rows = pl.ds(pl.multiple_of(target * 8, 8), 8)
            near[rows, :] = near[rows, :] + moved[8 * n : 8 * n + 8]

    pairs = [tuple(range(27)[n : n + 2]) for n in range(0, 27, 2)]

    @pl.when(step == 0)
    def _():
        columns = columns_of(cell_at(0))
        for m in range(grains // 8):
            spread_columns(0, columns, m)

    def tile_step(local, carry):
        tile = step * plane + local
        columns = columns_of(cell_at(jnp.minimum(tile + 1, bx * plane - 1)))

        def beside(m):
            spread_columns((tile + 1) % 2, columns, m)
            for pair in pairs[m :: grains // 8]:
                bridges(local, pair)

        contacts(local, tile % 2, True, beside)
        return carry

    lax.fori_loop(0, plane, tile_step, 0)
    distribute(0)

    def more(group, carry):
        build(group, [])
        summed[...] = jnp.zeros_like(summed)

        def again(local, inner):
            @pl.when(counts[now, local] > group * grains)
            def _():
                columns = columns_of(cell_at(step * plane + local))
                for m in range(grains // 8):
                    spread_columns(2, columns, m)
                contacts(local, 2, False, lambda m: None)

            return inner

        lax.fori_loop(0, plane, again, 0)
        distribute(group)
        return carry

    lax.fori_loop(1, (most + grains - 1) // grains, more, 0)
    scan(1 - now)
    for c in range(4):
        line = pl.ds(far_row(step + 1, 4, c), plane)
        far[line, :] = far[line, :] + owned[c]

    @pl.when(step == pl.num_programs(0) - 1)
    def _():
        def fold(x, carry):
            for j in range(9):
                ey, ez = j // 3, j % 3
                for c in range(4 if j == 4 else 3):
                    for z in range(bz):
                        start = ((x * wy + ey) * wz + z + ez) * 8 + c
                        line = pl.ds(start, by, stride=wz * 8)
                        add = far[pl.ds(((x * 9 + j) * 4 + c) * plane + z, by, stride=bz), :]
                        near[line, :] = near[line, :] + add
            return carry

        lax.fori_loop(0, bx + 2, fold, 0)

        def finish(cell, carry):
            value = near[pl.ds(pl.multiple_of(cell * 8, 8), 8), :]
            totals_ref[cell] = value[0:4] + value[4:8]
            return carry

        lax.fori_loop(0, cells, finish, 0)


def shards(positions, grain_radii, film_liquid, pair_live, partner, rupture, volume):
    bx, by, bz, grains = grain_radii.shape
    tiles = bx * by * bz
    slots = 27 * tiles
    cells = (bx + 2) * (by + 2) * (bz + 2)
    extents = (bx, by, bz)
    zero = jnp.zeros_like(grain_radii)
    parts = [positions[c] for c in range(3)]
    parts += [grain_radii, film_liquid, 1.0 / grain_radii, zero, zero]
    state = jnp.stack(parts, axis=3)
    border = spread(state, extents).reshape(cells * 8, grains)
    plane = by * bz
    span = 27 * plane
    wide = pl.BlockSpec((span, grains), lambda i: (i, 0))
    f32 = jnp.float32
    totals, fresh = pl.pallas_call(
        functools.partial(kernel, (bx, by, bz, grains)),
        grid_spec=pltpu.PrefetchScalarGridSpec(
            num_scalar_prefetch=0,
            grid=(bx,),
            in_specs=[
                pl.BlockSpec(border.shape, lambda i: (0, 0)),
                pl.BlockSpec((1, slots), lambda i: (0, 0)),
                wide,
                wide,
                wide,
            ],
            out_specs=[pl.BlockSpec((cells, 4, grains), lambda i: (0, 0, 0)), wide],
            scratch_shapes=[
                pltpu.VMEM(((bx + 2) * 9 * 5 * plane, grains), f32),
                pltpu.VMEM((tiles, grains), f32),
                pltpu.VMEM((grains, 2 * grains), jnp.bfloat16),
                pltpu.VMEM((span * 8, grains), f32),
                pltpu.VMEM((span, grains), f32),
                pltpu.VMEM((2, span, grains), f32),
                pltpu.VMEM((2, span + plane, grains), f32),
                pltpu.VMEM((2, span, grains), jnp.int32),
                pltpu.VMEM((5 * plane, grains), f32),
                pltpu.VMEM((3 * plane, grains), f32),
                pltpu.VMEM((4, plane, grains), f32),
                pltpu.VMEM((3, 5, grains, grains), f32),
                pltpu.VMEM((3, grains, grains), f32),
                pltpu.VMEM((cells * 8, grains), f32),
                pltpu.VMEM(((bx + 2) * 9 * 4 * plane, grains), f32),
                pltpu.SMEM((2, plane + 1), jnp.int32),
            ],
        ),
        out_shape=[
            jax.ShapeDtypeStruct((cells, 4, grains), f32),
            jax.ShapeDtypeStruct((slots, grains), f32),
        ],
        name="slots",
    )(
        border,
        pair_live.reshape(1, slots),
        partner.reshape(slots, grains),
        rupture.reshape(slots, grains),
        volume.reshape(slots, grains),
    )
    totals = totals.reshape(bx + 2, by + 2, bz + 2, 4, grains)
    folded = collect(totals, extents).transpose(3, 0, 1, 2, 4)
    return (folded[:3], film_liquid + folded[3], fresh.reshape(1, 1, 1, slots, grains))


def solution(mesh):
    return jax.shard_map(
        shards,
        mesh=mesh,
        in_specs=(
            P(None, "gx", "gy", "gz", None),
            P("gx", "gy", "gz", None),
            P("gx", "gy", "gz", None),
            P("gx", "gy", "gz", None),
            P("gx", "gy", "gz", None, None),
            P("gx", "gy", "gz", None, None),
            P("gx", "gy", "gz", None, None),
        ),
        out_specs=(
            P(None, "gx", "gy", "gz", None),
            P("gx", "gy", "gz", None),
            P("gx", "gy", "gz", None, None),
        ),
        check_vma=False,
    )
```

```python
import functools

import jax
import jax.numpy as jnp
from jax import lax
from jax.experimental import pallas as pl
from jax.experimental.pallas import tpu as pltpu
from jax.sharding import PartitionSpec as P

ABSORB = 0.02
TINY = 1e-30
RADIUS_MAX = 0.6
SLACK = 4e-3
AWAY = -1e4
FLOOR = 1e-12


def neighbours():
    return [
        (ex, ey, ez)
        for ex in (-1, 0, 1)
        for ey in (-1, 0, 1)
        for ez in (-1, 0, 1)
        if (ex, ey, ez) != (0, 0, 0)
    ]


AXES = ("gx", "gy", "gz")


def present(offset):
    found = None
    for axis, shift in zip(AXES, offset):
        if shift == 0:
            continue
        place = lax.axis_index(axis) + shift
        here = (place >= 0) & (place < lax.axis_size(axis))
        found = here if found is None else found & here
    return found


def device_at(offset):
    return tuple(lax.axis_index(axis) + shift for axis, shift in zip(AXES, offset))


def opposite(offset):
    return tuple(-shift for shift in offset)


def greet(offsets):
    barrier = pltpu.get_barrier_semaphore()
    count = jnp.int32(0)
    for offset in offsets:
        here = present(offset)
        count = count + here.astype(jnp.int32)

        @pl.when(here)
        def _():
            pl.semaphore_signal(
                barrier, inc=1, device_id=device_at(offset), device_id_type=pl.DeviceIdType.MESH
            )

    pl.semaphore_wait(barrier, count)


def cut(offset, extents, low, whole, high):
    pick = []
    for shift, extent in zip(offset, extents):
        if shift < 0:
            pick.append(pl.ds(low(extent), 1))
        elif shift > 0:
            pick.append(pl.ds(high(extent), 1))
        else:
            pick.append(pl.ds(whole, extent))
    return (slice(None),) + tuple(pick)


def rim(offset, extents):
    return cut(offset, extents, lambda n: 0, 1, lambda n: n + 1)


def edge(offset, extents):
    return cut(offset, extents, lambda n: 0, 0, lambda n: n - 1)


def spread_kernel(
    extents, place_ref, radius_ref, film_ref, border_ref, state, blank, local_sem, send_sem, recv_sem
):
    offsets = neighbours()
    loads = [
        pltpu.make_async_copy(place_ref, state.at[pl.ds(0, 3)], local_sem.at[0]),
        pltpu.make_async_copy(radius_ref, state.at[pl.ds(3, 1)], local_sem.at[1]),
        pltpu.make_async_copy(film_ref, state.at[pl.ds(4, 1)], local_sem.at[2]),
    ]
    for load in loads:
        load.start()
    greet(offsets)
    blank[...] = jnp.zeros_like(blank)
    for load in loads:
        load.wait()
    copies, fills = [], []
    for i, offset in enumerate(offsets):
        copy = pltpu.make_async_remote_copy(
            src_ref=state.at[edge(offset, extents)],
            dst_ref=border_ref.at[rim(opposite(offset), extents)],
            send_sem=send_sem.at[i],
            recv_sem=recv_sem.at[i],
            device_id=device_at(offset),
            device_id_type=pl.DeviceIdType.MESH,
        )
        copies.append(copy)
        pl.when(present(offset))(copy.start)
    inner = pltpu.make_async_copy(
        state, border_ref.at[rim((0, 0, 0), extents)], local_sem.at[3]
    )
    inner.start()
    for i, offset in enumerate(offsets):
        fill = pltpu.make_async_copy(
            blank.at[edge(offset, extents)],
            border_ref.at[rim(offset, extents)],
            local_sem.at[4 + i],
        )
        fills.append(fill)
        pl.when(jnp.logical_not(present(offset)))(fill.start)
    inner.wait()
    for offset, copy, fill in zip(offsets, copies, fills):
        pl.when(jnp.logical_not(present(offset)))(fill.wait)
        pl.when(present(offset))(copy.wait_send)
        pl.when(present(opposite(offset)))(copy.wait_recv)


def return_kernel(extents, totals_ref, film_ref, force_ref, next_ref, *scratch):
    offsets = neighbours()
    inbox, (inner, local_sem, send_sem, recv_sem) = scratch[:-4], scratch[-4:]
    load = pltpu.make_async_copy(totals_ref.at[rim((0, 0, 0), extents)], inner, local_sem)
    load.start()
    greet(offsets)
    copies = []
    for i, offset in enumerate(offsets):
        copy = pltpu.make_async_remote_copy(
            src_ref=totals_ref.at[rim(offset, extents)],
            dst_ref=inbox[i],
            send_sem=send_sem.at[i],
            recv_sem=recv_sem.at[i],
            device_id=device_at(offset),
            device_id_type=pl.DeviceIdType.MESH,
        )
        copies.append(copy)
        pl.when(present(offset))(copy.start)
    load.wait()
    force_ref[...] = inner[0:3]
    next_ref[...] = film_ref[...] + inner[3:4]
    order = sorted(range(len(offsets)), key=lambda i: sum(map(abs, offsets[i])))
    for i in order:
        offset, copy = offsets[i], copies[i]

        @pl.when(present(opposite(offset)))
        def _():
            copy.wait_recv()
            region = edge(opposite(offset), extents)
            got = inbox[i][...]
            force_ref[region] = force_ref[region] + got[0:3]
            next_ref[region] = next_ref[region] + got[3:4]

    for offset, copy in zip(offsets, copies):
        pl.when(present(offset))(copy.wait_send)


def spread(place, radius, film, extents):
    sems = pltpu.SemaphoreType.DMA((26,))
    anywhere = pl.BlockSpec(memory_space=pl.ANY)
    tail = place.shape[4:]
    shape = (5,) + tuple(n + 2 for n in extents) + tail
    own = pltpu.VMEM((5,) + tuple(extents) + tail, jnp.float32)
    return pl.pallas_call(
        functools.partial(spread_kernel, extents),
        out_shape=jax.ShapeDtypeStruct(shape, jnp.float32),
        in_specs=[anywhere] * 3,
        out_specs=anywhere,
        scratch_shapes=[own, own, pltpu.SemaphoreType.DMA((30,)), sems, sems],
        compiler_params=pltpu.CompilerParams(collective_id=0, has_side_effects=True),
        name="spread",
    )(place, radius, film)


def collect(totals, film, extents):
    sems = pltpu.SemaphoreType.DMA((26,))
    vmem = pl.BlockSpec(memory_space=pltpu.VMEM)
    tail = totals.shape[4:]
    boxes = [
        pltpu.VMEM(
            (4,) + tuple(1 if e else n for e, n in zip(offset, extents)) + tail, jnp.float32
        )
        for offset in neighbours()
    ]
    return pl.pallas_call(
        functools.partial(return_kernel, extents),
        out_shape=[
            jax.ShapeDtypeStruct((3,) + tuple(extents) + tail, jnp.float32),
            jax.ShapeDtypeStruct((1,) + tuple(extents) + tail, jnp.float32),
        ],
        in_specs=[pl.BlockSpec(memory_space=pl.ANY), vmem],
        out_specs=[vmem, vmem],
        scratch_shapes=boxes
        + [
            pltpu.VMEM((4,) + tuple(extents) + tail, jnp.float32),
            pltpu.SemaphoreType.DMA,
            sems,
            sems,
        ],
        compiler_params=pltpu.CompilerParams(collective_id=1, has_side_effects=True),
        name="collect",
    )(totals, film)


def split(values):
    high = values.astype(jnp.bfloat16)
    low = (values - high.astype(jnp.float32)).astype(jnp.bfloat16)
    return high, low


def take(values, index):
    return jnp.take_along_axis(
        values, index, axis=1, mode="promise_in_bounds", wrap_negative_indices=False
    )


def kernel(
    dims,
    border_ref,
    live_ref,
    partner_ref,
    rupture_ref,
    volume_ref,
    totals_ref,
    fresh_ref,
    others,
    flags,
    triangle,
    held,
    mask,
    before,
    offset,
    place,
    lists,
    summed,
    owned,
    table,
    acc,
    near,
    far,
    counts,
):
    bx, by, bz, grains = dims
    wy, wz = by + 2, bz + 2
    plane = by * bz
    step = pl.program_id(0)
    cells = (bx + 2) * wy * wz
    f32 = jnp.float32

    def other_row(x, j, c):
        return pl.multiple_of(((x * 9 + j) * 6 + c) * plane, plane)

    def far_row(x, j, c):
        return pl.multiple_of(((x * 9 + j) * 4 + c) * plane, plane)

    @pl.when(step == 0)
    def _():
        near[...] = jnp.zeros_like(near)
        far[...] = jnp.zeros_like(far)
        rows = lax.broadcasted_iota(jnp.int32, (grains, 2 * grains), 0)
        cols = lax.broadcasted_iota(jnp.int32, (grains, 2 * grains), 1)
        triangle[...] = (rows <= cols).astype(f32).astype(jnp.bfloat16)
        flags[...] = jnp.zeros_like(flags)
        for t in range(bx * plane):
            flags[t : t + 1, 0:27] = live_ref[0:1, t * 27 : t * 27 + 27].astype(f32)

        def arrange(x, carry):
            for j in range(9):
                ey, ez = j // 3, j % 3
                for c in range(5):
                    for z in range(bz):
                        start = c * cells + (x * wy + ey) * wz + z + ez
                        got = border_ref[pl.ds(start, by, stride=wz), :]
                        others[pl.ds(((x * 9 + j) * 6 + c) * plane + z, by, stride=bz), :] = got
            for j in range(9):
                radius = others[pl.ds(other_row(x, j, 3), plane), :]
                others[pl.ds(other_row(x, j, 5), plane), :] = 1.0 / radius
            return carry

        lax.fori_loop(0, bx + 2, arrange, 0)

    def plane_of(x):
        return pl.ds(pl.multiple_of(x * plane, plane), plane)

    def prescan(x):
        mine = [others[pl.ds(other_row(x + 1, 4, c), plane), :] for c in range(4)]
        highs = [jnp.max(mine[c], axis=1, keepdims=True) for c in range(3)]
        lows = [jnp.min(mine[c], axis=1, keepdims=True) for c in range(3)]
        widest = jnp.max(mine[3], axis=1, keepdims=True) + SLACK
        listed = flags[plane_of(x), :]

        def select(s):
            part = slice(s * plane, (s + 1) * plane)
            if s == 13:
                mask[part, :] = jnp.zeros((plane, grains), f32)
                return
            there = [others[pl.ds(other_row(x + s // 9, s % 9, c), plane), :] for c in range(4)]
            away = [
                jnp.maximum(jnp.maximum(lows[c] - there[c], there[c] - highs[c]), 0.0)
                for c in range(3)
            ]
            reach = widest + there[3]
            inside = away[0] * away[0] + away[1] * away[1] + away[2] * away[2] < reach * reach
            active = jnp.broadcast_to(listed[:, s : s + 1], (plane, grains))
            mask[part, :] = jnp.where(inside, active, 0.0)

        return select

    def scan(slot):
        prefix = lax.dot_general(
            mask[...].astype(jnp.bfloat16),
            triangle[...],
            (((1,), (0,)), ((), ())),
            preferred_element_type=f32,
        )
        total = jnp.zeros((plane, grains), f32)
        for s in range(27):
            part = slice(s * plane, (s + 1) * plane)
            ahead = prefix[part, 0:grains]
            before[slot, part, :] = ahead
            offset[slot, part, :] = total
            spot = jnp.where(mask[part, :] > 0.0, total + ahead - 1.0, -1.0)
            place[slot, part, :] = spot.astype(jnp.int32)
            total = total + prefix[part, grains : 2 * grains]
        offset[slot, 27 * plane : 28 * plane, :] = total
        for t in range(plane):
            counts[slot, t] = total[t, 0].astype(jnp.int32)
        counts[slot, plane] = jnp.max(total).astype(jnp.int32)

    now = step % 2
    lane = lax.broadcasted_iota(jnp.int32, (plane, grains), 1)
    outer = [s for s in range(27) if s != 13]

    def build(group, beside):
        wanted = (lane + group * grains).astype(f32)
        index = {s: jnp.zeros((plane, grains), jnp.int32) for s in outer}
        bit = grains // 2
        level = 0
        while bit:
            for s in outer:
                part = slice(s * plane, (s + 1) * plane)
                rank = wanted - offset[now, part, :]
                probe = take(before[now, part, :], index[s] + (bit - 1))
                index[s] = jnp.where(probe <= rank, index[s] + bit, index[s])
            for work in beside[level::7]:
                work()
            bit //= 2
            level += 1
        found = [jnp.full((plane, grains), AWAY, f32)] * 3 + [jnp.full((plane, grains), 0.5, f32)]
        for s in outer:
            low = offset[now, s * plane : (s + 1) * plane, :]
            high = offset[now, (s + 1) * plane : (s + 2) * plane, :]
            here = (wanted >= low) & (wanted < high)
            for c in range(4):
                member = others[pl.ds(other_row(step + s // 9, s % 9, c), plane), :]
                found[c] = jnp.where(here, take(member, index[s]), found[c])
        for c in range(4):
            lists[c * plane : (c + 1) * plane, :] = found[c]
        lists[4 * plane : 5 * plane, :] = 1.0 / found[3]

    @pl.when(step == 0)
    def _():
        select = prescan(0)
        for s in range(27):
            select(s)
        scan(0)

    own = [others[pl.ds(other_row(step + 1, 4, c), plane), :] for c in range(5)]
    twice = 2.0 * own[3]
    active_of = flags[plane_of(step), :]
    sums = [jnp.zeros((plane, grains), f32)] * 4
    select = prescan(jnp.minimum(step + 1, bx - 1))

    def bridge(s):
        near_by = [others[pl.ds(other_row(step + s // 9, s % 9, c), plane), :] for c in range(5)]
        lines = pl.ds(s, plane, stride=27)
        partner = partner_ref[lines, :]
        got = [take(member, partner) for member in near_by]
        active = jnp.broadcast_to(active_of[:, s : s + 1], (plane, grains))
        gap = [own[c] - got[c] for c in range(3)]
        square = gap[0] * gap[0] + gap[1] * gap[1] + gap[2] * gap[2]
        inverse = lax.rsqrt(square)
        radius_sum = own[3] + got[3]
        product = twice * got[3]
        vol = volume_ref[lines, :]
        root = product * lax.rsqrt(product * (radius_sum * vol))
        scaled = jnp.maximum(square * inverse - radius_sum, 0.0) * root
        broken = rupture_ref[lines, :].astype(f32)
        intact = active * (1.0 - broken)
        curve = 1.0 + scaled * (1.05 + 2.5 * scaled)
        tension = jnp.where(intact > 0.0, product * inverse / (radius_sum * curve), 0.0)
        force = [tension * member for member in gap]
        released = 0.5 * active * broken * vol
        soaked = ABSORB * intact
        from_own = soaked * own[4]
        from_got = soaked * got[4]
        fresh_ref[lines, :] = intact * vol + (from_own + from_got)
        for c, member in enumerate(force + [released - from_got]):
            high = member.astype(jnp.bfloat16).astype(f32)
            held[pl.ds(s * 8 + c, plane, stride=27 * 8), :] = high
            held[pl.ds(s * 8 + c + 4, plane, stride=27 * 8), :] = member - high
        for c in range(3):
            sums[c] = sums[c] - force[c]
        sums[3] = sums[3] + (released - from_own)
        select(s)

    build(0, [functools.partial(bridge, s) for s in range(27)])
    for c in range(4):
        owned[c] = sums[c]
    most = counts[now, plane]

    def distribute(group):
        rows = [summed[c * plane : (c + 1) * plane, :] for c in range(3)]
        for s in outer:
            spot = place[now, s * plane : (s + 1) * plane, :] - group * grains
            here = (spot >= 0) & (spot < grains)
            index = spot & (grains - 1)
            for c in range(3):
                moved = jnp.where(here, take(rows[c], index), 0.0)
                line = pl.ds(far_row(step + s // 9, s % 9, c), plane)
                far[line, :] = far[line, :] - moved

    def cell_at(tile):
        x, local = tile // plane, tile % plane
        return ((x + 1) * wy + local // bz + 1) * wz + local % bz + 1

    def own_row(tile, c):
        x, local = tile // plane, tile % plane
        return (((x + 1) * 9 + 4) * 6 + c) * plane + local

    def columns_of(tile):
        block = others[pl.ds(own_row(tile, 0), 6, stride=plane), :]
        return jnp.concatenate([block, jnp.zeros((2, grains), f32)], axis=0).T

    def spread_columns(slot, columns, m):
        part = slice(8 * m, 8 * m + 8)
        for n, c in enumerate((0, 1, 2, 3, 5)):
            table[slot, n, part] = jnp.broadcast_to(columns[part, c : c + 1], (8, grains))

    def pushes(mine, theirs, own_tile):
        deltas = [mine[c] - theirs[c] for c in range(3)]
        square = deltas[0] * deltas[0] + deltas[1] * deltas[1] + deltas[2] * deltas[2]
        if own_tile:
            square = jnp.maximum(square, FLOOR)
        inverse = lax.rsqrt(square)
        inter = jnp.maximum(mine[3] + theirs[3] - square * inverse, TINY)
        push = inter * inter * inverse * lax.rsqrt(inter * (mine[4] + theirs[4]))
        return [push * member for member in deltas]

    def contacts(local, slot, own_tile, beside):
        listed = [
            jnp.broadcast_to(lists[pl.ds(c * plane + local, 1), :], (8, grains)) for c in range(5)
        ]
        selves = [
            jnp.broadcast_to(others[pl.ds(own_row(step * plane + local, c), 1), :], (8, grains))
            for c in (0, 1, 2, 3, 5)
        ]
        collected = [jnp.zeros((8, grains), f32)] * 3
        for m in range(grains // 8):
            part = slice(8 * m, 8 * m + 8)
            mine = [table[slot, c, part] for c in range(5)]
            products = pushes(mine, listed, False)
            for c in range(3):
                collected[c] = collected[c] + products[c]
            if own_tile:
                inner = pushes(mine, selves, True)
                products = [a + b for a, b in zip(products, inner)]
            for c in range(3):
                acc[c, part] = products[c]
            beside(m)
        for c in range(3):
            line = jnp.sum(collected[c], axis=0, keepdims=True)
            summed[pl.ds(c * plane + local, 1), :] = line
        ones = jnp.ones((8, 2 * grains), jnp.bfloat16)
        for c in range(3):
            both = jnp.concatenate(split(acc[c]), axis=1)
            value = lax.dot_general(ones, both, across, preferred_element_type=f32)
            line = pl.ds(local, 1)
            owned[c, line, :] = owned[c, line, :] + value[0:1]

    across = (((1,), (1,)), ((), ()))
    lanes = lax.broadcasted_iota(jnp.int32, (grains, grains), 0).astype(f32).astype(jnp.bfloat16)
    one = jnp.ones((grains, grains), jnp.bfloat16)
    zero = jnp.zeros((grains, grains), jnp.bfloat16)
    blank = jnp.zeros((8, grains), jnp.bfloat16)

    def bridges(local, pair):
        cell = cell_at(step * plane + local)
        slots = pair if len(pair) == 2 else (pair[0], pair[0])
        chosen, left = [], []
        for s in slots:
            line = local * 27 + s
            left.append(held[pl.ds(pl.multiple_of(line * 8, 8), 8), :])
            aim = partner_ref[pl.ds(line, 1), :].astype(f32).astype(jnp.bfloat16)
            chosen.append(jnp.where(lanes == jnp.broadcast_to(aim, (grains, grains)), one, zero))
        none = jnp.zeros((8, grains), f32)
        first = jnp.concatenate([left[0], none], axis=0).astype(jnp.bfloat16)
        second = jnp.concatenate([none, left[1]], axis=0).astype(jnp.bfloat16)
        moved = lax.dot_general(
            jnp.concatenate([first, second], axis=1),
            jnp.concatenate(chosen, axis=1),
            across,
            preferred_element_type=f32,
        )
        for n, s in enumerate(pair):
            target = cell + ((s // 9 - 1) * wy + s // 3 % 3 - 1) * wz + s % 3 - 1
            rows = pl.ds(pl.multiple_of(target * 8, 8), 8)
            near[rows, :] = near[rows, :] + moved[8 * n : 8 * n + 8]

    pairs = [tuple(range(27)[n : n + 2]) for n in range(0, 27, 2)]

    @pl.when(step == 0)
    def _():
        columns = columns_of(0)
        for m in range(grains // 8):
            spread_columns(0, columns, m)

    def tile_step(local, carry):
        tile = step * plane + local
        columns = columns_of(jnp.minimum(tile + 1, bx * plane - 1))

        def beside(m):
            spread_columns((tile + 1) % 2, columns, m)
            for pair in pairs[m :: grains // 8]:
                bridges(local, pair)

        contacts(local, tile % 2, True, beside)
        return carry

    lax.fori_loop(0, plane, tile_step, 0)
    distribute(0)

    def more(group, carry):
        build(group, [])
        summed[...] = jnp.zeros_like(summed)

        def again(local, inner):
            @pl.when(counts[now, local] > group * grains)
            def _():
                columns = columns_of(step * plane + local)
                for m in range(grains // 8):
                    spread_columns(2, columns, m)
                contacts(local, 2, False, lambda m: None)

            return inner

        lax.fori_loop(0, plane, again, 0)
        distribute(group)
        return carry

    lax.fori_loop(1, (most + grains - 1) // grains, more, 0)
    scan(1 - now)
    for c in range(4):
        line = pl.ds(far_row(step + 1, 4, c), plane)
        far[line, :] = far[line, :] + owned[c]

    @pl.when(step == pl.num_programs(0) - 1)
    def _():
        def fold(x, carry):
            for j in range(9):
                ey, ez = j // 3, j % 3
                for c in range(4 if j == 4 else 3):
                    for z in range(bz):
                        start = ((x * wy + ey) * wz + z + ez) * 8 + c
                        line = pl.ds(start, by, stride=wz * 8)
                        add = far[pl.ds(((x * 9 + j) * 4 + c) * plane + z, by, stride=bz), :]
                        near[line, :] = near[line, :] + add
            return carry

        lax.fori_loop(0, bx + 2, fold, 0)

        def finish(cell, carry):
            value = near[pl.ds(pl.multiple_of(cell * 8, 8), 8), :]
            totals_ref[pl.ds(cell, 4, stride=cells), :] = value[0:4] + value[4:8]
            return carry

        lax.fori_loop(0, cells, finish, 0)


def shards(positions, grain_radii, film_liquid, pair_live, partner, rupture, volume):
    bx, by, bz, grains = grain_radii.shape
    tiles = bx * by * bz
    slots = 27 * tiles
    cells = (bx + 2) * (by + 2) * (bz + 2)
    extents = (bx, by, bz)
    film = film_liquid.reshape(1, bx, by, bz, 1, grains)
    border = spread(
        positions.reshape(3, bx, by, bz, 1, grains),
        grain_radii.reshape(1, bx, by, bz, 1, grains),
        film,
        extents,
    ).reshape(5 * cells, grains)
    plane = by * bz
    span = 27 * plane
    wide = pl.BlockSpec((span, grains), lambda i: (i, 0))
    f32 = jnp.float32
    totals, fresh = pl.pallas_call(
        functools.partial(kernel, (bx, by, bz, grains)),
        grid_spec=pltpu.PrefetchScalarGridSpec(
            num_scalar_prefetch=0,
            grid=(bx,),
            in_specs=[
                pl.BlockSpec(border.shape, lambda i: (0, 0)),
                pl.BlockSpec((1, slots), lambda i: (0, 0)),
                wide,
                wide,
                wide,
            ],
            out_specs=[pl.BlockSpec((4 * cells, grains), lambda i: (0, 0)), wide],
            scratch_shapes=[
                pltpu.VMEM(((bx + 2) * 9 * 6 * plane, grains), f32),
                pltpu.VMEM((tiles, grains), f32),
                pltpu.VMEM((grains, 2 * grains), jnp.bfloat16),
                pltpu.VMEM((span * 8, grains), f32),
                pltpu.VMEM((span, grains), f32),
                pltpu.VMEM((2, span, grains), f32),
                pltpu.VMEM((2, span + plane, grains), f32),
                pltpu.VMEM((2, span, grains), jnp.int32),
                pltpu.VMEM((5 * plane, grains), f32),
                pltpu.VMEM((3 * plane, grains), f32),
                pltpu.VMEM((4, plane, grains), f32),
                pltpu.VMEM((3, 5, grains, grains), f32),
                pltpu.VMEM((3, grains, grains), f32),
                pltpu.VMEM((cells * 8, grains), f32),
                pltpu.VMEM(((bx + 2) * 9 * 4 * plane, grains), f32),
                pltpu.SMEM((2, plane + 1), jnp.int32),
            ],
        ),
        out_shape=[
            jax.ShapeDtypeStruct((4 * cells, grains), f32),
            jax.ShapeDtypeStruct((slots, grains), f32),
        ],
        name="slots",
    )(
        border,
        pair_live.reshape(1, slots),
        partner.reshape(slots, grains),
        rupture.reshape(slots, grains),
        volume.reshape(slots, grains),
    )
    totals = totals.reshape(4, bx + 2, by + 2, bz + 2, 1, grains)
    forces, film_next = collect(totals, film, extents)
    return (
        forces.reshape(positions.shape),
        film_next.reshape(film_liquid.shape),
        fresh.reshape(volume.shape),
    )


def solution(mesh):
    return jax.shard_map(
        shards,
        mesh=mesh,
        in_specs=(
            P(None, "gx", "gy", "gz", None),
            P("gx", "gy", "gz", None),
            P("gx", "gy", "gz", None),
            P("gx", "gy", "gz", None),
            P("gx", "gy", "gz", None, None),
            P("gx", "gy", "gz", None, None),
            P("gx", "gy", "gz", None, None),
        ),
        out_specs=(
            P(None, "gx", "gy", "gz", None),
            P("gx", "gy", "gz", None),
            P("gx", "gy", "gz", None, None),
        ),
        check_vma=False,
    )
```

```python
import functools

import jax
import jax.numpy as jnp
from jax import lax
from jax.experimental import pallas as pl
from jax.experimental.pallas import tpu as pltpu
from jax.sharding import PartitionSpec as P

ABSORB = 0.02
TINY = 1e-30
RADIUS_MAX = 0.6
SLACK = 4e-3
AWAY = -1e4
FLOOR = 1e-12


def neighbours():
    return [
        (ex, ey, ez)
        for ex in (-1, 0, 1)
        for ey in (-1, 0, 1)
        for ez in (-1, 0, 1)
        if (ex, ey, ez) != (0, 0, 0)
    ]


AXES = ("gx", "gy", "gz")


def present(offset):
    found = None
    for axis, shift in zip(AXES, offset):
        if shift == 0:
            continue
        place = lax.axis_index(axis) + shift
        here = (place >= 0) & (place < lax.axis_size(axis))
        found = here if found is None else found & here
    return found


def device_at(offset):
    return tuple(lax.axis_index(axis) + shift for axis, shift in zip(AXES, offset))


def opposite(offset):
    return tuple(-shift for shift in offset)


def greet(offsets):
    barrier = pltpu.get_barrier_semaphore()
    count = jnp.int32(0)
    for offset in offsets:
        here = present(offset)
        count = count + here.astype(jnp.int32)

        @pl.when(here)
        def _():
            pl.semaphore_signal(
                barrier, inc=1, device_id=device_at(offset), device_id_type=pl.DeviceIdType.MESH
            )

    pl.semaphore_wait(barrier, count)


def cut(offset, extents, low, whole, high):
    pick = []
    for shift, extent in zip(offset, extents):
        if shift < 0:
            pick.append(pl.ds(low(extent), 1))
        elif shift > 0:
            pick.append(pl.ds(high(extent), 1))
        else:
            pick.append(pl.ds(whole, extent))
    return (slice(None),) + tuple(pick)


def rim(offset, extents):
    return cut(offset, extents, lambda n: 0, 1, lambda n: n + 1)


def edge(offset, extents):
    return cut(offset, extents, lambda n: 0, 0, lambda n: n - 1)


def spread_kernel(
    extents, place_ref, radius_ref, film_ref, border_ref, state, blank, local_sem, send_sem, recv_sem
):
    offsets = neighbours()
    loads = [
        pltpu.make_async_copy(place_ref, state.at[pl.ds(0, 3)], local_sem.at[0]),
        pltpu.make_async_copy(radius_ref, state.at[pl.ds(3, 1)], local_sem.at[1]),
        pltpu.make_async_copy(film_ref, state.at[pl.ds(4, 1)], local_sem.at[2]),
    ]
    for load in loads:
        load.start()
    greet(offsets)
    blank[...] = jnp.zeros_like(blank)
    for load in loads:
        load.wait()
    copies, fills = [], []
    for i, offset in enumerate(offsets):
        copy = pltpu.make_async_remote_copy(
            src_ref=state.at[edge(offset, extents)],
            dst_ref=border_ref.at[rim(opposite(offset), extents)],
            send_sem=send_sem.at[i],
            recv_sem=recv_sem.at[i],
            device_id=device_at(offset),
            device_id_type=pl.DeviceIdType.MESH,
        )
        copies.append(copy)
        pl.when(present(offset))(copy.start)
    inner = pltpu.make_async_copy(
        state, border_ref.at[rim((0, 0, 0), extents)], local_sem.at[3]
    )
    inner.start()
    for i, offset in enumerate(offsets):
        fill = pltpu.make_async_copy(
            blank.at[edge(offset, extents)],
            border_ref.at[rim(offset, extents)],
            local_sem.at[4 + i],
        )
        fills.append(fill)
        pl.when(jnp.logical_not(present(offset)))(fill.start)
    inner.wait()
    for offset, copy, fill in zip(offsets, copies, fills):
        pl.when(jnp.logical_not(present(offset)))(fill.wait)
        pl.when(present(offset))(copy.wait_send)
        pl.when(present(opposite(offset)))(copy.wait_recv)


def return_kernel(extents, totals_ref, film_ref, force_ref, next_ref, *scratch):
    offsets = neighbours()
    inbox, (inner, local_sem, send_sem, recv_sem) = scratch[:-4], scratch[-4:]
    load = pltpu.make_async_copy(totals_ref.at[rim((0, 0, 0), extents)], inner, local_sem)
    load.start()
    greet(offsets)
    copies = []
    for i, offset in enumerate(offsets):
        copy = pltpu.make_async_remote_copy(
            src_ref=totals_ref.at[rim(offset, extents)],
            dst_ref=inbox[i],
            send_sem=send_sem.at[i],
            recv_sem=recv_sem.at[i],
            device_id=device_at(offset),
            device_id_type=pl.DeviceIdType.MESH,
        )
        copies.append(copy)
        pl.when(present(offset))(copy.start)
    load.wait()
    force_ref[...] = inner[0:3]
    next_ref[...] = film_ref[...] + inner[3:4]
    order = sorted(range(len(offsets)), key=lambda i: sum(map(abs, offsets[i])))
    for i in order:
        offset, copy = offsets[i], copies[i]

        @pl.when(present(opposite(offset)))
        def _():
            copy.wait_recv()
            region = edge(opposite(offset), extents)
            got = inbox[i][...]
            force_ref[region] = force_ref[region] + got[0:3]
            next_ref[region] = next_ref[region] + got[3:4]

    for offset, copy in zip(offsets, copies):
        pl.when(present(offset))(copy.wait_send)


def spread(place, radius, film, extents):
    sems = pltpu.SemaphoreType.DMA((26,))
    anywhere = pl.BlockSpec(memory_space=pl.ANY)
    tail = place.shape[4:]
    shape = (5,) + tuple(n + 2 for n in extents) + tail
    own = pltpu.VMEM((5,) + tuple(extents) + tail, jnp.float32)
    return pl.pallas_call(
        functools.partial(spread_kernel, extents),
        out_shape=jax.ShapeDtypeStruct(shape, jnp.float32),
        in_specs=[anywhere] * 3,
        out_specs=anywhere,
        scratch_shapes=[own, own, pltpu.SemaphoreType.DMA((30,)), sems, sems],
        compiler_params=pltpu.CompilerParams(collective_id=0, has_side_effects=True),
        name="spread",
    )(place, radius, film)


def collect(totals, film, extents):
    sems = pltpu.SemaphoreType.DMA((26,))
    vmem = pl.BlockSpec(memory_space=pltpu.VMEM)
    tail = totals.shape[4:]
    boxes = [
        pltpu.VMEM(
            (4,) + tuple(1 if e else n for e, n in zip(offset, extents)) + tail, jnp.float32
        )
        for offset in neighbours()
    ]
    return pl.pallas_call(
        functools.partial(return_kernel, extents),
        out_shape=[
            jax.ShapeDtypeStruct((3,) + tuple(extents) + tail, jnp.float32),
            jax.ShapeDtypeStruct((1,) + tuple(extents) + tail, jnp.float32),
        ],
        in_specs=[pl.BlockSpec(memory_space=pl.ANY), vmem],
        out_specs=[vmem, vmem],
        scratch_shapes=boxes
        + [
            pltpu.VMEM((4,) + tuple(extents) + tail, jnp.float32),
            pltpu.SemaphoreType.DMA,
            sems,
            sems,
        ],
        compiler_params=pltpu.CompilerParams(collective_id=1, has_side_effects=True),
        name="collect",
    )(totals, film)


def split(values):
    high = values.astype(jnp.bfloat16)
    low = (values - high.astype(jnp.float32)).astype(jnp.bfloat16)
    return high, low


def take(values, index):
    return jnp.take_along_axis(
        values, index, axis=1, mode="promise_in_bounds", wrap_negative_indices=False
    )


def kernel(
    dims,
    border_ref,
    live_ref,
    live_smem,
    partner_ref,
    rupture_ref,
    volume_ref,
    totals_ref,
    fresh_ref,
    others,
    flags,
    wide,
    triangle,
    held,
    mask,
    before,
    probes,
    offset,
    place,
    lists,
    summed,
    owned,
    table_even,
    table_odd,
    table_more,
    acc,
    near,
    far,
    counts,
    lines_of,
    cells_of,
    amount,
):
    bx, by, bz, grains = dims
    tables = (table_even, table_odd, table_more)
    wy, wz = by + 2, bz + 2
    plane = by * bz
    step = pl.program_id(0)
    cells = (bx + 2) * wy * wz
    f32 = jnp.float32
    faces = [4, 22, 10, 16, 12, 14]
    outer = [s for s in range(27) if s != 13 and s not in faces] + faces

    def other_row(x, j, c):
        return pl.multiple_of(((x * 9 + j) * 6 + c) * plane, plane)

    deep = -(-wy * bz // 8) * 8

    def far_base(x, ez, c):
        return pl.multiple_of(((ez * (bx + 2) + x) * 4 + c) * deep, 8)

    def far_line(x, j, c):
        return pl.ds(far_base(x, j % 3, c) + j // 3 * bz, plane)

    @pl.when(step == 0)
    def _():
        near[...] = jnp.zeros_like(near)
        far[...] = jnp.zeros_like(far)
        held[27 * plane * 8 :, :] = jnp.zeros((8, grains), f32)
        rows = lax.broadcasted_iota(jnp.int32, (grains, grains), 0)
        cols = lax.broadcasted_iota(jnp.int32, (grains, grains), 1)
        half = grains // 2
        for n, last in enumerate((cols, grains, half - 1, half // 2 - 1, half + half // 2 - 1)):
            block = (rows <= last).astype(f32).astype(jnp.bfloat16)
            triangle[:, n * grains : (n + 1) * grains] = block
        flags[...] = jnp.zeros_like(flags)
        for t in range(bx * plane):
            flags[t : t + 1, 0:27] = live_ref[0:1, t * 27 : t * 27 + 27].astype(f32)

        def widen(x, carry):
            row = flags[pl.ds(pl.multiple_of(x * plane, plane), plane), :]
            for s in range(27):
                line = pl.ds(pl.multiple_of((x * 27 + s) * plane, plane), plane)
                wide[line, :] = jnp.broadcast_to(row[:, s : s + 1], (plane, grains))
            return carry

        lax.fori_loop(0, bx, widen, 0)

        def arrange(x, carry):
            for j in range(9):
                ey, ez = j // 3, j % 3
                for c in range(5):
                    for z in range(bz):
                        start = c * cells + (x * wy + ey) * wz + z + ez
                        got = border_ref[pl.ds(start, by, stride=wz), :]
                        others[pl.ds(((x * 9 + j) * 6 + c) * plane + z, by, stride=bz), :] = got
            for j in range(9):
                radius = others[pl.ds(other_row(x, j, 3), plane), :]
                others[pl.ds(other_row(x, j, 5), plane), :] = 1.0 / radius
            return carry

        lax.fori_loop(0, bx + 2, arrange, 0)

    def cell_at(tile):
        x, local = tile // plane, tile % plane
        return ((x + 1) * wy + local // bz + 1) * wz + local % bz + 1

    def plane_of(x):
        return pl.ds(pl.multiple_of(x * plane, plane), plane)

    def lit(x, s):
        return wide[pl.ds(pl.multiple_of((x * 27 + s) * plane, plane), plane), :]

    def prescan(x):
        mine = [others[pl.ds(other_row(x + 1, 4, c), plane), :] for c in range(4)]
        highs = [jnp.max(mine[c], axis=1, keepdims=True) for c in range(3)]
        lows = [jnp.min(mine[c], axis=1, keepdims=True) for c in range(3)]
        widest = jnp.max(mine[3], axis=1, keepdims=True) + SLACK
        def select(s):
            part = slice(s * plane, (s + 1) * plane)
            if s == 13:
                mask[part, :] = jnp.zeros((plane, grains), f32)
                return
            there = [others[pl.ds(other_row(x + s // 9, s % 9, c), plane), :] for c in range(4)]
            away = [
                jnp.maximum(jnp.maximum(lows[c] - there[c], there[c] - highs[c]), 0.0)
                for c in range(3)
            ]
            reach = widest + there[3]
            inside = away[0] * away[0] + away[1] * away[1] + away[2] * away[2] < reach * reach
            mask[part, :] = jnp.where(inside, lit(x, s), 0.0)

        return select

    def scan(slot):
        prefix = lax.dot_general(
            mask[...].astype(jnp.bfloat16),
            triangle[...],
            (((1,), (0,)), ((), ())),
            preferred_element_type=f32,
        )
        total = jnp.zeros((plane, grains), f32)
        for i, s in enumerate(outer):
            part = slice(s * plane, (s + 1) * plane)
            ahead = prefix[part, 0:grains]
            before[slot, part, :] = ahead
            for n in range(3):
                probes[slot, n, part, :] = prefix[part, (n + 2) * grains : (n + 3) * grains]
            offset[slot, i * plane : (i + 1) * plane, :] = total
            spot = jnp.where(mask[part, :] > 0.0, total + ahead - 1.0, -1.0)
            place[slot, part, :] = spot.astype(jnp.int32)
            if i == len(outer) - 4:
                counts[slot, plane + 1] = jnp.max(total).astype(jnp.int32)
            total = total + prefix[part, grains : 2 * grains]
        offset[slot, 26 * plane : 27 * plane, :] = total
        for t in range(plane):
            counts[slot, t] = total[t, 0].astype(jnp.int32)
        counts[slot, plane] = jnp.max(total).astype(jnp.int32)

    now = step % 2
    lane = lax.broadcasted_iota(jnp.int32, (plane, grains), 1)

    def build(group, beside, first):
        wanted = (lane + group * grains).astype(f32)
        half = grains // 2
        index = {}
        bit = half // 2
        level = 0
        while bit:
            for i, s in list(enumerate(outer))[first:]:
                part = slice(s * plane, (s + 1) * plane)
                rank = wanted - offset[now, i * plane : (i + 1) * plane, :]
                if bit == half // 2:
                    upper = probes[now, 0, part, :] <= rank
                    probe = jnp.where(upper, probes[now, 2, part, :], probes[now, 1, part, :])
                    index[s] = jnp.where(upper, half, 0)
                else:
                    probe = take(before[now, part, :], index[s] + (bit - 1))
                index[s] = jnp.where(probe <= rank, index[s] + bit, index[s])
            for work in beside[level::6]:
                work()
            bit //= 2
            level += 1
        found = [jnp.full((plane, grains), AWAY, f32)] * 3 + [jnp.full((plane, grains), 0.5, f32)]
        for i, s in list(enumerate(outer))[first:]:
            low = offset[now, i * plane : (i + 1) * plane, :]
            high = offset[now, (i + 1) * plane : (i + 2) * plane, :]
            here = (wanted >= low) & (wanted < high)
            for c in range(4):
                member = others[pl.ds(other_row(step + s // 9, s % 9, c), plane), :]
                found[c] = jnp.where(here, take(member, index[s]), found[c])
        for c in range(4):
            lists[c * plane : (c + 1) * plane, :] = found[c]
        lists[4 * plane : 5 * plane, :] = 1.0 / found[3]

    @pl.when(step == 0)
    def _():
        select = prescan(0)
        for s in range(27):
            select(s)
        scan(0)

    own = [others[pl.ds(other_row(step + 1, 4, c), plane), :] for c in range(5)]
    twice = 2.0 * own[3]
    sums = [jnp.zeros((plane, grains), f32)] * 4
    select = prescan(jnp.minimum(step + 1, bx - 1))

    def bridge(s):
        near_by = [others[pl.ds(other_row(step + s // 9, s % 9, c), plane), :] for c in range(5)]
        lines = pl.ds(s, plane, stride=27)
        partner = partner_ref[lines, :]
        got = [take(member, partner) for member in near_by]
        active = lit(step, s)
        gap = [own[c] - got[c] for c in range(3)]
        square = gap[0] * gap[0] + gap[1] * gap[1] + gap[2] * gap[2]
        inverse = lax.rsqrt(square)
        radius_sum = own[3] + got[3]
        product = twice * got[3]
        vol = volume_ref[lines, :]
        root = product * lax.rsqrt(product * (radius_sum * vol))
        scaled = jnp.maximum(square * inverse - radius_sum, 0.0) * root
        broken = rupture_ref[lines, :].astype(f32)
        intact = active * (1.0 - broken)
        curve = 1.0 + scaled * (1.05 + 2.5 * scaled)
        tension = jnp.where(intact > 0.0, product * inverse / (radius_sum * curve), 0.0)
        force = [tension * member for member in gap]
        released = 0.5 * active * broken * vol
        soaked = ABSORB * intact
        from_own = soaked * own[4]
        from_got = soaked * got[4]
        fresh_ref[lines, :] = intact * vol + (from_own + from_got)
        for c, member in enumerate(force + [released - from_got]):
            high = member.astype(jnp.bfloat16).astype(f32)
            held[pl.ds(s * 8 + c, plane, stride=27 * 8), :] = high
            held[pl.ds(s * 8 + c + 4, plane, stride=27 * 8), :] = member - high
        for c in range(3):
            sums[c] = sums[c] - force[c]
        sums[3] = sums[3] + (released - from_own)
        select(s)

    def enlist(t):
        cell = cell_at(step * plane + t)
        count = jnp.int32(0)
        for s in range(27):
            lines_of[t * 32 + count] = t * 27 + s
            cells_of[t * 32 + count] = cell + ((s // 9 - 1) * wy + s // 3 % 3 - 1) * wz + s % 3 - 1
            count = count + live_smem[0, (step * plane + t) * 27 + s]
        amount[t] = count

    beside = []
    for s in range(27):
        beside.append(functools.partial(bridge, s))
        if s % 3 == 0 and s // 3 < plane:
            beside.append(functools.partial(enlist, s // 3))
    build(0, beside, 0)
    for c in range(4):
        owned[c] = sums[c]
    most = counts[now, plane]

    def distribute(group, first):
        rows = [summed[c * plane : (c + 1) * plane, :] for c in range(3)]
        for s in outer[first:]:
            spot = place[now, s * plane : (s + 1) * plane, :] - group * grains
            here = (spot >= 0) & (spot < grains)
            index = spot & (grains - 1)
            for c in range(3):
                moved = jnp.where(here, take(rows[c], index), 0.0)
                line = far_line(step + s // 9, s % 9, c)
                far[line, :] = far[line, :] - moved

    def own_row(tile, c):
        x, local = tile // plane, tile % plane
        return (((x + 1) * 9 + 4) * 6 + c) * plane + local

    def columns_of(tile):
        block = others[pl.ds(own_row(tile, 0), 6, stride=plane), :]
        return jnp.concatenate([block, jnp.zeros((2, grains), f32)], axis=0).T

    def spread_columns(table, columns, m):
        for at in range(5 * m, 5 * m + 5):
            n, block = at // (grains // 8), at % (grains // 8)
            c = (0, 1, 2, 3, 5)[n]
            part = slice(8 * block, 8 * block + 8)
            table[n, part] = jnp.broadcast_to(columns[part, c : c + 1], (8, grains))

    def pushes(mine, theirs, own_tile):
        deltas = [mine[c] - theirs[c] for c in range(3)]
        square = deltas[0] * deltas[0] + deltas[1] * deltas[1] + deltas[2] * deltas[2]
        if own_tile:
            square = jnp.maximum(square, FLOOR)
        inverse = lax.rsqrt(square)
        inter = jnp.maximum(mine[3] + theirs[3] - square * inverse, TINY)
        push = inter * inter * inverse * lax.rsqrt(inter * (mine[4] + theirs[4]))
        return [push * member for member in deltas]

    def contacts(local, table, own_tile, beside):
        listed = [
            jnp.broadcast_to(lists[pl.ds(c * plane + local, 1), :], (8, grains)) for c in range(5)
        ]
        selves = [
            jnp.broadcast_to(others[pl.ds(own_row(step * plane + local, c), 1), :], (8, grains))
            for c in (0, 1, 2, 3, 5)
        ]
        collected = [jnp.zeros((8, grains), f32)] * 3
        for m in range(grains // 8):
            part = slice(8 * m, 8 * m + 8)
            mine = [table[c, part] for c in range(5)]
            products = pushes(mine, listed, False)
            for c in range(3):
                collected[c] = collected[c] + products[c]
            if own_tile:
                inner = pushes(mine, selves, True)
                products = [a + b for a, b in zip(products, inner)]
            for c in range(3):
                acc[c, part] = products[c]
            beside(m)
        for c in range(3):
            line = jnp.sum(collected[c], axis=0, keepdims=True)
            summed[pl.ds(c * plane + local, 1), :] = line
        ones = jnp.ones((8, 2 * grains), jnp.bfloat16)
        for c in range(3):
            both = jnp.concatenate(split(acc[c]), axis=1)
            value = lax.dot_general(ones, both, across, preferred_element_type=f32)
            line = pl.ds(local, 1)
            owned[c, line, :] = owned[c, line, :] + value[0:1]

    across = (((1,), (1,)), ((), ()))
    lanes = lax.broadcasted_iota(jnp.int32, (grains, grains), 0).astype(f32).astype(jnp.bfloat16)
    one = jnp.ones((grains, grains), jnp.bfloat16)
    zero = jnp.zeros((grains, grains), jnp.bfloat16)
    blank = jnp.zeros((8, grains), jnp.bfloat16)

    def bridges(local, pair):
        chosen, left, targets = [], [], []
        for k in (2 * pair, 2 * pair + 1):
            listed = k < amount[local]
            line = jnp.where(listed, lines_of[local * 32 + k], 27 * plane)
            targets.append(jnp.where(listed, cells_of[local * 32 + k], cells))
            left.append(held[pl.ds(pl.multiple_of(line * 8, 8), 8), :])
            aim = partner_ref[pl.ds(jnp.minimum(line, 27 * plane - 1), 1), :]
            aim = jnp.broadcast_to(aim.astype(f32).astype(jnp.bfloat16), (grains, grains))
            chosen.append(jnp.where(lanes == aim, one, zero))
        none = jnp.zeros((8, grains), f32)
        first = jnp.concatenate([left[0], none], axis=0).astype(jnp.bfloat16)
        second = jnp.concatenate([none, left[1]], axis=0).astype(jnp.bfloat16)
        moved = lax.dot_general(
            jnp.concatenate([first, second], axis=1),
            jnp.concatenate(chosen, axis=1),
            across,
            preferred_element_type=f32,
        )
        for n, target in enumerate(targets):
            rows = pl.ds(pl.multiple_of(target * 8, 8), 8)
            near[rows, :] = near[rows, :] + moved[8 * n : 8 * n + 8]

    @pl.when(step == 0)
    def _():
        columns = columns_of(0)
        for m in range(grains // 8):
            spread_columns(tables[0], columns, m)

    def tile_step(couple, carry):
        for half in range(2):
            local = 2 * couple + half
            tile = step * plane + local
            columns = columns_of(jnp.minimum(tile + 1, bx * plane - 1))

            def beside(m):
                spread_columns(tables[1 - half], columns, m)
                if m % 2 == 0:
                    bridges(local, m // 2)

            contacts(local, tables[half], True, beside)

        for half in range(2):
            local = 2 * couple + half

            def spare(pair, inner):
                bridges(local, pair)
                return inner

            lax.fori_loop(grains // 16, (amount[local] + 1) // 2, spare, 0)
        return carry

    lax.fori_loop(0, plane // 2, tile_step, 0)
    distribute(0, 0)

    def more(group, carry):
        early = counts[now, plane + 1] > group * grains

        @pl.when(early)
        def _():
            build(group, [], 0)

        @pl.when(jnp.logical_not(early))
        def _():
            build(group, [], 22)

        summed[...] = jnp.zeros_like(summed)

        def again(local, inner):
            @pl.when(counts[now, local] > group * grains)
            def _():
                columns = columns_of(step * plane + local)
                for m in range(grains // 8):
                    spread_columns(tables[2], columns, m)
                contacts(local, tables[2], False, lambda m: None)

            return inner

        lax.fori_loop(0, plane, again, 0)

        @pl.when(early)
        def _():
            distribute(group, 0)

        @pl.when(jnp.logical_not(early))
        def _():
            distribute(group, 22)

        return carry

    lax.fori_loop(1, (most + grains - 1) // grains, more, 0)
    scan(1 - now)
    for c in range(4):
        line = far_line(step + 1, 4, c)
        far[line, :] = far[line, :] + owned[c]

    @pl.when(step == pl.num_programs(0) - 1)
    def _():
        def fold(x, carry):
            sheet = wy * wz
            for c in range(4):
                base = pl.multiple_of(x * (sheet * 8), 8)
                value = near[pl.ds(base + c, sheet, stride=8), :]
                value = value + near[pl.ds(base + c + 4, sheet, stride=8), :]
                totals_ref[pl.ds(c * cells + x * sheet, sheet), :] = value
                for ez in range(3) if c < 3 else (1,):
                    for z in range(bz):
                        line = pl.ds(c * cells + x * sheet + z + ez, wy, stride=wz)
                        add = far[pl.ds(far_base(x, ez, c) + z, wy, stride=bz), :]
                        totals_ref[line, :] = totals_ref[line, :] + add
            return carry

        lax.fori_loop(0, bx + 2, fold, 0)


def shards(positions, grain_radii, film_liquid, pair_live, partner, rupture, volume):
    bx, by, bz, grains = grain_radii.shape
    tiles = bx * by * bz
    slots = 27 * tiles
    cells = (bx + 2) * (by + 2) * (bz + 2)
    extents = (bx, by, bz)
    film = film_liquid.reshape(1, bx, by, bz, 1, grains)
    border = spread(
        positions.reshape(3, bx, by, bz, 1, grains),
        grain_radii.reshape(1, bx, by, bz, 1, grains),
        film,
        extents,
    ).reshape(5 * cells, grains)
    plane = by * bz
    span = 27 * plane
    wide = pl.BlockSpec((span, grains), lambda i: (i, 0))
    f32 = jnp.float32
    totals, fresh = pl.pallas_call(
        functools.partial(kernel, (bx, by, bz, grains)),
        grid_spec=pltpu.PrefetchScalarGridSpec(
            num_scalar_prefetch=0,
            grid=(bx,),
            in_specs=[
                pl.BlockSpec(border.shape, lambda i: (0, 0)),
                pl.BlockSpec((1, slots), lambda i: (0, 0)),
                pl.BlockSpec((1, slots), lambda i: (0, 0), memory_space=pltpu.SMEM),
                wide,
                wide,
                wide,
            ],
            out_specs=[pl.BlockSpec((4 * cells, grains), lambda i: (0, 0)), wide],
            scratch_shapes=[
                pltpu.VMEM(((bx + 2) * 9 * 6 * plane, grains), f32),
                pltpu.VMEM((tiles, grains), f32),
                pltpu.VMEM((slots, grains), f32),
                pltpu.VMEM((grains, 5 * grains), jnp.bfloat16),
                pltpu.VMEM((span * 8 + 8, grains), f32),
                pltpu.VMEM((span, grains), f32),
                pltpu.VMEM((2, span, grains), f32),
                pltpu.VMEM((2, 3, span, grains), f32),
                pltpu.VMEM((2, span + plane, grains), f32),
                pltpu.VMEM((2, span, grains), jnp.int32),
                pltpu.VMEM((5 * plane, grains), f32),
                pltpu.VMEM((3 * plane, grains), f32),
                pltpu.VMEM((4, plane, grains), f32),
                pltpu.VMEM((5, grains, grains), f32),
                pltpu.VMEM((5, grains, grains), f32),
                pltpu.VMEM((5, grains, grains), f32),
                pltpu.VMEM((3, grains, grains), f32),
                pltpu.VMEM((cells * 8 + 8, grains), f32),
                pltpu.VMEM((3 * (bx + 2) * 4 * (-(-(by + 2) * bz // 8) * 8), grains), f32),
                pltpu.SMEM((2, plane + 2), jnp.int32),
                pltpu.SMEM((plane * 32,), jnp.int32),
                pltpu.SMEM((plane * 32,), jnp.int32),
                pltpu.SMEM((plane,), jnp.int32),
            ],
        ),
        out_shape=[
            jax.ShapeDtypeStruct((4 * cells, grains), f32),
            jax.ShapeDtypeStruct((slots, grains), f32),
        ],
        name="slots",
    )(
        border,
        pair_live.reshape(1, slots),
        pair_live.reshape(1, slots),
        partner.reshape(slots, grains),
        rupture.reshape(slots, grains),
        volume.reshape(slots, grains),
    )
    totals = totals.reshape(4, bx + 2, by + 2, bz + 2, 1, grains)
    forces, film_next = collect(totals, film, extents)
    return (
        forces.reshape(positions.shape),
        film_next.reshape(film_liquid.shape),
        fresh.reshape(volume.shape),
    )


def solution(mesh):
    return jax.shard_map(
        shards,
        mesh=mesh,
        in_specs=(
            P(None, "gx", "gy", "gz", None),
            P("gx", "gy", "gz", None),
            P("gx", "gy", "gz", None),
            P("gx", "gy", "gz", None),
            P("gx", "gy", "gz", None, None),
            P("gx", "gy", "gz", None, None),
            P("gx", "gy", "gz", None, None),
        ),
        out_specs=(
            P(None, "gx", "gy", "gz", None),
            P("gx", "gy", "gz", None),
            P("gx", "gy", "gz", None, None),
        ),
        check_vma=False,
    )
```

```python
import functools

import jax
import jax.numpy as jnp
from jax import lax
from jax.experimental import pallas as pl
from jax.experimental.pallas import tpu as pltpu
from jax.sharding import PartitionSpec as P

ABSORB = 0.02
TINY = 1e-30
RADIUS_MAX = 0.6
SLACK = 4e-3
AWAY = -1e4
FLOOR = 1e-12


def neighbours():
    found = [
        (ex, ey, ez)
        for ex in (-1, 0, 1)
        for ey in (-1, 0, 1)
        for ez in (-1, 0, 1)
        if (ex, ey, ez) != (0, 0, 0)
    ]
    return sorted(found, key=lambda offset: -sum(map(abs, offset)))


AXES = ("gx", "gy", "gz")


def present(offset):
    found = None
    for axis, shift in zip(AXES, offset):
        if shift == 0:
            continue
        place = lax.axis_index(axis) + shift
        here = (place >= 0) & (place < lax.axis_size(axis))
        found = here if found is None else found & here
    return found


def device_at(offset):
    return tuple(lax.axis_index(axis) + shift for axis, shift in zip(AXES, offset))


def opposite(offset):
    return tuple(-shift for shift in offset)


def greet(offsets):
    barrier = pltpu.get_barrier_semaphore()
    count = jnp.int32(0)
    for offset in offsets:
        here = present(offset)
        count = count + here.astype(jnp.int32)

        @pl.when(here)
        def _():
            pl.semaphore_signal(
                barrier, inc=1, device_id=device_at(offset), device_id_type=pl.DeviceIdType.MESH
            )

    pl.semaphore_wait(barrier, count)


def cut(offset, extents, low, whole, high):
    pick = []
    for shift, extent in zip(offset, extents):
        if shift < 0:
            pick.append(pl.ds(low(extent), 1))
        elif shift > 0:
            pick.append(pl.ds(high(extent), 1))
        else:
            pick.append(pl.ds(whole, extent))
    return (slice(None),) + tuple(pick)


def rim(offset, extents):
    return cut(offset, extents, lambda n: 0, 1, lambda n: n + 1)


def edge(offset, extents):
    return cut(offset, extents, lambda n: 0, 0, lambda n: n - 1)


def spread_kernel(
    extents, place_ref, radius_ref, film_ref, border_ref, state, blank, local_sem, send_sem, recv_sem
):
    offsets = neighbours()
    loads = [
        pltpu.make_async_copy(place_ref, state.at[pl.ds(0, 3)], local_sem.at[0]),
        pltpu.make_async_copy(radius_ref, state.at[pl.ds(3, 1)], local_sem.at[1]),
        pltpu.make_async_copy(film_ref, state.at[pl.ds(4, 1)], local_sem.at[2]),
    ]
    for load in loads:
        load.start()
    greet(offsets)
    blank[...] = jnp.zeros_like(blank)
    for load in loads:
        load.wait()
    copies, fills = [], []
    for i, offset in enumerate(offsets):
        copy = pltpu.make_async_remote_copy(
            src_ref=state.at[edge(offset, extents)],
            dst_ref=border_ref.at[rim(opposite(offset), extents)],
            send_sem=send_sem.at[i],
            recv_sem=recv_sem.at[i],
            device_id=device_at(offset),
            device_id_type=pl.DeviceIdType.MESH,
        )
        copies.append(copy)
        pl.when(present(offset))(copy.start)
    inner = pltpu.make_async_copy(
        state, border_ref.at[rim((0, 0, 0), extents)], local_sem.at[3]
    )
    inner.start()
    for i, offset in enumerate(offsets):
        fill = pltpu.make_async_copy(
            blank.at[edge(offset, extents)],
            border_ref.at[rim(offset, extents)],
            local_sem.at[4 + i],
        )
        fills.append(fill)
        pl.when(jnp.logical_not(present(offset)))(fill.start)
    inner.wait()
    for offset, copy, fill in reversed(list(zip(offsets, copies, fills))):
        pl.when(jnp.logical_not(present(offset)))(fill.wait)
        pl.when(present(offset))(copy.wait_send)
        pl.when(present(opposite(offset)))(copy.wait_recv)


def return_kernel(extents, totals_ref, sum_ref, *scratch):
    offsets = neighbours()
    inbox, (inner, local_sem, send_sem, recv_sem) = scratch[:-4], scratch[-4:]
    load = pltpu.make_async_copy(totals_ref.at[rim((0, 0, 0), extents)], inner, local_sem)
    load.start()
    greet(offsets)
    copies = []
    for i, offset in enumerate(offsets):
        copy = pltpu.make_async_remote_copy(
            src_ref=totals_ref.at[rim(offset, extents)],
            dst_ref=inbox[i],
            send_sem=send_sem.at[i],
            recv_sem=recv_sem.at[i],
            device_id=device_at(offset),
            device_id_type=pl.DeviceIdType.MESH,
        )
        copies.append(copy)
        pl.when(present(offset))(copy.start)
    load.wait()
    sum_ref[...] = inner[...]
    order = sorted(range(len(offsets)), key=lambda i: sum(map(abs, offsets[i])))
    for i in order:
        offset, copy = offsets[i], copies[i]

        @pl.when(present(opposite(offset)))
        def _():
            copy.wait_recv()
            region = edge(opposite(offset), extents)
            sum_ref[region] = sum_ref[region] + inbox[i][...]

    for offset, copy in zip(offsets, copies):
        pl.when(present(offset))(copy.wait_send)


def finish_kernel(sum_ref, film_ref, force_ref, next_ref):
    count = force_ref.shape[0]
    force_ref[...] = sum_ref[0:count, :]
    next_ref[...] = film_ref[...] + sum_ref[count:, :]


def spread(place, radius, film, extents):
    sems = pltpu.SemaphoreType.DMA((26,))
    anywhere = pl.BlockSpec(memory_space=pl.ANY)
    tail = place.shape[4:]
    shape = (5,) + tuple(n + 2 for n in extents) + tail
    own = pltpu.VMEM((5,) + tuple(extents) + tail, jnp.float32)
    return pl.pallas_call(
        functools.partial(spread_kernel, extents),
        out_shape=jax.ShapeDtypeStruct(shape, jnp.float32),
        in_specs=[anywhere] * 3,
        out_specs=anywhere,
        scratch_shapes=[own, own, pltpu.SemaphoreType.DMA((30,)), sems, sems],
        compiler_params=pltpu.CompilerParams(collective_id=0, has_side_effects=True),
        name="spread",
    )(place, radius, film)


def collect(totals, extents):
    sems = pltpu.SemaphoreType.DMA((26,))
    vmem = pl.BlockSpec(memory_space=pltpu.VMEM)
    tail = totals.shape[4:]
    boxes = [
        pltpu.VMEM(
            (4,) + tuple(1 if e else n for e, n in zip(offset, extents)) + tail, jnp.float32
        )
        for offset in neighbours()
    ]
    return pl.pallas_call(
        functools.partial(return_kernel, extents),
        out_shape=jax.ShapeDtypeStruct((4,) + tuple(extents) + tail, jnp.float32),
        in_specs=[pl.BlockSpec(memory_space=pl.ANY)],
        out_specs=vmem,
        scratch_shapes=boxes
        + [
            pltpu.VMEM((4,) + tuple(extents) + tail, jnp.float32),
            pltpu.SemaphoreType.DMA,
            sems,
            sems,
        ],
        compiler_params=pltpu.CompilerParams(collective_id=1, has_side_effects=True),
        name="collect",
    )(totals)


def split(values):
    high = values.astype(jnp.bfloat16)
    low = (values - high.astype(jnp.float32)).astype(jnp.bfloat16)
    return high, low


def take(values, index):
    return jnp.take_along_axis(
        values, index, axis=1, mode="promise_in_bounds", wrap_negative_indices=False
    )


def kernel(
    dims,
    border_hbm,
    live_ref,
    partner_ref,
    rupture_ref,
    volume_ref,
    totals_ref,
    fresh_ref,
    others,
    flags,
    wide,
    triangle,
    held,
    mask,
    before,
    probes,
    offset,
    place,
    lists,
    summed,
    owned,
    table_even,
    table_odd,
    table_more,
    acc,
    near,
    far,
    counts,
    todo,
    agenda,
    agenda_sem,
    border_ref,
    border_sem,
):
    bx, by, bz, grains = dims
    tables = (table_even, table_odd)
    wy, wz = by + 2, bz + 2
    plane = by * bz
    step = pl.program_id(0)
    cells = (bx + 2) * wy * wz
    f32 = jnp.float32
    faces = [4, 22, 10, 16, 12, 14]
    outer = [s for s in range(27) if s != 13 and s not in faces] + faces

    def other_row(x, j, c):
        return pl.multiple_of(((x * 9 + j) * 6 + c) * plane, plane)

    deep = -(-wy * bz // 8) * 8

    def far_base(x, ez, c):
        return pl.multiple_of(((ez * (bx + 2) + x) * 4 + c) * deep, 8)

    def far_line(x, j, c):
        return pl.ds(far_base(x, j % 3, c) + j // 3 * bz, plane)

    def enlist():
        shape = (bx * plane, grains)
        dims_p = (((1,), (0,)), ((), ()))
        listed = flags[...].astype(jnp.bfloat16)
        ahead = lax.dot_general(
            listed, triangle[:, 0 : 2 * grains], dims_p, preferred_element_type=f32
        )
        amount = ahead[:, grains : 2 * grains].astype(jnp.int32)
        ahead = ahead[:, 0:grains].astype(jnp.int32)
        at = lax.broadcasted_iota(jnp.int32, shape, 1)
        rank = at & 31
        slot = jnp.zeros(shape, jnp.int32)
        for bit in (16, 8, 4, 2, 1):
            slot = jnp.where(take(ahead, slot + (bit - 1)) <= rank, slot + bit, slot)
        valid = rank < amount

        def parts(value, size, number):
            high = sum((value >= size * n).astype(jnp.int32) for n in range(1, number))
            return high, value - size * high

        ix, local = parts(lax.broadcasted_iota(jnp.int32, shape, 0), plane, bx)
        iy, iz = parts(local, bz, by)
        ex, rest = parts(slot, 9, 3)
        ey, ez = parts(rest, 3, 3)
        cell = ((ix + ex) * wy + iy + ey) * wz + iz + ez
        line = local * 27 + slot
        first = jnp.where(valid, line, 0)
        second = jnp.where(valid, line * 8, 27 * plane * 8)
        third = jnp.where(valid, cell * 8, cells * 8)
        low = jnp.where(at < 32, first, second)
        high = jnp.where(at < 96, third, amount)
        todo[...] = jnp.where(at < 64, low, high)
        pltpu.make_async_copy(todo, agenda, agenda_sem).start()

    @pl.when(step == 0)
    def _():
        fetch = pltpu.make_async_copy(border_hbm, border_ref, border_sem)
        fetch.start()
        near[...] = jnp.zeros_like(near)
        far[...] = jnp.zeros_like(far)
        summed[...] = jnp.zeros_like(summed)
        held[27 * plane * 8 :, :] = jnp.zeros((8, grains), f32)
        rows = lax.broadcasted_iota(jnp.int32, (grains, grains), 0)
        cols = lax.broadcasted_iota(jnp.int32, (grains, grains), 1)
        half = grains // 2
        for n, last in enumerate((cols, grains, half - 1, half // 2 - 1, half + half // 2 - 1)):
            block = (rows <= last).astype(f32).astype(jnp.bfloat16)
            triangle[:, n * grains : (n + 1) * grains] = block
        flags[...] = jnp.zeros_like(flags)
        for t in range(bx * plane):
            flags[t : t + 1, 0:27] = live_ref[0:1, t * 27 : t * 27 + 27].astype(f32)

        def widen(x, carry):
            row = flags[pl.ds(pl.multiple_of(x * plane, plane), plane), :]
            for s in range(27):
                line = pl.ds(pl.multiple_of((x * 27 + s) * plane, plane), plane)
                wide[line, :] = jnp.broadcast_to(row[:, s : s + 1], (plane, grains))
            return carry

        lax.fori_loop(0, bx, widen, 0)

        def arrange(x, carry):
            for j in range(9):
                ey, ez = j // 3, j % 3
                for c in range(5):
                    for z in range(bz):
                        start = c * cells + (x * wy + ey) * wz + z + ez
                        got = border_ref[pl.ds(start, by, stride=wz), :]
                        others[pl.ds(((x * 9 + j) * 6 + c) * plane + z, by, stride=bz), :] = got
            for j in range(9):
                radius = others[pl.ds(other_row(x, j, 3), plane), :]
                others[pl.ds(other_row(x, j, 5), plane), :] = 1.0 / radius
            return carry

        enlist()
        fetch.wait()
        lax.fori_loop(0, bx + 2, arrange, 0)

    def cell_at(tile):
        x, local = tile // plane, tile % plane
        return ((x + 1) * wy + local // bz + 1) * wz + local % bz + 1

    def plane_of(x):
        return pl.ds(pl.multiple_of(x * plane, plane), plane)

    def lit(x, s):
        return wide[pl.ds(pl.multiple_of((x * 27 + s) * plane, plane), plane), :]

    def prescan(x):
        mine = [others[pl.ds(other_row(x + 1, 4, c), plane), :] for c in range(4)]
        highs = [jnp.max(mine[c], axis=1, keepdims=True) for c in range(3)]
        lows = [jnp.min(mine[c], axis=1, keepdims=True) for c in range(3)]
        widest = jnp.max(mine[3], axis=1, keepdims=True) + SLACK
        def select(s):
            part = slice(s * plane, (s + 1) * plane)
            if s == 13:
                mask[part, :] = jnp.zeros((plane, grains), f32)
                return
            there = [others[pl.ds(other_row(x + s // 9, s % 9, c), plane), :] for c in range(4)]
            away = [
                jnp.maximum(jnp.maximum(lows[c] - there[c], there[c] - highs[c]), 0.0)
                for c in range(3)
            ]
            reach = widest + there[3]
            inside = away[0] * away[0] + away[1] * away[1] + away[2] * away[2] < reach * reach
            mask[part, :] = jnp.where(inside, lit(x, s), 0.0)

        return select

    def scan(slot):
        prefix = lax.dot_general(
            mask[...].astype(jnp.bfloat16),
            triangle[...],
            (((1,), (0,)), ((), ())),
            preferred_element_type=f32,
        )
        total = jnp.zeros((plane, grains), f32)
        for i, s in enumerate(outer):
            part = slice(s * plane, (s + 1) * plane)
            ahead = prefix[part, 0:grains]
            before[slot, part, :] = ahead
            for n in range(3):
                probes[slot, n, part, :] = prefix[part, (n + 2) * grains : (n + 3) * grains]
            offset[slot, i * plane : (i + 1) * plane, :] = total
            spot = jnp.where(mask[part, :] > 0.0, total + ahead - 1.0, -1.0)
            place[slot, part, :] = spot.astype(jnp.int32)
            if i == len(outer) - 4:
                counts[slot, plane + 1] = jnp.max(total).astype(jnp.int32)
            total = total + prefix[part, grains : 2 * grains]
        offset[slot, 26 * plane : 27 * plane, :] = total
        for t in range(plane):
            counts[slot, t] = total[t, 0].astype(jnp.int32)
        counts[slot, plane] = jnp.max(total).astype(jnp.int32)

    now = step % 2
    lane = lax.broadcasted_iota(jnp.int32, (plane, grains), 1)

    def build(group, beside, first, into, after=()):
        wanted = (lane + group * grains).astype(f32)
        half = grains // 2
        index = {}
        bit = half // 2
        level = 0
        while bit:
            for i, s in list(enumerate(outer))[first:]:
                part = slice(s * plane, (s + 1) * plane)
                rank = wanted - offset[now, i * plane : (i + 1) * plane, :]
                if bit == half // 2:
                    upper = probes[now, 0, part, :] <= rank
                    probe = jnp.where(upper, probes[now, 2, part, :], probes[now, 1, part, :])
                    index[s] = jnp.where(upper, half, 0)
                else:
                    probe = take(before[now, part, :], index[s] + (bit - 1))
                index[s] = jnp.where(probe <= rank, index[s] + bit, index[s])
            for work in beside[level::6]:
                work()
            bit //= 2
            level += 1
        for work in after:
            work()
        found = [jnp.full((plane, grains), AWAY, f32)] * 3 + [jnp.full((plane, grains), 0.5, f32)]
        for i, s in list(enumerate(outer))[first:]:
            low = offset[now, i * plane : (i + 1) * plane, :]
            high = offset[now, (i + 1) * plane : (i + 2) * plane, :]
            here = (wanted >= low) & (wanted < high)
            for c in range(4):
                member = others[pl.ds(other_row(step + s // 9, s % 9, c), plane), :]
                found[c] = jnp.where(here, take(member, index[s]), found[c])
        for c, member in enumerate(found + [1.0 / found[3]]):
            lists[into, c * plane : (c + 1) * plane, :] = member

    @pl.when(step == 0)
    def _():
        select = prescan(0)
        for s in range(27):
            select(s)
        scan(0)

    own = [others[pl.ds(other_row(step + 1, 4, c), plane), :] for c in range(5)]
    twice = 2.0 * own[3]
    sums = [jnp.zeros((plane, grains), f32)] * 4
    select = prescan(jnp.minimum(step + 1, bx - 1))

    def bridge(s):
        near_by = [others[pl.ds(other_row(step + s // 9, s % 9, c), plane), :] for c in range(5)]
        lines = pl.ds(s, plane, stride=27)
        partner = partner_ref[lines, :]
        got = [take(member, partner) for member in near_by]
        active = lit(step, s)
        gap = [own[c] - got[c] for c in range(3)]
        square = gap[0] * gap[0] + gap[1] * gap[1] + gap[2] * gap[2]
        inverse = lax.rsqrt(square)
        radius_sum = own[3] + got[3]
        product = twice * got[3]
        vol = volume_ref[lines, :]
        root = product * lax.rsqrt(product * (radius_sum * vol))
        scaled = jnp.maximum(square * inverse - radius_sum, 0.0) * root
        broken = rupture_ref[lines, :].astype(f32)
        intact = active * (1.0 - broken)
        curve = 1.0 + scaled * (1.05 + 2.5 * scaled)
        tension = jnp.where(intact > 0.0, product * inverse / (radius_sum * curve), 0.0)
        force = [tension * member for member in gap]
        released = 0.5 * active * broken * vol
        soaked = ABSORB * intact
        from_own = soaked * own[4]
        from_got = soaked * got[4]
        fresh_ref[lines, :] = intact * vol + (from_own + from_got)
        for c, member in enumerate(force + [released - from_got]):
            high = member.astype(jnp.bfloat16).astype(f32)
            held[pl.ds(s * 8 + c, plane, stride=27 * 8), :] = high
            held[pl.ds(s * 8 + c + 4, plane, stride=27 * 8), :] = member - high
        for c in range(3):
            sums[c] = sums[c] - force[c]
        sums[3] = sums[3] + (released - from_own)
        select(s)

    build(
        0,
        [functools.partial(bridge, s) for s in range(27)],
        0,
        0,
        [functools.partial(scan, 1 - now)],
    )
    for c in range(4):
        owned[c] = sums[c]
    most = counts[now, plane]

    def distribute(group, first, into):
        rows = [summed[into, c * plane : (c + 1) * plane, :] for c in range(3)]
        for s in outer[first:]:
            spot = place[now, s * plane : (s + 1) * plane, :] - group * grains
            here = (spot >= 0) & (spot < grains)
            index = spot & (grains - 1)
            for c in range(3):
                moved = jnp.where(here, take(rows[c], index), 0.0)
                line = far_line(step + s // 9, s % 9, c)
                far[line, :] = far[line, :] - moved

    def own_row(tile, c):
        x, local = tile // plane, tile % plane
        return (((x + 1) * 9 + 4) * 6 + c) * plane + local

    def columns_of(tile):
        block = others[pl.ds(own_row(tile, 0), 6, stride=plane), :]
        return jnp.concatenate([block, jnp.zeros((2, grains), f32)], axis=0).T

    def spread_columns(table, columns, m):
        for at in range(5 * m, 5 * m + 5):
            n, block = at // (grains // 8), at % (grains // 8)
            c = (0, 1, 2, 3, 5)[n]
            part = slice(8 * block, 8 * block + 8)
            table[n, part] = jnp.broadcast_to(columns[part, c : c + 1], (8, grains))

    def pushes(mine, theirs, own_tile):
        deltas = [mine[c] - theirs[c] for c in range(3)]
        square = deltas[0] * deltas[0] + deltas[1] * deltas[1] + deltas[2] * deltas[2]
        if own_tile:
            square = jnp.maximum(square, FLOOR)
        inverse = lax.rsqrt(square)
        inter = jnp.maximum(mine[3] + theirs[3] - square * inverse, TINY)
        push = inter * inter * inverse * lax.rsqrt(inter * (mine[4] + theirs[4]))
        return [push * member for member in deltas]

    def contacts(local, table, groups, own_tile, beside):
        listed = [
            [
                jnp.broadcast_to(lists[g, pl.ds(c * plane + local, 1), :], (8, grains))
                for c in range(5)
            ]
            for g in groups
        ]
        selves = [
            jnp.broadcast_to(others[pl.ds(own_row(step * plane + local, c), 1), :], (8, grains))
            for c in (0, 1, 2, 3, 5)
        ]
        collected = [[jnp.zeros((8, grains), f32)] * 3 for g in groups]
        for m in range(grains // 8):
            part = slice(8 * m, 8 * m + 8)
            mine = [table[c, part] for c in range(5)]
            both = pushes(mine, selves, True) if own_tile else None
            for g, theirs in enumerate(listed):
                products = pushes(mine, theirs, False)
                for c in range(3):
                    collected[g][c] = collected[g][c] + products[c]
                both = [a + b for a, b in zip(both, products)] if both else products
            for c in range(3):
                acc[c, part] = both[c]
            beside(m)
        for g, into in enumerate(groups):
            for c in range(3):
                line = jnp.sum(collected[g][c], axis=0, keepdims=True)
                summed[into, pl.ds(c * plane + local, 1), :] = line
        ones = jnp.ones((8, 2 * grains), jnp.bfloat16)
        for c in range(3):
            both = jnp.concatenate(split(acc[c]), axis=1)
            value = lax.dot_general(ones, both, across, preferred_element_type=f32)
            line = pl.ds(local, 1)
            owned[c, line, :] = owned[c, line, :] + value[0:1]

    across = (((1,), (1,)), ((), ()))
    lanes = lax.broadcasted_iota(jnp.int32, (grains, grains), 0).astype(f32).astype(jnp.bfloat16)
    one = jnp.ones((grains, grains), jnp.bfloat16)
    zero = jnp.zeros((grains, grains), jnp.bfloat16)
    blank = jnp.zeros((8, grains), jnp.bfloat16)

    def bridges(local, pair):
        chosen, left, targets = [], [], []
        tile = step * plane + local
        for k in (2 * pair, 2 * pair + 1):
            targets.append(agenda[tile, 64 + k])
            left.append(held[pl.ds(pl.multiple_of(agenda[tile, 32 + k], 8), 8), :])
            aim = partner_ref[pl.ds(agenda[tile, k], 1), :]
            aim = jnp.broadcast_to(aim.astype(f32).astype(jnp.bfloat16), (grains, grains))
            chosen.append(jnp.where(lanes == aim, one, zero))
        none = jnp.zeros((8, grains), f32)
        first = jnp.concatenate([left[0], none], axis=0).astype(jnp.bfloat16)
        second = jnp.concatenate([none, left[1]], axis=0).astype(jnp.bfloat16)
        moved = lax.dot_general(
            jnp.concatenate([first, second], axis=1),
            jnp.concatenate(chosen, axis=1),
            across,
            preferred_element_type=f32,
        )
        for n, target in enumerate(targets):
            rows = pl.ds(pl.multiple_of(target, 8), 8)
            near[rows, :] = near[rows, :] + moved[8 * n : 8 * n + 8]

    @pl.when(step == 0)
    def _():
        columns = columns_of(0)
        for m in range(grains // 8):
            spread_columns(tables[0], columns, m)

    early = counts[now, plane + 1]

    @pl.when((most > grains) & (early > grains))
    def _():
        build(1, [], 0, 1)

    @pl.when((most > grains) & (early <= grains))
    def _():
        build(1, [], 22, 1)

    def tile_step(couple, carry):
        def run(groups):
            for half in range(2):
                local = 2 * couple + half
                tile = step * plane + local
                columns = columns_of(jnp.minimum(tile + 1, bx * plane - 1))

                def beside(m):
                    spread_columns(tables[1 - half], columns, m)
                    if m % 2 == 0:
                        bridges(local, m // 2)

                contacts(local, tables[half], groups, True, beside)

        crowded = jnp.maximum(counts[now, 2 * couple], counts[now, 2 * couple + 1]) > grains

        @pl.when(crowded)
        def _():
            run((0, 1))

        @pl.when(jnp.logical_not(crowded))
        def _():
            run((0,))

        for half in range(2):
            local = 2 * couple + half

            def spare(pair, inner):
                bridges(local, pair)
                return inner

            lax.fori_loop(grains // 16, (agenda[step * plane + local, 96] + 1) // 2, spare, 0)
        return carry

    @pl.when(step == 0)
    def _():
        pltpu.make_async_copy(todo, agenda, agenda_sem).wait()

    lax.fori_loop(0, plane // 2, tile_step, 0)
    distribute(0, 0, 0)

    @pl.when((most > grains) & (early > grains))
    def _():
        distribute(1, 0, 1)

    @pl.when((most > grains) & (early <= grains))
    def _():
        distribute(1, 22, 1)

    def more(group, carry):
        build(group, [], 0, 0)

        def again(local, inner):
            @pl.when(counts[now, local] > group * grains)
            def _():
                columns = columns_of(step * plane + local)
                for m in range(grains // 8):
                    spread_columns(table_more, columns, m)
                contacts(local, table_more, (0,), False, lambda m: None)

            return inner

        lax.fori_loop(0, plane, again, 0)
        distribute(group, 0, 0)
        return carry

    lax.fori_loop(2, (most + grains - 1) // grains, more, 0)
    for c in range(4):
        line = far_line(step + 1, 4, c)
        far[line, :] = far[line, :] + owned[c]

    @pl.when(step == pl.num_programs(0) - 1)
    def _():
        def fold(x, carry):
            sheet = wy * wz
            for c in range(4):
                base = pl.multiple_of(x * (sheet * 8), 8)
                value = near[pl.ds(base + c, sheet, stride=8), :]
                value = value + near[pl.ds(base + c + 4, sheet, stride=8), :]
                totals_ref[pl.ds(c * cells + x * sheet, sheet), :] = value
                for ez in range(3) if c < 3 else (1,):
                    for z in range(bz):
                        line = pl.ds(c * cells + x * sheet + z + ez, wy, stride=wz)
                        add = far[pl.ds(far_base(x, ez, c) + z, wy, stride=bz), :]
                        totals_ref[line, :] = totals_ref[line, :] + add
            return carry

        lax.fori_loop(0, bx + 2, fold, 0)


def shards(positions, grain_radii, film_liquid, pair_live, partner, rupture, volume):
    bx, by, bz, grains = grain_radii.shape
    tiles = bx * by * bz
    slots = 27 * tiles
    cells = (bx + 2) * (by + 2) * (bz + 2)
    extents = (bx, by, bz)
    film = film_liquid.reshape(1, bx, by, bz, 1, grains)
    border = spread(
        positions.reshape(3, bx, by, bz, 1, grains),
        grain_radii.reshape(1, bx, by, bz, 1, grains),
        film,
        extents,
    ).reshape(5 * cells, grains)
    plane = by * bz
    span = 27 * plane
    wide = pl.BlockSpec((span, grains), lambda i: (i, 0))
    f32 = jnp.float32
    totals, fresh = pl.pallas_call(
        functools.partial(kernel, (bx, by, bz, grains)),
        grid_spec=pltpu.PrefetchScalarGridSpec(
            num_scalar_prefetch=0,
            grid=(bx,),
            in_specs=[
                pl.BlockSpec(memory_space=pl.ANY),
                pl.BlockSpec((1, slots), lambda i: (0, 0)),
                wide,
                wide,
                wide,
            ],
            out_specs=[pl.BlockSpec((4 * cells, grains), lambda i: (0, 0)), wide],
            scratch_shapes=[
                pltpu.VMEM(((bx + 2) * 9 * 6 * plane, grains), f32),
                pltpu.VMEM((tiles, grains), f32),
                pltpu.VMEM((slots, grains), f32),
                pltpu.VMEM((grains, 5 * grains), jnp.bfloat16),
                pltpu.VMEM((span * 8 + 8, grains), f32),
                pltpu.VMEM((span, grains), f32),
                pltpu.VMEM((2, span, grains), f32),
                pltpu.VMEM((2, 3, span, grains), f32),
                pltpu.VMEM((2, span + plane, grains), f32),
                pltpu.VMEM((2, span, grains), jnp.int32),
                pltpu.VMEM((2, 5 * plane, grains), f32),
                pltpu.VMEM((2, 3 * plane, grains), f32),
                pltpu.VMEM((4, plane, grains), f32),
                pltpu.VMEM((5, grains, grains), f32),
                pltpu.VMEM((5, grains, grains), f32),
                pltpu.VMEM((5, grains, grains), f32),
                pltpu.VMEM((3, grains, grains), f32),
                pltpu.VMEM((cells * 8 + 8, grains), f32),
                pltpu.VMEM((3 * (bx + 2) * 4 * (-(-(by + 2) * bz // 8) * 8), grains), f32),
                pltpu.SMEM((2, plane + 2), jnp.int32),
                pltpu.VMEM((tiles, grains), jnp.int32),
                pltpu.SMEM((tiles, grains), jnp.int32),
                pltpu.SemaphoreType.DMA,
                pltpu.VMEM((5 * cells, grains), f32),
                pltpu.SemaphoreType.DMA,
            ],
        ),
        out_shape=[
            jax.ShapeDtypeStruct((4 * cells, grains), f32),
            jax.ShapeDtypeStruct((slots, grains), f32),
        ],
        name="slots",
    )(
        border,
        pair_live.reshape(1, slots),
        partner.reshape(slots, grains),
        rupture.reshape(slots, grains),
        volume.reshape(slots, grains),
    )
    totals = totals.reshape(4, bx + 2, by + 2, bz + 2, 1, grains)
    summed = collect(totals, extents).reshape(4 * tiles, grains)
    vmem = pl.BlockSpec(memory_space=pltpu.VMEM)
    forces, film_next = pl.pallas_call(
        finish_kernel,
        out_shape=[
            jax.ShapeDtypeStruct((3 * tiles, grains), f32),
            jax.ShapeDtypeStruct((tiles, grains), f32),
        ],
        in_specs=[vmem, vmem],
        out_specs=[vmem, vmem],
        name="finish",
    )(summed, film_liquid.reshape(tiles, grains))
    return (
        forces.reshape(positions.shape),
        film_next.reshape(film_liquid.shape),
        fresh.reshape(volume.shape),
    )


def solution(mesh):
    return jax.shard_map(
        shards,
        mesh=mesh,
        in_specs=(
            P(None, "gx", "gy", "gz", None),
            P("gx", "gy", "gz", None),
            P("gx", "gy", "gz", None),
            P("gx", "gy", "gz", None),
            P("gx", "gy", "gz", None, None),
            P("gx", "gy", "gz", None, None),
            P("gx", "gy", "gz", None, None),
        ),
        out_specs=(
            P(None, "gx", "gy", "gz", None),
            P("gx", "gy", "gz", None),
            P("gx", "gy", "gz", None, None),
        ),
        check_vma=False,
    )
```

```python
import functools
import math

import jax
import jax.numpy as jnp
from jax import lax
from jax.experimental import pallas as pl
from jax.experimental.pallas import tpu as pltpu
from jax.sharding import PartitionSpec as P

ABSORB = 0.02
TINY = 1e-30
RADIUS_MAX = 0.6
SLACK = 4e-3
AWAY = -1e4
FLOOR = 1e-12


def neighbours():
    found = [
        (ex, ey, ez)
        for ex in (-1, 0, 1)
        for ey in (-1, 0, 1)
        for ez in (-1, 0, 1)
        if (ex, ey, ez) != (0, 0, 0)
    ]
    return sorted(found, key=lambda offset: -sum(map(abs, offset)))


AXES = ("gx", "gy", "gz")


def present(offset):
    found = None
    for axis, shift in zip(AXES, offset):
        if shift == 0:
            continue
        place = lax.axis_index(axis) + shift
        here = (place >= 0) & (place < lax.axis_size(axis))
        found = here if found is None else found & here
    return found


def device_at(offset):
    return tuple(lax.axis_index(axis) + shift for axis, shift in zip(AXES, offset))


def opposite(offset):
    return tuple(-shift for shift in offset)


def greet(offsets, meanwhile=None):
    barrier = pltpu.get_barrier_semaphore()
    count = jnp.int32(0)
    for offset in offsets:
        here = present(offset)
        count = count + here.astype(jnp.int32)

        @pl.when(here)
        def _():
            pl.semaphore_signal(
                barrier, inc=1, device_id=device_at(offset), device_id_type=pl.DeviceIdType.MESH
            )

    if meanwhile:
        meanwhile()
    pl.semaphore_wait(barrier, count)


def cut(offset, extents, low, whole, high):
    pick = []
    for shift, extent in zip(offset, extents):
        if shift < 0:
            pick.append(pl.ds(low(extent), 1))
        elif shift > 0:
            pick.append(pl.ds(high(extent), 1))
        else:
            pick.append(pl.ds(whole, extent))
    return (slice(None),) + tuple(pick)


def rim(offset, extents):
    return cut(offset, extents, lambda n: 0, 1, lambda n: n + 1)


def edge(offset, extents):
    return cut(offset, extents, lambda n: 0, 0, lambda n: n - 1)


def pushes(mine, theirs, own_tile):
    deltas = [mine[c] - theirs[c] for c in range(3)]
    square = deltas[0] * deltas[0] + deltas[1] * deltas[1] + deltas[2] * deltas[2]
    if own_tile:
        square = jnp.maximum(square, FLOOR)
    inverse = lax.rsqrt(square)
    inter = jnp.maximum(mine[3] + theirs[3] - square * inverse, TINY)
    push = inter * inter * inverse * lax.rsqrt(inter * (mine[4] + theirs[4]))
    return [push * member for member in deltas]


def spread_kernel(
    extents,
    place_ref,
    radius_ref,
    film_ref,
    flat_place_ref,
    flat_radius_ref,
    border_ref,
    inner_ref,
    state,
    blank,
    flat,
    picker,
    local_sem,
    flat_sem,
    send_sem,
    recv_sem,
):
    offsets = neighbours()
    tiles, grains = flat_radius_ref.shape
    flats = [
        pltpu.make_async_copy(flat_place_ref, flat.at[pl.ds(0, 3 * tiles)], flat_sem.at[0]),
        pltpu.make_async_copy(flat_radius_ref, flat.at[pl.ds(3 * tiles, tiles)], flat_sem.at[1]),
    ]

    def rows_of(tile):
        block = flat[pl.ds(tile, 4, stride=tiles), :]
        rows = [block[c : c + 1] for c in range(4)]
        return rows + [1.0 / rows[3]]

    def own_contacts(batch, carry):
        for n in range(4):
            tile = 4 * batch + n
            rows = rows_of(tile)
            block = jnp.concatenate(rows + [jnp.zeros((3, grains), jnp.float32)], axis=0)
            pieces = []
            for _ in range(3):
                piece = block.astype(jnp.bfloat16).astype(jnp.float32)
                pieces.append(piece)
                block = block - piece
            columns = jnp.concatenate(pieces + [jnp.zeros((8, grains), jnp.float32)], axis=0).T
            table = lax.dot_general(
                columns.astype(jnp.bfloat16),
                picker[...],
                (((1,), (0,)), ((), ())),
                preferred_element_type=jnp.float32,
            )
            theirs = [jnp.broadcast_to(row, (8, grains)) for row in rows]
            total = [jnp.zeros((8, grains), jnp.float32)] * 3
            for m in range(grains // 8):
                part = slice(8 * m, 8 * m + 8)
                mine = [table[part, c * grains : (c + 1) * grains] for c in range(5)]
                for c, member in enumerate(pushes(mine, theirs, True)):
                    total[c] = total[c] - member
            for c in range(3):
                line = jnp.sum(total[c], axis=0, keepdims=True)
                inner_ref[pl.ds(c * tiles + tile, 1), :] = line
        return carry

    batches = tiles // 4
    early = 3 * batches // 8
    loads = [
        pltpu.make_async_copy(place_ref, state.at[pl.ds(0, 3)], local_sem.at[0]),
        pltpu.make_async_copy(radius_ref, state.at[pl.ds(3, 1)], local_sem.at[1]),
        pltpu.make_async_copy(film_ref, state.at[pl.ds(4, 1)], local_sem.at[2]),
    ]
    for load in loads + flats:
        load.start()

    def meanwhile():
        for load in flats:
            load.wait()
        row = lax.broadcasted_iota(jnp.int32, (32, grains), 0)
        for c in range(5):
            here = (row == c) | (row == c + 8) | (row == c + 16)
            picker[:, c * grains : (c + 1) * grains] = here.astype(jnp.float32).astype(jnp.bfloat16)
        lax.fori_loop(0, early, own_contacts, 0)

    greet(offsets, meanwhile)
    blank[...] = jnp.zeros_like(blank)
    for load in loads:
        load.wait()
    copies, fills = [], []
    for i, offset in enumerate(offsets):
        copy = pltpu.make_async_remote_copy(
            src_ref=state.at[edge(offset, extents)],
            dst_ref=border_ref.at[rim(opposite(offset), extents)],
            send_sem=send_sem.at[i],
            recv_sem=recv_sem.at[i],
            device_id=device_at(offset),
            device_id_type=pl.DeviceIdType.MESH,
        )
        copies.append(copy)
        pl.when(present(offset))(copy.start)
    inner = pltpu.make_async_copy(
        state, border_ref.at[rim((0, 0, 0), extents)], local_sem.at[3]
    )
    inner.start()
    for i, offset in enumerate(offsets):
        fill = pltpu.make_async_copy(
            blank.at[edge(offset, extents)],
            border_ref.at[rim(offset, extents)],
            local_sem.at[4 + i],
        )
        fills.append(fill)
        pl.when(jnp.logical_not(present(offset)))(fill.start)
    lax.fori_loop(early, batches, own_contacts, 0)
    inner.wait()
    for offset, copy, fill in reversed(list(zip(offsets, copies, fills))):
        pl.when(jnp.logical_not(present(offset)))(fill.wait)
        pl.when(present(offset))(copy.wait_send)
        pl.when(present(opposite(offset)))(copy.wait_recv)


def return_kernel(extents, totals_ref, sum_ref, *scratch):
    offsets = neighbours()
    inbox, (inner, local_sem, send_sem, recv_sem) = scratch[:-4], scratch[-4:]
    load = pltpu.make_async_copy(totals_ref.at[rim((0, 0, 0), extents)], inner, local_sem)
    load.start()
    greet(offsets)
    copies = []
    for i, offset in enumerate(offsets):
        copy = pltpu.make_async_remote_copy(
            src_ref=totals_ref.at[rim(offset, extents)],
            dst_ref=inbox[i],
            send_sem=send_sem.at[i],
            recv_sem=recv_sem.at[i],
            device_id=device_at(offset),
            device_id_type=pl.DeviceIdType.MESH,
        )
        copies.append(copy)
        pl.when(present(offset))(copy.start)
    load.wait()
    sum_ref[...] = inner[...]
    order = sorted(range(len(offsets)), key=lambda i: sum(map(abs, offsets[i])))
    for i in order:
        offset, copy = offsets[i], copies[i]

        @pl.when(present(opposite(offset)))
        def _():
            copy.wait_recv()
            region = edge(opposite(offset), extents)
            sum_ref[region] = sum_ref[region] + inbox[i][...]

    for offset, copy in zip(offsets, copies):
        pl.when(present(offset))(copy.wait_send)


def finish_kernel(sum_ref, film_ref, force_ref, next_ref):
    count = force_ref.shape[0]
    force_ref[...] = sum_ref[0:count, :]
    next_ref[...] = film_ref[...] + sum_ref[count:, :]


def spread(place, radius, film, extents):
    sems = pltpu.SemaphoreType.DMA((26,))
    anywhere = pl.BlockSpec(memory_space=pl.ANY)
    tail = place.shape[4:]
    shape = (5,) + tuple(n + 2 for n in extents) + tail
    own = pltpu.VMEM((5,) + tuple(extents) + tail, jnp.float32)
    tiles, grains = math.prod(extents), tail[-1]
    return pl.pallas_call(
        functools.partial(spread_kernel, extents),
        out_shape=[
            jax.ShapeDtypeStruct(shape, jnp.float32),
            jax.ShapeDtypeStruct((3 * tiles, grains), jnp.float32),
        ],
        in_specs=[anywhere] * 5,
        out_specs=[anywhere, pl.BlockSpec(memory_space=pltpu.VMEM)],
        scratch_shapes=[
            own,
            own,
            pltpu.VMEM((4 * tiles, grains), jnp.float32),
            pltpu.VMEM((32, 5 * grains), jnp.bfloat16),
            pltpu.SemaphoreType.DMA((30,)),
            pltpu.SemaphoreType.DMA((2,)),
            sems,
            sems,
        ],
        compiler_params=pltpu.CompilerParams(collective_id=0, has_side_effects=True),
        name="spread",
    )(place, radius, film, place.reshape(3 * tiles, grains), radius.reshape(tiles, grains))


def collect(totals, extents):
    sems = pltpu.SemaphoreType.DMA((26,))
    vmem = pl.BlockSpec(memory_space=pltpu.VMEM)
    tail = totals.shape[4:]
    boxes = [
        pltpu.VMEM(
            (4,) + tuple(1 if e else n for e, n in zip(offset, extents)) + tail, jnp.float32
        )
        for offset in neighbours()
    ]
    return pl.pallas_call(
        functools.partial(return_kernel, extents),
        out_shape=jax.ShapeDtypeStruct((4,) + tuple(extents) + tail, jnp.float32),
        in_specs=[pl.BlockSpec(memory_space=pl.ANY)],
        out_specs=vmem,
        scratch_shapes=boxes
        + [
            pltpu.VMEM((4,) + tuple(extents) + tail, jnp.float32),
            pltpu.SemaphoreType.DMA,
            sems,
            sems,
        ],
        compiler_params=pltpu.CompilerParams(collective_id=1, has_side_effects=True),
        name="collect",
    )(totals)


def split(values):
    high = values.astype(jnp.bfloat16)
    low = (values - high.astype(jnp.float32)).astype(jnp.bfloat16)
    return high, low


def take(values, index):
    return jnp.take_along_axis(
        values, index, axis=1, mode="promise_in_bounds", wrap_negative_indices=False
    )


def kernel(
    dims,
    border_hbm,
    inner_ref,
    live_ref,
    partner_ref,
    rupture_ref,
    volume_ref,
    totals_ref,
    fresh_ref,
    others,
    flags,
    wide,
    triangle,
    held,
    mask,
    before,
    probes,
    offset,
    place,
    lists,
    summed,
    owned,
    table_even,
    table_odd,
    table_more,
    acc_even,
    acc_odd,
    near,
    far,
    counts,
    todo,
    agenda,
    agenda_sem,
    border_ref,
    border_sem,
):
    bx, by, bz, grains = dims
    tables = (table_even, table_odd)
    accs = (acc_even, acc_odd)
    wy, wz = by + 2, bz + 2
    plane = by * bz
    step = pl.program_id(0)
    cells = (bx + 2) * wy * wz
    f32 = jnp.float32
    faces = [4, 22, 10, 16, 12, 14]
    outer = [s for s in range(27) if s != 13 and s not in faces] + faces

    def other_row(x, j, c):
        return pl.multiple_of(((x * 9 + j) * 6 + c) * plane, plane)

    deep = -(-wy * bz // 8) * 8

    def far_base(x, ez, c):
        return pl.multiple_of(((ez * (bx + 2) + x) * 4 + c) * deep, 8)

    def far_line(x, j, c):
        return pl.ds(far_base(x, j % 3, c) + j // 3 * bz, plane)

    def enlist():
        shape = (bx * plane, grains)
        dims_p = (((1,), (0,)), ((), ()))
        listed = flags[...].astype(jnp.bfloat16)
        ahead = lax.dot_general(
            listed, triangle[:, 0 : 2 * grains], dims_p, preferred_element_type=f32
        )
        amount = ahead[:, grains : 2 * grains].astype(jnp.int32)
        ahead = ahead[:, 0:grains].astype(jnp.int32)
        at = lax.broadcasted_iota(jnp.int32, shape, 1)
        rank = at & 31
        slot = jnp.zeros(shape, jnp.int32)
        for bit in (16, 8, 4, 2, 1):
            slot = jnp.where(take(ahead, slot + (bit - 1)) <= rank, slot + bit, slot)
        valid = rank < amount

        def parts(value, size, number):
            high = sum((value >= size * n).astype(jnp.int32) for n in range(1, number))
            return high, value - size * high

        ix, local = parts(lax.broadcasted_iota(jnp.int32, shape, 0), plane, bx)
        iy, iz = parts(local, bz, by)
        ex, rest = parts(slot, 9, 3)
        ey, ez = parts(rest, 3, 3)
        cell = ((ix + ex) * wy + iy + ey) * wz + iz + ez
        line = local * 27 + slot
        first = jnp.where(valid, line, 0)
        second = jnp.where(valid, line * 8, 27 * plane * 8)
        third = jnp.where(valid, cell * 8, cells * 8)
        low = jnp.where(at < 32, first, second)
        high = jnp.where(at < 96, third, amount)
        todo[...] = jnp.where(at < 64, low, high)
        pltpu.make_async_copy(todo, agenda, agenda_sem).start()

    @pl.when(step == 0)
    def _():
        fetch = pltpu.make_async_copy(border_hbm, border_ref, border_sem)
        fetch.start()
        near[...] = jnp.zeros_like(near)
        far[...] = jnp.zeros_like(far)
        summed[...] = jnp.zeros_like(summed)
        acc_odd[...] = jnp.zeros_like(acc_odd)
        held[27 * plane * 8 :, :] = jnp.zeros((8, grains), f32)
        rows = lax.broadcasted_iota(jnp.int32, (grains, grains), 0)
        cols = lax.broadcasted_iota(jnp.int32, (grains, grains), 1)
        half = grains // 2
        for n, last in enumerate((cols, grains, half - 1, half // 2 - 1, half + half // 2 - 1)):
            block = (rows <= last).astype(f32).astype(jnp.bfloat16)
            triangle[:, n * grains : (n + 1) * grains] = block
        flags[...] = jnp.zeros_like(flags)
        for t in range(bx * plane):
            flags[t : t + 1, 0:27] = live_ref[0:1, t * 27 : t * 27 + 27].astype(f32)

        def widen(x, carry):
            row = flags[pl.ds(pl.multiple_of(x * plane, plane), plane), :]
            for s in range(27):
                line = pl.ds(pl.multiple_of((x * 27 + s) * plane, plane), plane)
                wide[line, :] = jnp.broadcast_to(row[:, s : s + 1], (plane, grains))
            return carry

        lax.fori_loop(0, bx, widen, 0)

        def arrange(x, carry):
            for j in range(9):
                ey, ez = j // 3, j % 3
                for c in range(5):
                    for z in range(bz):
                        start = c * cells + (x * wy + ey) * wz + z + ez
                        got = border_ref[pl.ds(start, by, stride=wz), :]
                        others[pl.ds(((x * 9 + j) * 6 + c) * plane + z, by, stride=bz), :] = got
            for j in range(9):
                radius = others[pl.ds(other_row(x, j, 3), plane), :]
                others[pl.ds(other_row(x, j, 5), plane), :] = 1.0 / radius
            return carry

        enlist()
        fetch.wait()
        lax.fori_loop(0, bx + 2, arrange, 0)

    def cell_at(tile):
        x, local = tile // plane, tile % plane
        return ((x + 1) * wy + local // bz + 1) * wz + local % bz + 1

    def plane_of(x):
        return pl.ds(pl.multiple_of(x * plane, plane), plane)

    def lit(x, s):
        return wide[pl.ds(pl.multiple_of((x * 27 + s) * plane, plane), plane), :]

    def prescan(x):
        mine = [others[pl.ds(other_row(x + 1, 4, c), plane), :] for c in range(4)]
        highs = [jnp.max(mine[c], axis=1, keepdims=True) for c in range(3)]
        lows = [jnp.min(mine[c], axis=1, keepdims=True) for c in range(3)]
        widest = jnp.max(mine[3], axis=1, keepdims=True) + SLACK
        def select(s):
            part = slice(s * plane, (s + 1) * plane)
            if s == 13:
                mask[part, :] = jnp.zeros((plane, grains), f32)
                return
            there = [others[pl.ds(other_row(x + s // 9, s % 9, c), plane), :] for c in range(4)]
            away = [
                jnp.maximum(jnp.maximum(lows[c] - there[c], there[c] - highs[c]), 0.0)
                for c in range(3)
            ]
            reach = widest + there[3]
            inside = away[0] * away[0] + away[1] * away[1] + away[2] * away[2] < reach * reach
            mask[part, :] = jnp.where(inside, lit(x, s), 0.0)

        return select

    def scan(slot):
        prefix = lax.dot_general(
            mask[...].astype(jnp.bfloat16),
            triangle[...],
            (((1,), (0,)), ((), ())),
            preferred_element_type=f32,
        )
        total = jnp.zeros((plane, grains), f32)
        for i, s in enumerate(outer):
            part = slice(s * plane, (s + 1) * plane)
            ahead = prefix[part, 0:grains]
            before[slot, part, :] = ahead
            for n in range(3):
                probes[slot, n, part, :] = prefix[part, (n + 2) * grains : (n + 3) * grains]
            offset[slot, i * plane : (i + 1) * plane, :] = total
            spot = jnp.where(mask[part, :] > 0.0, total + ahead - 1.0, -1.0)
            place[slot, part, :] = spot.astype(jnp.int32)
            if i == len(outer) - 4:
                counts[slot, plane + 1] = jnp.max(total).astype(jnp.int32)
            total = total + prefix[part, grains : 2 * grains]
        offset[slot, 26 * plane : 27 * plane, :] = total
        for t in range(plane):
            counts[slot, t] = total[t, 0].astype(jnp.int32)
        counts[slot, plane] = jnp.max(total).astype(jnp.int32)

    now = step % 2
    lane = lax.broadcasted_iota(jnp.int32, (plane, grains), 1)

    def build(group, beside, first, into, after=()):
        wanted = (lane + group * grains).astype(f32)
        half = grains // 2
        index = {}
        bit = half // 2
        level = 0
        while bit:
            for i, s in list(enumerate(outer))[first:]:
                part = slice(s * plane, (s + 1) * plane)
                rank = wanted - offset[now, i * plane : (i + 1) * plane, :]
                if bit == half // 2:
                    upper = probes[now, 0, part, :] <= rank
                    probe = jnp.where(upper, probes[now, 2, part, :], probes[now, 1, part, :])
                    index[s] = jnp.where(upper, half, 0)
                else:
                    probe = take(before[now, part, :], index[s] + (bit - 1))
                index[s] = jnp.where(probe <= rank, index[s] + bit, index[s])
            for work in beside[level::6]:
                work()
            bit //= 2
            level += 1
        for work in after:
            work()
        found = [jnp.full((plane, grains), AWAY, f32)] * 3 + [jnp.full((plane, grains), 0.5, f32)]
        for i, s in list(enumerate(outer))[first:]:
            low = offset[now, i * plane : (i + 1) * plane, :]
            high = offset[now, (i + 1) * plane : (i + 2) * plane, :]
            here = (wanted >= low) & (wanted < high)
            for c in range(4):
                member = others[pl.ds(other_row(step + s // 9, s % 9, c), plane), :]
                found[c] = jnp.where(here, take(member, index[s]), found[c])
        for c, member in enumerate(found + [1.0 / found[3]]):
            lists[into, c * plane : (c + 1) * plane, :] = member

    @pl.when(step == 0)
    def _():
        select = prescan(0)
        for s in range(27):
            select(s)
        scan(0)

    own = [others[pl.ds(other_row(step + 1, 4, c), plane), :] for c in range(5)]
    twice = 2.0 * own[3]
    sums = [jnp.zeros((plane, grains), f32)] * 4
    select = prescan(jnp.minimum(step + 1, bx - 1))

    def bridge(s):
        near_by = [others[pl.ds(other_row(step + s // 9, s % 9, c), plane), :] for c in range(5)]
        lines = pl.ds(s, plane, stride=27)
        partner = partner_ref[lines, :]
        got = [take(member, partner) for member in near_by]
        active = lit(step, s)
        gap = [own[c] - got[c] for c in range(3)]
        square = gap[0] * gap[0] + gap[1] * gap[1] + gap[2] * gap[2]
        inverse = lax.rsqrt(square)
        radius_sum = own[3] + got[3]
        product = twice * got[3]
        vol = volume_ref[lines, :]
        root = product * lax.rsqrt(product * (radius_sum * vol))
        scaled = jnp.maximum(square * inverse - radius_sum, 0.0) * root
        broken = rupture_ref[lines, :].astype(f32)
        intact = active * (1.0 - broken)
        curve = 1.0 + scaled * (1.05 + 2.5 * scaled)
        tension = jnp.where(intact > 0.0, product * inverse / (radius_sum * curve), 0.0)
        force = [tension * member for member in gap]
        released = 0.5 * active * broken * vol
        soaked = ABSORB * intact
        from_own = soaked * own[4]
        from_got = soaked * got[4]
        fresh_ref[lines, :] = intact * vol + (from_own + from_got)
        for c, member in enumerate(force + [released - from_got]):
            high = member.astype(jnp.bfloat16).astype(f32)
            held[pl.ds(s * 8 + c, plane, stride=27 * 8), :] = high
            held[pl.ds(s * 8 + c + 4, plane, stride=27 * 8), :] = member - high
        for c in range(3):
            sums[c] = sums[c] - force[c]
        sums[3] = sums[3] + (released - from_own)
        select(s)

    build(
        0,
        [functools.partial(bridge, s) for s in range(27)],
        0,
        0,
        [functools.partial(scan, 1 - now)],
    )
    for c in range(3):
        rows = pl.ds(pl.multiple_of(c * bx * plane + step * plane, plane), plane)
        owned[c, 8:, :] = sums[c] + inner_ref[rows, :]
    owned[3, 8:, :] = sums[3]
    most = counts[now, plane]

    def distribute(group, first, into):
        rows = [summed[into, c * plane : (c + 1) * plane, :] for c in range(3)]
        for s in outer[first:]:
            spot = place[now, s * plane : (s + 1) * plane, :] - group * grains
            here = (spot >= 0) & (spot < grains)
            index = spot & (grains - 1)
            for c in range(3):
                moved = jnp.where(here, take(rows[c], index), 0.0)
                line = far_line(step + s // 9, s % 9, c)
                far[line, :] = far[line, :] - moved

    def own_row(tile, c):
        x, local = tile // plane, tile % plane
        return (((x + 1) * 9 + 4) * 6 + c) * plane + local

    def columns_of(tile):
        block = others[pl.ds(own_row(tile, 0), 6, stride=plane), :]
        return jnp.concatenate([block, jnp.zeros((2, grains), f32)], axis=0).T

    def spread_columns(table, columns, m):
        for at in range(5 * m, 5 * m + 5):
            n, block = at // (grains // 8), at % (grains // 8)
            c = (0, 1, 2, 3, 5)[n]
            part = slice(8 * block, 8 * block + 8)
            table[n, part] = jnp.broadcast_to(columns[part, c : c + 1], (8, grains))

    def reduce(acc, local):
        ones = jnp.ones((8, 2 * grains), jnp.bfloat16)
        for c in range(3):
            both = jnp.concatenate(split(acc[c]), axis=1)
            value = lax.dot_general(ones, both, across, preferred_element_type=f32)
            line = pl.ds(local + 8, 1)
            owned[c, line, :] = owned[c, line, :] + value[0:1]

    def contacts(local, table, acc, groups, beside):
        listed = [
            [
                jnp.broadcast_to(lists[g, pl.ds(c * plane + local, 1), :], (8, grains))
                for c in range(5)
            ]
            for g in groups
        ]
        collected = [[jnp.zeros((8, grains), f32)] * 3 for g in groups]
        for m in range(grains // 8):
            part = slice(8 * m, 8 * m + 8)
            mine = [table[c, part] for c in range(5)]
            both = None
            for g, theirs in enumerate(listed):
                products = pushes(mine, theirs, False)
                for c in range(3):
                    collected[g][c] = collected[g][c] + products[c]
                both = [a + b for a, b in zip(both, products)] if both else products
            for c in range(3):
                acc[c, part] = both[c]
            beside(m)
        for g, into in enumerate(groups):
            for c in range(3):
                line = jnp.sum(collected[g][c], axis=0, keepdims=True)
                summed[into, pl.ds(c * plane + local, 1), :] = line

    across = (((1,), (1,)), ((), ()))
    lanes = lax.broadcasted_iota(jnp.int32, (grains, grains), 0).astype(f32).astype(jnp.bfloat16)
    one = jnp.ones((grains, grains), jnp.bfloat16)
    zero = jnp.zeros((grains, grains), jnp.bfloat16)
    blank = jnp.zeros((8, grains), jnp.bfloat16)

    def bridges(local, pair):
        chosen, left, targets = [], [], []
        tile = step * plane + local
        for k in (2 * pair, 2 * pair + 1):
            targets.append(agenda[tile, 64 + k])
            left.append(held[pl.ds(pl.multiple_of(agenda[tile, 32 + k], 8), 8), :])
            aim = partner_ref[pl.ds(agenda[tile, k], 1), :]
            aim = jnp.broadcast_to(aim.astype(f32).astype(jnp.bfloat16), (grains, grains))
            chosen.append(jnp.where(lanes == aim, one, zero))
        none = jnp.zeros((8, grains), f32)
        first = jnp.concatenate([left[0], none], axis=0).astype(jnp.bfloat16)
        second = jnp.concatenate([none, left[1]], axis=0).astype(jnp.bfloat16)
        moved = lax.dot_general(
            jnp.concatenate([first, second], axis=1),
            jnp.concatenate(chosen, axis=1),
            across,
            preferred_element_type=f32,
        )
        for n, target in enumerate(targets):
            rows = pl.ds(pl.multiple_of(target, 8), 8)
            near[rows, :] = near[rows, :] + moved[8 * n : 8 * n + 8]

    @pl.when(step == 0)
    def _():
        columns = columns_of(0)
        for m in range(grains // 8):
            spread_columns(tables[0], columns, m)

    early = counts[now, plane + 1]

    @pl.when((most > grains) & (early > grains))
    def _():
        build(1, [], 0, 1)

    @pl.when((most > grains) & (early <= grains))
    def _():
        build(1, [], 22, 1)

    def tile_step(couple, carry):
        def run(groups):
            reduce(acc_odd, 2 * couple - 1)
            for half in range(2):
                local = 2 * couple + half
                tile = step * plane + local
                columns = columns_of(jnp.minimum(tile + 1, bx * plane - 1))

                def beside(m):
                    spread_columns(tables[1 - half], columns, m)
                    if m < grains // 16:
                        bridges(local, m)

                contacts(local, tables[half], accs[half], groups, beside)
                if half == 0:
                    reduce(acc_even, local)

        crowded = jnp.maximum(counts[now, 2 * couple], counts[now, 2 * couple + 1]) > grains

        @pl.when(crowded)
        def _():
            run((0, 1))

        @pl.when(jnp.logical_not(crowded))
        def _():
            run((0,))

        for half in range(2):
            local = 2 * couple + half

            def spare(pair, inner):
                bridges(local, pair)
                return inner

            lax.fori_loop(grains // 16, (agenda[step * plane + local, 96] + 1) // 2, spare, 0)
        return carry

    @pl.when(step == 0)
    def _():
        pltpu.make_async_copy(todo, agenda, agenda_sem).wait()

    lax.fori_loop(0, plane // 2, tile_step, 0)
    reduce(acc_odd, plane - 1)
    distribute(0, 0, 0)

    @pl.when((most > grains) & (early > grains))
    def _():
        distribute(1, 0, 1)

    @pl.when((most > grains) & (early <= grains))
    def _():
        distribute(1, 22, 1)

    def more(group, carry):
        build(group, [], 0, 0)

        def again(local, inner):
            @pl.when(counts[now, local] > group * grains)
            def _():
                columns = columns_of(step * plane + local)
                for m in range(grains // 8):
                    spread_columns(table_more, columns, m)
                contacts(local, table_more, acc_even, (0,), lambda m: None)
                reduce(acc_even, local)

            return inner

        lax.fori_loop(0, plane, again, 0)
        distribute(group, 0, 0)
        return carry

    lax.fori_loop(2, (most + grains - 1) // grains, more, 0)
    for c in range(4):
        line = far_line(step + 1, 4, c)
        far[line, :] = far[line, :] + owned[c, 8:, :]

    @pl.when(step == pl.num_programs(0) - 1)
    def _():
        def fold(x, carry):
            sheet = wy * wz
            for c in range(4):
                base = pl.multiple_of(x * (sheet * 8), 8)
                value = near[pl.ds(base + c, sheet, stride=8), :]
                value = value + near[pl.ds(base + c + 4, sheet, stride=8), :]
                totals_ref[pl.ds(c * cells + x * sheet, sheet), :] = value
                for ez in range(3) if c < 3 else (1,):
                    for z in range(bz):
                        line = pl.ds(c * cells + x * sheet + z + ez, wy, stride=wz)
                        add = far[pl.ds(far_base(x, ez, c) + z, wy, stride=bz), :]
                        totals_ref[line, :] = totals_ref[line, :] + add
            return carry

        lax.fori_loop(0, bx + 2, fold, 0)


def shards(positions, grain_radii, film_liquid, pair_live, partner, rupture, volume):
    bx, by, bz, grains = grain_radii.shape
    tiles = bx * by * bz
    slots = 27 * tiles
    cells = (bx + 2) * (by + 2) * (bz + 2)
    extents = (bx, by, bz)
    film = film_liquid.reshape(1, bx, by, bz, 1, grains)
    border, inner = spread(
        positions.reshape(3, bx, by, bz, 1, grains),
        grain_radii.reshape(1, bx, by, bz, 1, grains),
        film,
        extents,
    )
    border = border.reshape(5 * cells, grains)
    plane = by * bz
    span = 27 * plane
    wide = pl.BlockSpec((span, grains), lambda i: (i, 0))
    f32 = jnp.float32
    totals, fresh = pl.pallas_call(
        functools.partial(kernel, (bx, by, bz, grains)),
        grid_spec=pltpu.PrefetchScalarGridSpec(
            num_scalar_prefetch=0,
            grid=(bx,),
            in_specs=[
                pl.BlockSpec(memory_space=pl.ANY),
                pl.BlockSpec((3 * tiles, grains), lambda i: (0, 0)),
                pl.BlockSpec((1, slots), lambda i: (0, 0)),
                wide,
                wide,
                wide,
            ],
            out_specs=[pl.BlockSpec((4 * cells, grains), lambda i: (0, 0)), wide],
            scratch_shapes=[
                pltpu.VMEM(((bx + 2) * 9 * 6 * plane, grains), f32),
                pltpu.VMEM((tiles, grains), f32),
                pltpu.VMEM((slots, grains), f32),
                pltpu.VMEM((grains, 5 * grains), jnp.bfloat16),
                pltpu.VMEM((span * 8 + 8, grains), f32),
                pltpu.VMEM((span, grains), f32),
                pltpu.VMEM((2, span, grains), f32),
                pltpu.VMEM((2, 3, span, grains), f32),
                pltpu.VMEM((2, span + plane, grains), f32),
                pltpu.VMEM((2, span, grains), jnp.int32),
                pltpu.VMEM((2, 5 * plane, grains), f32),
                pltpu.VMEM((2, 3 * plane, grains), f32),
                pltpu.VMEM((4, plane + 8, grains), f32),
                pltpu.VMEM((5, grains, grains), f32),
                pltpu.VMEM((5, grains, grains), f32),
                pltpu.VMEM((5, grains, grains), f32),
                pltpu.VMEM((3, grains, grains), f32),
                pltpu.VMEM((3, grains, grains), f32),
                pltpu.VMEM((cells * 8 + 8, grains), f32),
                pltpu.VMEM((3 * (bx + 2) * 4 * (-(-(by + 2) * bz // 8) * 8), grains), f32),
                pltpu.SMEM((2, plane + 2), jnp.int32),
                pltpu.VMEM((tiles, grains), jnp.int32),
                pltpu.SMEM((tiles, grains), jnp.int32),
                pltpu.SemaphoreType.DMA,
                pltpu.VMEM((5 * cells, grains), f32),
                pltpu.SemaphoreType.DMA,
            ],
        ),
        out_shape=[
            jax.ShapeDtypeStruct((4 * cells, grains), f32),
            jax.ShapeDtypeStruct((slots, grains), f32),
        ],
        name="slots",
    )(
        border,
        inner,
        pair_live.reshape(1, slots),
        partner.reshape(slots, grains),
        rupture.reshape(slots, grains),
        volume.reshape(slots, grains),
    )
    totals = totals.reshape(4, bx + 2, by + 2, bz + 2, 1, grains)
    summed = collect(totals, extents).reshape(4 * tiles, grains)
    vmem = pl.BlockSpec(memory_space=pltpu.VMEM)
    forces, film_next = pl.pallas_call(
        finish_kernel,
        out_shape=[
            jax.ShapeDtypeStruct((3 * tiles, grains), f32),
            jax.ShapeDtypeStruct((tiles, grains), f32),
        ],
        in_specs=[vmem, vmem],
        out_specs=[vmem, vmem],
        name="finish",
    )(summed, film_liquid.reshape(tiles, grains))
    return (
        forces.reshape(positions.shape),
        film_next.reshape(film_liquid.shape),
        fresh.reshape(volume.shape),
    )


def solution(mesh):
    return jax.shard_map(
        shards,
        mesh=mesh,
        in_specs=(
            P(None, "gx", "gy", "gz", None),
            P("gx", "gy", "gz", None),
            P("gx", "gy", "gz", None),
            P("gx", "gy", "gz", None),
            P("gx", "gy", "gz", None, None),
            P("gx", "gy", "gz", None, None),
            P("gx", "gy", "gz", None, None),
        ),
        out_specs=(
            P(None, "gx", "gy", "gz", None),
            P("gx", "gy", "gz", None),
            P("gx", "gy", "gz", None, None),
        ),
        check_vma=False,
    )
```

```python
import functools
import math

import jax
import jax.numpy as jnp
from jax import lax
from jax.experimental import pallas as pl
from jax.experimental.pallas import tpu as pltpu
from jax.sharding import PartitionSpec as P

ABSORB = 0.02
TINY = 1e-30
RADIUS_MAX = 0.6
SLACK = 4e-3
AWAY = -1e4
FLOOR = 1e-12


def neighbours():
    found = [
        (ex, ey, ez)
        for ex in (-1, 0, 1)
        for ey in (-1, 0, 1)
        for ez in (-1, 0, 1)
        if (ex, ey, ez) != (0, 0, 0)
    ]
    return sorted(found, key=lambda offset: -sum(map(abs, offset)))


AXES = ("gx", "gy", "gz")


def present(offset):
    found = None
    for axis, shift in zip(AXES, offset):
        if shift == 0:
            continue
        place = lax.axis_index(axis) + shift
        here = (place >= 0) & (place < lax.axis_size(axis))
        found = here if found is None else found & here
    return found


def device_at(offset):
    return tuple(lax.axis_index(axis) + shift for axis, shift in zip(AXES, offset))


def opposite(offset):
    return tuple(-shift for shift in offset)


def greet(offsets, meanwhile=None):
    barrier = pltpu.get_barrier_semaphore()
    count = jnp.int32(0)
    for offset in offsets:
        here = present(offset)
        count = count + here.astype(jnp.int32)

        @pl.when(here)
        def _():
            pl.semaphore_signal(
                barrier, inc=1, device_id=device_at(offset), device_id_type=pl.DeviceIdType.MESH
            )

    if meanwhile:
        meanwhile()
    pl.semaphore_wait(barrier, count)


def cut(offset, extents, low, whole, high):
    pick = []
    for shift, extent in zip(offset, extents):
        if shift < 0:
            pick.append(pl.ds(low(extent), 1))
        elif shift > 0:
            pick.append(pl.ds(high(extent), 1))
        else:
            pick.append(pl.ds(whole, extent))
    return (slice(None),) + tuple(pick)


def rim(offset, extents):
    return cut(offset, extents, lambda n: 0, 1, lambda n: n + 1)


def edge(offset, extents):
    return cut(offset, extents, lambda n: 0, 0, lambda n: n - 1)


def pushes(mine, theirs, own_tile):
    deltas = [mine[c] - theirs[c] for c in range(3)]
    square = deltas[0] * deltas[0] + deltas[1] * deltas[1] + deltas[2] * deltas[2]
    if own_tile:
        square = jnp.maximum(square, FLOOR)
    inverse = lax.rsqrt(square)
    inter = jnp.maximum(mine[3] + theirs[3] - square * inverse, TINY)
    push = inter * inter * inverse * lax.rsqrt(inter * (mine[4] + theirs[4]))
    return [push * member for member in deltas]


def spread_kernel(
    extents,
    place_ref,
    radius_ref,
    film_ref,
    flat_place_ref,
    flat_radius_ref,
    border_ref,
    inner_ref,
    state,
    blank,
    flat,
    picker,
    local_sem,
    flat_sem,
    send_sem,
    recv_sem,
):
    offsets = neighbours()
    tiles, grains = flat_radius_ref.shape
    flats = [
        pltpu.make_async_copy(flat_place_ref, flat.at[pl.ds(0, 3 * tiles)], flat_sem.at[0]),
        pltpu.make_async_copy(flat_radius_ref, flat.at[pl.ds(3 * tiles, tiles)], flat_sem.at[1]),
    ]

    def rows_of(tile):
        block = flat[pl.ds(tile, 4, stride=tiles), :]
        rows = [block[c : c + 1] for c in range(4)]
        return rows + [1.0 / rows[3]]

    def own_contacts(batch, carry):
        for n in range(4):
            tile = 4 * batch + n
            rows = rows_of(tile)
            block = jnp.concatenate(rows + [jnp.zeros((3, grains), jnp.float32)], axis=0)
            pieces = []
            for _ in range(3):
                piece = block.astype(jnp.bfloat16).astype(jnp.float32)
                pieces.append(piece)
                block = block - piece
            columns = jnp.concatenate(pieces + [jnp.zeros((8, grains), jnp.float32)], axis=0).T
            table = lax.dot_general(
                columns.astype(jnp.bfloat16),
                picker[...],
                (((1,), (0,)), ((), ())),
                preferred_element_type=jnp.float32,
            )
            theirs = [jnp.broadcast_to(row, (8, grains)) for row in rows]
            total = [jnp.zeros((8, grains), jnp.float32)] * 3
            for m in range(grains // 8):
                part = slice(8 * m, 8 * m + 8)
                mine = [table[part, c * grains : (c + 1) * grains] for c in range(5)]
                for c, member in enumerate(pushes(mine, theirs, True)):
                    total[c] = total[c] - member
            for c in range(3):
                line = jnp.sum(total[c], axis=0, keepdims=True)
                inner_ref[pl.ds(c * tiles + tile, 1), :] = line
        return carry

    batches = tiles // 4
    early = 3 * batches // 8
    loads = [
        pltpu.make_async_copy(place_ref, state.at[pl.ds(0, 3)], local_sem.at[0]),
        pltpu.make_async_copy(radius_ref, state.at[pl.ds(3, 1)], local_sem.at[1]),
        pltpu.make_async_copy(film_ref, state.at[pl.ds(4, 1)], local_sem.at[2]),
    ]
    for load in loads + flats:
        load.start()

    def meanwhile():
        for load in flats:
            load.wait()
        row = lax.broadcasted_iota(jnp.int32, (32, grains), 0)
        for c in range(5):
            here = (row == c) | (row == c + 8) | (row == c + 16)
            picker[:, c * grains : (c + 1) * grains] = here.astype(jnp.float32).astype(jnp.bfloat16)
        lax.fori_loop(0, early, own_contacts, 0)

    greet(offsets, meanwhile)
    blank[...] = jnp.zeros_like(blank)
    for load in loads:
        load.wait()
    copies, fills = [], []
    for i, offset in enumerate(offsets):
        copy = pltpu.make_async_remote_copy(
            src_ref=state.at[edge(offset, extents)],
            dst_ref=border_ref.at[rim(opposite(offset), extents)],
            send_sem=send_sem.at[i],
            recv_sem=recv_sem.at[i],
            device_id=device_at(offset),
            device_id_type=pl.DeviceIdType.MESH,
        )
        copies.append(copy)
        pl.when(present(offset))(copy.start)
    inner = pltpu.make_async_copy(
        state, border_ref.at[rim((0, 0, 0), extents)], local_sem.at[3]
    )
    inner.start()
    for i, offset in enumerate(offsets):
        fill = pltpu.make_async_copy(
            blank.at[edge(offset, extents)],
            border_ref.at[rim(offset, extents)],
            local_sem.at[4 + i],
        )
        fills.append(fill)
        pl.when(jnp.logical_not(present(offset)))(fill.start)
    lax.fori_loop(early, batches, own_contacts, 0)
    inner.wait()
    for offset, copy, fill in reversed(list(zip(offsets, copies, fills))):
        pl.when(jnp.logical_not(present(offset)))(fill.wait)
        pl.when(present(offset))(copy.wait_send)
        pl.when(present(opposite(offset)))(copy.wait_recv)


def return_kernel(extents, totals_ref, sum_ref, *scratch):
    offsets = neighbours()
    inbox, (inner, local_sem, send_sem, recv_sem) = scratch[:-4], scratch[-4:]
    load = pltpu.make_async_copy(totals_ref.at[rim((0, 0, 0), extents)], inner, local_sem)
    load.start()
    greet(offsets)
    copies = []
    for i, offset in enumerate(offsets):
        copy = pltpu.make_async_remote_copy(
            src_ref=totals_ref.at[rim(offset, extents)],
            dst_ref=inbox[i],
            send_sem=send_sem.at[i],
            recv_sem=recv_sem.at[i],
            device_id=device_at(offset),
            device_id_type=pl.DeviceIdType.MESH,
        )
        copies.append(copy)
        pl.when(present(offset))(copy.start)
    load.wait()
    sum_ref[...] = inner[...]
    order = sorted(range(len(offsets)), key=lambda i: sum(map(abs, offsets[i])))
    for i in order:
        offset, copy = offsets[i], copies[i]

        @pl.when(present(opposite(offset)))
        def _():
            copy.wait_recv()
            region = edge(opposite(offset), extents)
            sum_ref[region] = sum_ref[region] + inbox[i][...]

    for offset, copy in zip(offsets, copies):
        pl.when(present(offset))(copy.wait_send)


def finish_kernel(sum_ref, film_ref, force_ref, next_ref):
    count = force_ref.shape[0]
    force_ref[...] = sum_ref[0:count, :]
    next_ref[...] = film_ref[...] + sum_ref[count:, :]


def spread(place, radius, film, extents):
    sems = pltpu.SemaphoreType.DMA((26,))
    anywhere = pl.BlockSpec(memory_space=pl.ANY)
    tail = place.shape[4:]
    shape = (5,) + tuple(n + 2 for n in extents) + tail
    own = pltpu.VMEM((5,) + tuple(extents) + tail, jnp.float32)
    tiles, grains = math.prod(extents), tail[-1]
    return pl.pallas_call(
        functools.partial(spread_kernel, extents),
        out_shape=[
            jax.ShapeDtypeStruct(shape, jnp.float32),
            jax.ShapeDtypeStruct((3 * tiles, grains), jnp.float32),
        ],
        in_specs=[anywhere] * 5,
        out_specs=[anywhere, pl.BlockSpec(memory_space=pltpu.VMEM)],
        scratch_shapes=[
            own,
            own,
            pltpu.VMEM((4 * tiles, grains), jnp.float32),
            pltpu.VMEM((32, 5 * grains), jnp.bfloat16),
            pltpu.SemaphoreType.DMA((30,)),
            pltpu.SemaphoreType.DMA((2,)),
            sems,
            sems,
        ],
        compiler_params=pltpu.CompilerParams(collective_id=0, has_side_effects=True),
        name="spread",
    )(place, radius, film, place.reshape(3 * tiles, grains), radius.reshape(tiles, grains))


def collect(totals, extents):
    sems = pltpu.SemaphoreType.DMA((26,))
    vmem = pl.BlockSpec(memory_space=pltpu.VMEM)
    tail = totals.shape[4:]
    boxes = [
        pltpu.VMEM(
            (4,) + tuple(1 if e else n for e, n in zip(offset, extents)) + tail, jnp.float32
        )
        for offset in neighbours()
    ]
    return pl.pallas_call(
        functools.partial(return_kernel, extents),
        out_shape=jax.ShapeDtypeStruct((4,) + tuple(extents) + tail, jnp.float32),
        in_specs=[pl.BlockSpec(memory_space=pl.ANY)],
        out_specs=vmem,
        scratch_shapes=boxes
        + [
            pltpu.VMEM((4,) + tuple(extents) + tail, jnp.float32),
            pltpu.SemaphoreType.DMA,
            sems,
            sems,
        ],
        compiler_params=pltpu.CompilerParams(collective_id=1, has_side_effects=True),
        name="collect",
    )(totals)


def split(values):
    high = values.astype(jnp.bfloat16)
    low = (values - high.astype(jnp.float32)).astype(jnp.bfloat16)
    return high, low


def take(values, index):
    return jnp.take_along_axis(
        values, index, axis=1, mode="promise_in_bounds", wrap_negative_indices=False
    )


def kernel(
    dims,
    border_hbm,
    inner_ref,
    live_ref,
    partner_ref,
    rupture_ref,
    volume_ref,
    totals_ref,
    fresh_ref,
    others,
    flags,
    wide,
    triangle,
    held,
    mask,
    before,
    probes,
    offset,
    place,
    lists,
    summed,
    owned,
    table_even,
    table_odd,
    table_more,
    acc,
    near,
    far,
    counts,
    todo,
    agenda,
    agenda_sem,
    border_ref,
    border_sem,
):
    bx, by, bz, grains = dims
    tables = (table_even, table_odd)
    wy, wz = by + 2, bz + 2
    plane = by * bz
    step = pl.program_id(0)
    cells = (bx + 2) * wy * wz
    f32 = jnp.float32
    faces = [4, 22, 10, 16, 12, 14]
    outer = [s for s in range(27) if s != 13 and s not in faces] + faces

    def other_row(x, j, c):
        return pl.multiple_of(((x * 9 + j) * 6 + c) * plane, plane)

    deep = -(-wy * bz // 8) * 8

    def far_base(x, ez, c):
        return pl.multiple_of(((ez * (bx + 2) + x) * 4 + c) * deep, 8)

    def far_line(x, j, c):
        return pl.ds(far_base(x, j % 3, c) + j // 3 * bz, plane)

    def enlist():
        shape = (bx * plane, grains)
        dims_p = (((1,), (0,)), ((), ()))
        listed = flags[...].astype(jnp.bfloat16)
        ahead = lax.dot_general(
            listed, triangle[:, 0 : 2 * grains], dims_p, preferred_element_type=f32
        )
        amount = ahead[:, grains : 2 * grains].astype(jnp.int32)
        ahead = ahead[:, 0:grains].astype(jnp.int32)
        at = lax.broadcasted_iota(jnp.int32, shape, 1)
        rank = at & 31
        slot = jnp.zeros(shape, jnp.int32)
        for bit in (16, 8, 4, 2, 1):
            slot = jnp.where(take(ahead, slot + (bit - 1)) <= rank, slot + bit, slot)
        valid = rank < amount

        def parts(value, size, number):
            high = sum((value >= size * n).astype(jnp.int32) for n in range(1, number))
            return high, value - size * high

        ix, local = parts(lax.broadcasted_iota(jnp.int32, shape, 0), plane, bx)
        iy, iz = parts(local, bz, by)
        ex, rest = parts(slot, 9, 3)
        ey, ez = parts(rest, 3, 3)
        cell = ((ix + ex) * wy + iy + ey) * wz + iz + ez
        line = local * 27 + slot
        first = jnp.where(valid, line, 0)
        second = jnp.where(valid, line * 8, 27 * plane * 8)
        third = jnp.where(valid, cell * 8, cells * 8)
        low = jnp.where(at < 32, first, second)
        high = jnp.where(at < 96, third, amount)
        todo[...] = jnp.where(at < 64, low, high)
        pltpu.make_async_copy(todo, agenda, agenda_sem).start()

    @pl.when(step == 0)
    def _():
        fetch = pltpu.make_async_copy(border_hbm, border_ref, border_sem)
        fetch.start()
        near[...] = jnp.zeros_like(near)
        far[...] = jnp.zeros_like(far)
        summed[...] = jnp.zeros_like(summed)
        held[27 * plane * 8 :, :] = jnp.zeros((8, grains), f32)
        rows = lax.broadcasted_iota(jnp.int32, (grains, grains), 0)
        cols = lax.broadcasted_iota(jnp.int32, (grains, grains), 1)
        half = grains // 2
        marks = [half - 1, half // 2 - 1, half + half // 2 - 1]
        marks += [(2 * n + 1) * grains // 8 - 1 for n in range(4)]
        for n, last in enumerate([cols, grains] + marks):
            block = (rows <= last).astype(f32).astype(jnp.bfloat16)
            triangle[:, n * grains : (n + 1) * grains] = block
        flags[...] = jnp.zeros_like(flags)
        for t in range(bx * plane):
            flags[t : t + 1, 0:27] = live_ref[0:1, t * 27 : t * 27 + 27].astype(f32)

        def widen(x, carry):
            row = flags[pl.ds(pl.multiple_of(x * plane, plane), plane), :]
            for s in range(27):
                line = pl.ds(pl.multiple_of((x * 27 + s) * plane, plane), plane)
                wide[line, :] = jnp.broadcast_to(row[:, s : s + 1], (plane, grains))
            return carry

        lax.fori_loop(0, bx, widen, 0)

        def arrange(x, carry):
            for j in range(9):
                ey, ez = j // 3, j % 3
                for c in range(5):
                    for z in range(bz):
                        start = c * cells + (x * wy + ey) * wz + z + ez
                        got = border_ref[pl.ds(start, by, stride=wz), :]
                        others[pl.ds(((x * 9 + j) * 6 + c) * plane + z, by, stride=bz), :] = got
            for j in range(9):
                radius = others[pl.ds(other_row(x, j, 3), plane), :]
                others[pl.ds(other_row(x, j, 5), plane), :] = 1.0 / radius
            return carry

        enlist()
        fetch.wait()
        lax.fori_loop(0, bx + 2, arrange, 0)

    def cell_at(tile):
        x, local = tile // plane, tile % plane
        return ((x + 1) * wy + local // bz + 1) * wz + local % bz + 1

    def plane_of(x):
        return pl.ds(pl.multiple_of(x * plane, plane), plane)

    def lit(x, s):
        return wide[pl.ds(pl.multiple_of((x * 27 + s) * plane, plane), plane), :]

    def prescan(x):
        mine = [others[pl.ds(other_row(x + 1, 4, c), plane), :] for c in range(4)]
        highs = [jnp.max(mine[c], axis=1, keepdims=True) for c in range(3)]
        lows = [jnp.min(mine[c], axis=1, keepdims=True) for c in range(3)]
        widest = jnp.max(mine[3], axis=1, keepdims=True) + SLACK
        def select(s):
            part = slice(s * plane, (s + 1) * plane)
            if s == 13:
                mask[part, :] = jnp.zeros((plane, grains), f32)
                return
            there = [others[pl.ds(other_row(x + s // 9, s % 9, c), plane), :] for c in range(4)]
            away = [
                jnp.maximum(jnp.maximum(lows[c] - there[c], there[c] - highs[c]), 0.0)
                for c in range(3)
            ]
            reach = widest + there[3]
            inside = away[0] * away[0] + away[1] * away[1] + away[2] * away[2] < reach * reach
            mask[part, :] = jnp.where(inside, lit(x, s), 0.0)

        return select

    def scan(slot):
        prefix = lax.dot_general(
            mask[...].astype(jnp.bfloat16),
            triangle[...],
            (((1,), (0,)), ((), ())),
            preferred_element_type=f32,
        )
        total = jnp.zeros((plane, grains), f32)
        for i, s in enumerate(outer):
            part = slice(s * plane, (s + 1) * plane)
            ahead = prefix[part, 0:grains]
            before[slot, part, :] = ahead
            for n in range(7):
                probes[slot, n, part, :] = prefix[part, (n + 2) * grains : (n + 3) * grains]
            offset[slot, i * plane : (i + 1) * plane, :] = total
            spot = jnp.where(mask[part, :] > 0.0, total + ahead - 1.0, -1.0)
            place[slot, part, :] = spot.astype(jnp.int32)
            if i == len(outer) - 4:
                counts[slot, plane + 1] = jnp.max(total).astype(jnp.int32)
            total = total + prefix[part, grains : 2 * grains]
        offset[slot, 26 * plane : 27 * plane, :] = total
        for t in range(plane):
            counts[slot, t] = total[t, 0].astype(jnp.int32)
        counts[slot, plane] = jnp.max(total).astype(jnp.int32)

    now = step % 2
    lane = lax.broadcasted_iota(jnp.int32, (plane, grains), 1)

    def build(group, beside, first, into, after=()):
        wanted = (lane + group * grains).astype(f32)
        half = grains // 2
        index = {}
        bit = grains // 8
        level = 0
        while bit:
            for i, s in list(enumerate(outer))[first:]:
                part = slice(s * plane, (s + 1) * plane)
                rank = wanted - offset[now, i * plane : (i + 1) * plane, :]
                if bit == grains // 8:
                    marks = [probes[now, n, part, :] for n in range(7)]
                    upper = marks[0] <= rank
                    second = jnp.where(upper, marks[2], marks[1]) <= rank
                    high = jnp.where(second, marks[6], marks[5])
                    low = jnp.where(second, marks[4], marks[3])
                    probe = jnp.where(upper, high, low)
                    index[s] = jnp.where(upper, half, 0) + jnp.where(second, half // 2, 0)
                else:
                    probe = take(before[now, part, :], index[s] + (bit - 1))
                index[s] = jnp.where(probe <= rank, index[s] + bit, index[s])
            for work in beside[level::5]:
                work()
            bit //= 2
            level += 1
        for work in after:
            work()
        found = [jnp.full((plane, grains), AWAY, f32)] * 3 + [jnp.full((plane, grains), 0.5, f32)]
        for i, s in list(enumerate(outer))[first:]:
            low = offset[now, i * plane : (i + 1) * plane, :]
            high = offset[now, (i + 1) * plane : (i + 2) * plane, :]
            here = (wanted >= low) & (wanted < high)
            for c in range(4):
                member = others[pl.ds(other_row(step + s // 9, s % 9, c), plane), :]
                found[c] = jnp.where(here, take(member, index[s]), found[c])
        for c, member in enumerate(found + [1.0 / found[3]]):
            lists[into, c * plane : (c + 1) * plane, :] = member

    @pl.when(step == 0)
    def _():
        select = prescan(0)
        for s in range(27):
            select(s)
        scan(0)

    own = [others[pl.ds(other_row(step + 1, 4, c), plane), :] for c in range(5)]
    twice = 2.0 * own[3]
    sums = [jnp.zeros((plane, grains), f32)] * 4
    select = prescan(jnp.minimum(step + 1, bx - 1))

    def bridge(s):
        near_by = [others[pl.ds(other_row(step + s // 9, s % 9, c), plane), :] for c in range(5)]
        lines = pl.ds(s, plane, stride=27)
        partner = partner_ref[lines, :]
        got = [take(member, partner) for member in near_by]
        active = lit(step, s)
        gap = [own[c] - got[c] for c in range(3)]
        square = gap[0] * gap[0] + gap[1] * gap[1] + gap[2] * gap[2]
        inverse = lax.rsqrt(square)
        radius_sum = own[3] + got[3]
        product = twice * got[3]
        vol = volume_ref[lines, :]
        root = product * lax.rsqrt(product * (radius_sum * vol))
        scaled = jnp.maximum(square * inverse - radius_sum, 0.0) * root
        broken = rupture_ref[lines, :].astype(f32)
        intact = active * (1.0 - broken)
        curve = 1.0 + scaled * (1.05 + 2.5 * scaled)
        tension = jnp.where(intact > 0.0, product * inverse / (radius_sum * curve), 0.0)
        force = [tension * member for member in gap]
        released = 0.5 * active * broken * vol
        soaked = ABSORB * intact
        from_own = soaked * own[4]
        from_got = soaked * got[4]
        fresh_ref[lines, :] = intact * vol + (from_own + from_got)
        for c, member in enumerate(force + [released - from_got]):
            high = member.astype(jnp.bfloat16).astype(f32)
            held[pl.ds(s * 8 + c, plane, stride=27 * 8), :] = high
            held[pl.ds(s * 8 + c + 4, plane, stride=27 * 8), :] = member - high
        for c in range(3):
            sums[c] = sums[c] - force[c]
        sums[3] = sums[3] + (released - from_own)
        select(s)

    build(
        0,
        [functools.partial(bridge, s) for s in range(27)],
        0,
        0,
        [functools.partial(scan, 1 - now)],
    )
    for c in range(3):
        rows = pl.ds(pl.multiple_of(c * bx * plane + step * plane, plane), plane)
        owned[c] = sums[c] + inner_ref[rows, :]
    owned[3] = sums[3]
    most = counts[now, plane]

    def distribute(group, first, into):
        rows = [summed[into, c * plane : (c + 1) * plane, :] for c in range(3)]
        for s in outer[first:]:
            spot = place[now, s * plane : (s + 1) * plane, :] - group * grains
            here = (spot >= 0) & (spot < grains)
            index = spot & (grains - 1)
            for c in range(3):
                moved = jnp.where(here, take(rows[c], index), 0.0)
                line = far_line(step + s // 9, s % 9, c)
                far[line, :] = far[line, :] - moved

    def own_row(tile, c):
        x, local = tile // plane, tile % plane
        return (((x + 1) * 9 + 4) * 6 + c) * plane + local

    def columns_of(tile):
        block = others[pl.ds(own_row(tile, 0), 6, stride=plane), :]
        return jnp.concatenate([block, jnp.zeros((2, grains), f32)], axis=0).T

    def spread_columns(table, columns, m):
        for at in range(5 * m, 5 * m + 5):
            n, block = at // (grains // 8), at % (grains // 8)
            c = (0, 1, 2, 3, 5)[n]
            part = slice(8 * block, 8 * block + 8)
            table[n, part] = jnp.broadcast_to(columns[part, c : c + 1], (8, grains))

    def contacts(local, table, groups, beside):
        listed = [
            [
                jnp.broadcast_to(lists[g, pl.ds(c * plane + local, 1), :], (8, grains))
                for c in range(5)
            ]
            for g in groups
        ]
        collected = [[jnp.zeros((8, grains), f32)] * 3 for g in groups]
        for m in range(grains // 8):
            part = slice(8 * m, 8 * m + 8)
            mine = [table[c, part] for c in range(5)]
            both = None
            for g, theirs in enumerate(listed):
                products = pushes(mine, theirs, False)
                for c in range(3):
                    collected[g][c] = collected[g][c] + products[c]
                both = [a + b for a, b in zip(both, products)] if both else products
            for c in range(3):
                acc[c, part] = both[c]
            beside(m)
        for g, into in enumerate(groups):
            for c in range(3):
                line = jnp.sum(collected[g][c], axis=0, keepdims=True)
                summed[into, pl.ds(c * plane + local, 1), :] = line
        ones = jnp.ones((8, 2 * grains), jnp.bfloat16)
        for c in range(3):
            both = jnp.concatenate(split(acc[c]), axis=1)
            value = lax.dot_general(ones, both, across, preferred_element_type=f32)
            line = pl.ds(local, 1)
            owned[c, line, :] = owned[c, line, :] + value[0:1]

    across = (((1,), (1,)), ((), ()))
    lanes = lax.broadcasted_iota(jnp.int32, (grains, grains), 0).astype(f32).astype(jnp.bfloat16)
    one = jnp.ones((grains, grains), jnp.bfloat16)
    zero = jnp.zeros((grains, grains), jnp.bfloat16)
    blank = jnp.zeros((8, grains), jnp.bfloat16)

    def bridges(local, pair):
        chosen, left, targets = [], [], []
        tile = step * plane + local
        for k in (2 * pair, 2 * pair + 1):
            targets.append(agenda[tile, 64 + k])
            left.append(held[pl.ds(pl.multiple_of(agenda[tile, 32 + k], 8), 8), :])
            aim = partner_ref[pl.ds(agenda[tile, k], 1), :]
            aim = jnp.broadcast_to(aim.astype(f32).astype(jnp.bfloat16), (grains, grains))
            chosen.append(jnp.where(lanes == aim, one, zero))
        none = jnp.zeros((8, grains), f32)
        first = jnp.concatenate([left[0], none], axis=0).astype(jnp.bfloat16)
        second = jnp.concatenate([none, left[1]], axis=0).astype(jnp.bfloat16)
        moved = lax.dot_general(
            jnp.concatenate([first, second], axis=1),
            jnp.concatenate(chosen, axis=1),
            across,
            preferred_element_type=f32,
        )
        for n, target in enumerate(targets):
            rows = pl.ds(pl.multiple_of(target, 8), 8)
            near[rows, :] = near[rows, :] + moved[8 * n : 8 * n + 8]

    @pl.when(step == 0)
    def _():
        columns = columns_of(0)
        for m in range(grains // 8):
            spread_columns(tables[0], columns, m)

    early = counts[now, plane + 1]

    @pl.when((most > grains) & (early > grains))
    def _():
        build(1, [], 0, 1)

    @pl.when((most > grains) & (early <= grains))
    def _():
        build(1, [], 22, 1)

    def tile_step(couple, carry):
        def run(groups):
            for half in range(2):
                local = 2 * couple + half
                tile = step * plane + local
                columns = columns_of(jnp.minimum(tile + 1, bx * plane - 1))

                def beside(m):
                    spread_columns(tables[1 - half], columns, m)
                    if m % 2 == 0:
                        bridges(local, m // 2)

                contacts(local, tables[half], groups, beside)

        crowded = jnp.maximum(counts[now, 2 * couple], counts[now, 2 * couple + 1]) > grains

        @pl.when(crowded)
        def _():
            run((0, 1))

        @pl.when(jnp.logical_not(crowded))
        def _():
            run((0,))

        for half in range(2):
            local = 2 * couple + half

            def spare(pair, inner):
                bridges(local, pair)
                return inner

            lax.fori_loop(grains // 16, (agenda[step * plane + local, 96] + 1) // 2, spare, 0)
        return carry

    @pl.when(step == 0)
    def _():
        pltpu.make_async_copy(todo, agenda, agenda_sem).wait()

    lax.fori_loop(0, plane // 2, tile_step, 0)
    distribute(0, 0, 0)

    @pl.when((most > grains) & (early > grains))
    def _():
        distribute(1, 0, 1)

    @pl.when((most > grains) & (early <= grains))
    def _():
        distribute(1, 22, 1)

    def more(group, carry):
        build(group, [], 0, 0)

        def again(local, inner):
            @pl.when(counts[now, local] > group * grains)
            def _():
                columns = columns_of(step * plane + local)
                for m in range(grains // 8):
                    spread_columns(table_more, columns, m)
                contacts(local, table_more, (0,), lambda m: None)

            return inner

        lax.fori_loop(0, plane, again, 0)
        distribute(group, 0, 0)
        return carry

    lax.fori_loop(2, (most + grains - 1) // grains, more, 0)
    for c in range(4):
        line = far_line(step + 1, 4, c)
        far[line, :] = far[line, :] + owned[c]

    @pl.when(step == pl.num_programs(0) - 1)
    def _():
        def fold(x, carry):
            sheet = wy * wz
            for c in range(4):
                base = pl.multiple_of(x * (sheet * 8), 8)
                value = near[pl.ds(base + c, sheet, stride=8), :]
                value = value + near[pl.ds(base + c + 4, sheet, stride=8), :]
                totals_ref[pl.ds(c * cells + x * sheet, sheet), :] = value
                for ez in range(3) if c < 3 else (1,):
                    for z in range(bz):
                        line = pl.ds(c * cells + x * sheet + z + ez, wy, stride=wz)
                        add = far[pl.ds(far_base(x, ez, c) + z, wy, stride=bz), :]
                        totals_ref[line, :] = totals_ref[line, :] + add
            return carry

        lax.fori_loop(0, bx + 2, fold, 0)


def shards(positions, grain_radii, film_liquid, pair_live, partner, rupture, volume):
    bx, by, bz, grains = grain_radii.shape
    tiles = bx * by * bz
    slots = 27 * tiles
    cells = (bx + 2) * (by + 2) * (bz + 2)
    extents = (bx, by, bz)
    film = film_liquid.reshape(1, bx, by, bz, 1, grains)
    border, inner = spread(
        positions.reshape(3, bx, by, bz, 1, grains),
        grain_radii.reshape(1, bx, by, bz, 1, grains),
        film,
        extents,
    )
    border = border.reshape(5 * cells, grains)
    plane = by * bz
    span = 27 * plane
    wide = pl.BlockSpec((span, grains), lambda i: (i, 0))
    f32 = jnp.float32
    totals, fresh = pl.pallas_call(
        functools.partial(kernel, (bx, by, bz, grains)),
        grid_spec=pltpu.PrefetchScalarGridSpec(
            num_scalar_prefetch=0,
            grid=(bx,),
            in_specs=[
                pl.BlockSpec(memory_space=pl.ANY),
                pl.BlockSpec((3 * tiles, grains), lambda i: (0, 0)),
                pl.BlockSpec((1, slots), lambda i: (0, 0)),
                wide,
                wide,
                wide,
            ],
            out_specs=[pl.BlockSpec((4 * cells, grains), lambda i: (0, 0)), wide],
            scratch_shapes=[
                pltpu.VMEM(((bx + 2) * 9 * 6 * plane, grains), f32),
                pltpu.VMEM((tiles, grains), f32),
                pltpu.VMEM((slots, grains), f32),
                pltpu.VMEM((grains, 9 * grains), jnp.bfloat16),
                pltpu.VMEM((span * 8 + 8, grains), f32),
                pltpu.VMEM((span, grains), f32),
                pltpu.VMEM((2, span, grains), f32),
                pltpu.VMEM((2, 7, span, grains), f32),
                pltpu.VMEM((2, span + plane, grains), f32),
                pltpu.VMEM((2, span, grains), jnp.int32),
                pltpu.VMEM((2, 5 * plane, grains), f32),
                pltpu.VMEM((2, 3 * plane, grains), f32),
                pltpu.VMEM((4, plane, grains), f32),
                pltpu.VMEM((5, grains, grains), f32),
                pltpu.VMEM((5, grains, grains), f32),
                pltpu.VMEM((5, grains, grains), f32),
                pltpu.VMEM((3, grains, grains), f32),
                pltpu.VMEM((cells * 8 + 8, grains), f32),
                pltpu.VMEM((3 * (bx + 2) * 4 * (-(-(by + 2) * bz // 8) * 8), grains), f32),
                pltpu.SMEM((2, plane + 2), jnp.int32),
                pltpu.VMEM((tiles, grains), jnp.int32),
                pltpu.SMEM((tiles, grains), jnp.int32),
                pltpu.SemaphoreType.DMA,
                pltpu.VMEM((5 * cells, grains), f32),
                pltpu.SemaphoreType.DMA,
            ],
        ),
        out_shape=[
            jax.ShapeDtypeStruct((4 * cells, grains), f32),
            jax.ShapeDtypeStruct((slots, grains), f32),
        ],
        name="slots",
    )(
        border,
        inner,
        pair_live.reshape(1, slots),
        partner.reshape(slots, grains),
        rupture.reshape(slots, grains),
        volume.reshape(slots, grains),
    )
    totals = totals.reshape(4, bx + 2, by + 2, bz + 2, 1, grains)
    summed = collect(totals, extents).reshape(4 * tiles, grains)
    vmem = pl.BlockSpec(memory_space=pltpu.VMEM)
    forces, film_next = pl.pallas_call(
        finish_kernel,
        out_shape=[
            jax.ShapeDtypeStruct((3 * tiles, grains), f32),
            jax.ShapeDtypeStruct((tiles, grains), f32),
        ],
        in_specs=[vmem, vmem],
        out_specs=[vmem, vmem],
        name="finish",
    )(summed, film_liquid.reshape(tiles, grains))
    return (
        forces.reshape(positions.shape),
        film_next.reshape(film_liquid.shape),
        fresh.reshape(volume.shape),
    )


def solution(mesh):
    return jax.shard_map(
        shards,
        mesh=mesh,
        in_specs=(
            P(None, "gx", "gy", "gz", None),
            P("gx", "gy", "gz", None),
            P("gx", "gy", "gz", None),
            P("gx", "gy", "gz", None),
            P("gx", "gy", "gz", None, None),
            P("gx", "gy", "gz", None, None),
            P("gx", "gy", "gz", None, None),
        ),
        out_specs=(
            P(None, "gx", "gy", "gz", None),
            P("gx", "gy", "gz", None),
            P("gx", "gy", "gz", None, None),
        ),
        check_vma=False,
    )
```
